32 devices in a mesh: shard: 8 (over z, x), rep: 4 (over y, core).
Axes of the slice: x: 2, y: 2, z: 4, core: 2. Of those that a mesh axis runs over, the one named last changes fastest.
Arguments:
- tokens_in: float32 [31520, 768], P(('shard', 'rep')), may hold values from -6 to 6
- routes: int32 [31520, 2], P(('shard', 'rep')), may hold values from 0 to 3, all different within a row; in each aligned block of 985 rows (0 to 984, 985 to 1969, ...) at most 616 rows name the same one
- first_gain: bfloat16 [768], P('shard'), may hold values from 0.5 to 1.5
- first_shift: bfloat16 [768], P('shard'), may hold values from -3 to 3
- joint_weight: bfloat16 [768, 2304], P('shard'), may hold values from -0.21875 to 0.21875
- joint_bias: bfloat16 [2, 768], P(None, 'shard'), may hold values from -3 to 3
- mixer_weight: bfloat16 [768, 768], P('shard'), may hold values from -0.625 to 0.625
- mixer_bias: bfloat16 [768], P('shard'), may hold values from -3 to 3
- second_gain: bfloat16 [768], P('shard'), may hold values from 0.5 to 1.5
- second_shift: bfloat16 [768], P('shard'), may hold values from -3 to 3
- router_weight: bfloat16 [768, 4], P('shard'), may hold values from -0.4375 to 0.4375
- expert_up: bfloat16 [4, 768, 3072], P(None, None, 'shard'), may hold values from -0.21875 to 0.21875
- upward_bias: bfloat16 [4, 3072], P(None, 'shard'), may hold values from -3 to 3
- expert_down: bfloat16 [4, 3072, 768], P(None, 'shard'), may hold values from -0.3125 to 0.3125
- downward_bias: bfloat16 [4, 768], P(None, 'shard'), may hold values from -3 to 3
- out_grad: float32 [31520, 768], P(('shard', 'rep')), may hold values from -6 to 6
Outputs:
- block_out: float32 [31520, 768], P(('shard', 'rep'))
- input_grad: float32 [31520, 768], P(('shard', 'rep'))
- first_gain_grad: float32 [768], P('shard')
- first_shift_grad: float32 [768], P('shard')
- joint_weight_grad: float32 [768, 2304], P('shard')
- joint_bias_grad: float32 [2, 768], P(None, 'shard')
- mixer_weight_grad: float32 [768, 768], P('shard')
- mixer_bias_grad: float32 [768], P('shard')
- second_gain_grad: float32 [768], P('shard')
- second_shift_grad: float32 [768], P('shard')
- router_weight_grad: float32 [768, 4], P('shard')
- expert_up_grad: float32 [4, 768, 3072], P(None, None, 'shard')
- upward_bias_grad: float32 [4, 3072], P(None, 'shard')
- expert_down_grad: float32 [4, 3072, 768], P(None, 'shard')
- downward_bias_grad: float32 [4, 768], P(None, 'shard')
The draws below stay inside these ranges and needn't reach their ends.
Inputs may be any that keep to these rules, and one draw needn't show every extreme that they name: `routes`: the two experts of a token differ. Among the rows of one device (985 aligned rows), no expert is named more than 616 times.
All inputs are finite; a program needn't handle non-finite values.
Results may differ from the reference program's by a relative error of at most 0.02.
Values may be sent and summed in bfloat16 or wider, within the bound.
A program may use at most 320 MiB of HBM per device.

```python
import math
import jax
import jax.numpy as jnp
import numpy as np
from jax import lax

D = 768
HEADS = 12
HEAD_DIM = 64
FF = 3072
SEQ = 197
EXPERTS = 4
TOK_DEV = 985
CAP = 616
TOKENS = 31520


def raised(values, rng, source, target, parts, factor):
    owner, partner = [(jnp.arange(values.shape[dim]) // (values.shape[dim] // parts)).reshape([-1 if axis == dim else 1 for axis in range(values.ndim)]) for dim in (source, target)]
    chosen = jax.random.permutation(rng, parts)[partner]
    strong = (owner == chosen) | (owner == (partner + parts // 2) % parts)
    return jnp.where(strong, factor * values, values)


def shard_levels(rng, extent, shards, low, top_value):
    factor_of, own = 1.0, jax.random.fold_in(rng, 6)
    for dim, shards_of in shards:
        draws = jnp.exp(jax.random.uniform(jax.random.fold_in(own, dim), (shards_of,), jnp.float32, low / len(shards), top_value / len(shards)))
        factor_of = factor_of * jnp.repeat(draws, extent[dim] // shards_of).reshape([-1 if axis == dim else 1 for axis in range(len(extent))])
    return factor_of


def routed_block(rng, own, number, rows, amount, top, bound, skew):
    order = jax.random.permutation(rng, amount)
    crowded, ordinary = load_shares(amount, rows * top, bound, skew, True), load_shares(amount, rows * top, bound, skew, False)
    places = jnp.arange(amount)

    def named(lengths, rotation):
        used = int((lengths > 0).sum())
        fixed = max(1, used // 4)
        moved = fixed + (places - fixed + rotation * (used - fixed)) % max(1, amount - fixed)
        return jnp.zeros((amount,), jnp.int32).at[order[jnp.where(places < fixed, places, moved)]].set(jnp.asarray(lengths, jnp.int32))

    lengths = jnp.where(number % 4 == 0, named(crowded, number // 4), named(ordinary, number - number // 4 - 1))
    mixed = jax.random.permutation(jax.random.fold_in(own, 3), amount)
    source_of, sink = mixed[0:amount // 2 * 2:2], mixed[1:amount // 2 * 2:2]
    slack = jnp.minimum(lengths[source_of] - 1, bound - lengths[sink]) // 2
    slack = jnp.where((source_of == order[0]) | (sink == order[0]) | (lengths[sink] == 0), 0, jnp.maximum(slack, 0))
    moved = jax.random.randint(jax.random.fold_in(own, 4), (amount // 2,), 0, 1 << 20) % (slack + 1)
    lengths = lengths.at[source_of].add(-moved).at[sink].add(moved)
    members = jnp.searchsorted(jnp.cumsum(lengths), jnp.arange(rows * top), side="right").astype(jnp.int32)
    table = members.reshape(top, rows).T
    table = table[jax.random.permutation(jax.random.fold_in(own, 1), rows)]
    rotation = jax.random.randint(jax.random.fold_in(own, 2), (rows, 1), 0, top)
    return jnp.take_along_axis(table, (jnp.arange(top)[None, :] + rotation) % top, axis=1)


def load_shares(number_of, total, bound, lean, full):
    loads = [(1 << 20) // math.isqrt(standing ** lean) + 1 for standing in range(1, number_of + 1)]
    largest = bound if full else min(bound, max(-(-total // number_of), total * loads[0] // sum(loads)))
    least = 1 if total - largest >= number_of - 1 else 0
    given, surplus = [largest] + [least] * (number_of - 1), total - largest - least * (number_of - 1)
    while surplus > 0:
        movable = [i for i in range(1, number_of) if given[i] < largest] or [i for i in range(1, number_of) if given[i] < bound]
        mass, remaining = sum([loads[i] for i in movable]), surplus
        for i in movable:
            addition = min(bound - given[i], max(1, remaining * loads[i] // mass), surplus)
            given[i] = given[i] + addition
            surplus = surplus - addition
    return np.array(given)


def bell_draw(own_key, dims, scale, bound, split=(), kind=jnp.bfloat16):
    factor_of = shard_levels(own_key, dims, split, -0.22, 0.18) if split else 1.0
    values = jax.random.normal(own_key, dims, jnp.float32) * scale * factor_of
    return jnp.minimum(jnp.maximum(values, -bound), bound).astype(kind)


def noise_with(key, shape, scale, limit, split, heavy, held_as=jnp.bfloat16):
    drawn = scale * jax.random.normal(key, shape, jnp.float32)
    if split:
        drawn = drawn * shard_levels(key, shape, split, -0.22, 0.18)
    return jnp.clip(raised(drawn, jax.random.fold_in(key, 3), *heavy), -limit, limit).astype(held_as)


def setup_inputs(seed: int = 0) -> dict:
    key_of = jax.random.split(jax.random.key(seed), 17)
    tokens_in = bell_draw(key_of[0], (TOKENS, D), 1.0, 6.0, ((0, 32),), jnp.float32)
    routes_keys = jax.random.split(jax.random.fold_in(key_of[1], 1), TOKENS // TOK_DEV)
    routes_turns = jax.random.permutation(jax.random.fold_in(key_of[1], 3), TOKENS // TOK_DEV)
    routes = jax.vmap(lambda own, number: routed_block(jax.random.fold_in(key_of[1], 2), own, number, TOK_DEV, EXPERTS, 2, CAP, 1))(routes_keys, routes_turns).reshape((TOKENS, 2))
    first_gain = jnp.clip(1.0 + 0.1 * jax.random.normal(key_of[2], (D,), jnp.float32), 0.5, 1.5).astype(jnp.bfloat16)
    first_shift = bell_draw(key_of[3], (D,), 0.5, 3.0, ((0, 8),))
    joint_weight = bell_draw(key_of[4], (D, 3 * D), D ** -0.5, 0.21875, ((0, 8),))
    joint_bias = bell_draw(key_of[5], (2, D), 0.5, 3.0, ((1, 8),))
    mixer_weight = bell_draw(key_of[6], (D, D), (D // 8) ** -0.5, 0.625, ((0, 8),))
    mixer_bias = bell_draw(key_of[7], (D,), 0.5, 3.0, ((0, 8),))
    second_gain = jnp.clip(1.0 + 0.1 * jax.random.normal(key_of[8], (D,), jnp.float32), 0.5, 1.5).astype(jnp.bfloat16)
    second_shift = bell_draw(key_of[9], (D,), 0.5, 3.0, ((0, 8),))
    router_weight = bell_draw(key_of[10], (D, EXPERTS), (D // 4) ** -0.5, 0.4375, ((0, 8),))
    expert_up = bell_draw(key_of[11], (EXPERTS, D, FF), D ** -0.5, 0.21875, ((2, 8),))
    upward_bias = bell_draw(key_of[12], (EXPERTS, FF), 0.5, 3.0, ((1, 8),))
    expert_down = bell_draw(key_of[13], (EXPERTS, FF, D), (FF // 8) ** -0.5, 0.3125, ((1, 8),))
    downward_bias = bell_draw(key_of[14], (EXPERTS, D), 0.5, 3.0, ((1, 8),))
    out_grad = noise_with(key_of[15], (TOKENS, D), 1.0, 6.0, ((0, 32),), (0, 1, 32, 2.75), jnp.float32)
    return dict(tokens_in=tokens_in, routes=routes, first_gain=first_gain, first_shift=first_shift, joint_weight=joint_weight, joint_bias=joint_bias, mixer_weight=mixer_weight, mixer_bias=mixer_bias, second_gain=second_gain, second_shift=second_shift, router_weight=router_weight, expert_up=expert_up, upward_bias=upward_bias, expert_down=expert_down, downward_bias=downward_bias, out_grad=out_grad)


@jax.custom_vjp
def low(v):
    return lax.optimization_barrier(v.astype(jnp.bfloat16)).astype(jnp.float32)

@jax.custom_vjp
def low_back(v):
    return v

def low_keep(v):
    return (low(v), None)

def low_pass(kept, grad):
    return (grad,)

def back_keep(v):
    return (v, None)

def back_low(kept, grad):
    return (low(grad),)
low.defvjp(low_keep, low_pass)
low_back.defvjp(back_keep, back_low)
epsilon = 1e-06
highest = lax.Precision.HIGHEST

def layer_norm(values, gain, shift):
    centre = lax.optimization_barrier(jnp.mean(values, axis=-1, keepdims=True))
    centred = values - centre
    spread = lax.optimization_barrier(jnp.mean(centred * centred, axis=-1, keepdims=True))
    return centred * lax.rsqrt(spread + epsilon) * gain + shift

def dispatch_tables(routes, experts, capacity):
    token_count = routes.shape[0]
    flat_routes = routes.reshape(-1).astype(jnp.int32)
    hit_table = (flat_routes[:, None] == jnp.arange(experts, dtype=jnp.int32)[None, :]).astype(jnp.int32)
    earlier = jnp.cumsum(hit_table, axis=0) - hit_table
    slot_index = lax.optimization_barrier(jnp.sum(earlier * hit_table, axis=1)).astype(jnp.int32)
    position = (flat_routes * capacity + slot_index).astype(jnp.int32)
    entries = jnp.arange(2 * token_count, dtype=jnp.int32)
    owner = jnp.full((experts * capacity,), 2 * token_count, jnp.int32).at[position].set(entries)
    return (position, owner)

def block_forward(weights, rows, route_rows):
    gain_one, shift_one, joint_full, joint_shift, mixer_full, mixer_shift, gain_two, shift_two, router_full, up_full, up_shift, down_full, down_shift = weights
    token_count, width = rows.shape
    images = token_count // SEQ
    head_scale = HEAD_DIM ** (-0.5)
    normed_one = low(layer_norm(rows, gain_one, shift_one))
    shift_all = jnp.concatenate([joint_shift[0], jnp.zeros((width,), jnp.float32), joint_shift[1]])
    projected = low(low_back(jnp.dot(normed_one, joint_full, precision=highest) + shift_all))
    parted = projected.reshape(images, SEQ, 3, HEADS, HEAD_DIM)
    queries = parted[:, :, 0]
    key_rows = parted[:, :, 1]
    value_rows = parted[:, :, 2]
    scores = low_back(jnp.einsum('bqhd,bkhd->bhqk', queries, key_rows, precision=highest) * head_scale)
    attention = low(jax.nn.softmax(scores, axis=-1))
    mixed = jnp.einsum('bhqk,bkhd->bqhd', attention, value_rows, precision=highest).reshape(token_count, width)
    mixed = low(low_back(mixed))
    branch_one = low_back(jnp.dot(mixed, mixer_full, precision=highest) + mixer_shift)
    residual_one = rows + branch_one
    normed_two = low(layer_norm(residual_one, gain_two, shift_two))
    logits = low_back(jnp.dot(normed_two, router_full, precision=highest))
    router_probs = jax.nn.softmax(logits, axis=-1)
    experts = up_full.shape[0]
    position, owner = dispatch_tables(route_rows, experts, CAP)
    choose = (route_rows[:, :, None] == jnp.arange(experts, dtype=jnp.int32)[None, None, :]).astype(jnp.float32)
    gates = lax.optimization_barrier(jnp.sum(choose * router_probs[:, None, :], axis=-1))
    padded = jnp.concatenate([normed_two, jnp.zeros((1, width), jnp.float32)], axis=0)
    dispatched = padded[owner // 2].reshape(experts, CAP, width)
    hidden = low_back(jnp.einsum('ecd,edf->ecf', dispatched, up_full, precision=highest) + up_shift[:, None, :])
    active = low(jax.nn.gelu(hidden, approximate=False))
    expert_result = low_back(jnp.einsum('ecf,efd->ecd', active, down_full, precision=highest) + down_shift[:, None, :])
    picked = expert_result.reshape(experts * CAP, width)[position].reshape(token_count, 2, width)
    return residual_one + lax.optimization_barrier(jnp.sum(gates[:, :, None] * picked, axis=1))

def reference(tokens_in, routes, first_gain, first_shift, joint_weight, joint_bias, mixer_weight, mixer_bias, second_gain, second_shift, router_weight, expert_up, upward_bias, expert_down, downward_bias, out_grad):
    raw_params = (first_gain, first_shift, joint_weight, joint_bias, mixer_weight, mixer_bias, second_gain, second_shift, router_weight, expert_up, upward_bias, expert_down, downward_bias)
    params = tuple((weight_array.astype(jnp.float32) for weight_array in raw_params))
    block_count = TOKENS // TOK_DEV
    token_blocks = tokens_in.reshape(block_count, TOK_DEV, D)
    route_blocks = routes.reshape(block_count, TOK_DEV, 2)
    grad_blocks = out_grad.reshape(block_count, TOK_DEV, D)
    checked = jax.checkpoint(block_forward)

    def visit(totals, inputs):
        block_tokens, block_routes, block_grad = inputs

        def forward(weights, rows):
            return checked(weights, rows, block_routes)
        result, pullback = jax.vjp(forward, params, block_tokens)
        weight_grads, token_grads = pullback(block_grad)
        totals = jax.tree.map(lambda earlier_sum, block_sum: earlier_sum + block_sum, totals, weight_grads)
        return (totals, (result, token_grads))
    start_totals = jax.tree.map(jnp.zeros_like, params)
    totals, (outputs, token_grads) = lax.scan(visit, start_totals, (token_blocks, route_blocks, grad_blocks))
    block_out = outputs.reshape(TOKENS, D)
    input_grad = token_grads.reshape(TOKENS, D)
    return (block_out, input_grad, totals[0], totals[1], totals[2], totals[3], totals[4], totals[5], totals[6], totals[7], totals[8], totals[9], totals[10], totals[11], totals[12])
```

```python
import functools

import jax
import jax.numpy as jnp
from jax import lax
from jax.experimental import pallas as pl
from jax.experimental.pallas import tpu as pltpu
from jax.sharding import PartitionSpec as P

HEADS = 12
HEAD_DIM = 64
SEQ = 197
SLOTS = 624
GROUP = 4


epsilon = 1e-06


def layer_norm(values, gain, shift):
    centre = jnp.mean(values, axis=-1, keepdims=True)
    centred = values - centre
    spread = jnp.mean(centred * centred, axis=-1, keepdims=True)
    factor = lax.rsqrt(spread + epsilon)
    unit_rows = centred * factor
    return (unit_rows * gain + shift, unit_rows, factor)


def norm_back(upstream, unit_rows, factor, gain):
    scaled = upstream * gain
    middle = jnp.mean(scaled, axis=-1, keepdims=True)
    along = jnp.mean(scaled * unit_rows, axis=-1, keepdims=True)
    return factor * (scaled - middle - unit_rows * along)


def contract_first(left_rows, right_rows):
    return lax.dot_general(
        left_rows, right_rows, (((0,), (0,)), ((), ())), preferred_element_type=jnp.float32
    )


def contract_last(left_rows, right_rows):
    return lax.dot_general(
        left_rows, right_rows, (((1,), (1,)), ((), ())), preferred_element_type=jnp.float32
    )


def transposed(left_rows, right_rows):
    return lax.dot_general(
        left_rows, right_rows, (((1,), (1,)), ((), ())), preferred_element_type=jnp.float32
    )


def plain(left_rows, right_rows):
    return jnp.dot(left_rows, right_rows, preferred_element_type=jnp.float32)


def normal_parts(hidden):
    bell = jnp.exp(-0.5 * hidden * hidden)
    near = 1.0 / (1.0 + (0.3275911 * 0.7071067811865476) * jnp.abs(hidden))
    tail = near * (
        0.127414796
        + near * (-0.142248368 + near * (0.7107068705 + near * (-0.7265760135 + near * 0.5307027145)))
    )
    tail = tail * bell
    return jnp.where(hidden < 0.0, tail, 1.0 - tail), bell * 0.3989422804014327


def expert_kernel(steps, ways, *refs):
    low = jnp.bfloat16
    x_ref, g_ref, gate_ref, up_shift_ref, down_shift_ref = refs[:5]
    refs = refs[5:]
    pieces = [refs[k * ways : (k + 1) * ways] for k in range(steps)]
    refs = refs[steps * ways :]
    out_ref, dx_ref, gate_grad_ref, up_shift_grad_ref, down_shift_grad_ref = refs[:5]
    refs = refs[5:]
    grads = [refs[k * ways : (k + 1) * ways] for k in range(steps)]
    refs = refs[steps * ways :]
    rg, xt, rgt, act, hg, y_sum, dx_sum, weights, grad_buf, in_sem, out_sem, end_sem = refs
    rows, width = x_ref.shape
    part = pieces[0][0].shape[2]
    block = part * ways
    chunk = SLOTS
    chunks = rows // chunk

    def load(step):
        return [
            pltpu.make_async_copy(
                pieces[step][j],
                weights.at[step % 2, :, :, pl.ds(j * part, part)],
                in_sem.at[step % 2, j],
            )
            for j in range(ways)
        ]

    def save(step):
        return [
            pltpu.make_async_copy(
                grad_buf.at[:, :, pl.ds(j * part, part)], grads[step][j], out_sem.at[j]
            )
            for j in range(ways)
        ]

    for copy in load(0):
        copy.start()

    down_shift_grad_ref[...] = jnp.zeros_like(down_shift_grad_ref)

    @pl.loop(0, chunks)
    def _(c):
        span = pl.ds(pl.multiple_of(c * chunk, chunk), chunk)
        scaled = (g_ref[span, :].astype(jnp.float32) * gate_ref[span, :]).astype(low)
        rg[span, :] = scaled
        down_shift_grad_ref[...] += jnp.sum(scaled.astype(jnp.float32), axis=0, keepdims=True)
        y_sum[span, :] = jnp.zeros((chunk, width), jnp.float32)
        dx_sum[span, :] = jnp.zeros((chunk, width), jnp.float32)

    for start in range(0, width, 256):
        xt[start : start + 256, :] = x_ref[:, start : start + 256].T
        rgt[start : start + 256, :] = rg[:, start : start + 256].T

    for step in range(steps):
        for copy in load(step):
            copy.wait()
        if step + 1 < steps:
            for copy in load(step + 1):
                copy.start()
        slot = step % 2
        up_shift_grad_ref[step] = jnp.zeros((1, block), jnp.float32)

        @pl.loop(0, chunks)
        def _(c):
            span = pl.ds(pl.multiple_of(c * chunk, chunk), chunk)
            x_rows = x_ref[span, :]
            g_rows = rg[span, :]
            for start in range(0, block, 256):
                part_span = slice(start, start + 256)
                hidden = plain(x_rows, weights[slot, 0, :, part_span]) + up_shift_ref[step, :, part_span]
                back = plain(g_rows, weights[slot, 1, :, part_span])
                cdf, density = normal_parts(hidden)
                act[span, part_span] = (hidden * cdf).astype(low)
                hidden_grad = (back * (cdf + hidden * density)).astype(low)
                hg[span, part_span] = hidden_grad
                up_shift_grad_ref[step, :, part_span] += jnp.sum(
                    hidden_grad.astype(jnp.float32), axis=0, keepdims=True
                )
            y_sum[span, :] += transposed(act[span, :], weights[slot, 1])
            dx_sum[span, :] += transposed(hg[span, :], weights[slot, 0])

        if step > 0:
            for copy in save(step - 1):
                copy.wait()

        @pl.loop(0, width // 256)
        def _(c):
            span = pl.ds(pl.multiple_of(c * 256, 256), 256)
            grad_buf[0, span, :] = plain(xt[span, :], hg[...]).astype(low)
            grad_buf[1, span, :] = plain(rgt[span, :], act[...]).astype(low)

        for copy in save(step):
            copy.start()

    @pl.loop(0, chunks)
    def _(c):
        span = pl.ds(pl.multiple_of(c * chunk, chunk), chunk)
        hg[span, :width] = dx_sum[span, :].astype(low)
        result = y_sum[span, :] + down_shift_ref[...]
        act[span, :width] = (result * gate_ref[span, :]).astype(low)
        gate_grad_ref[span, :] = jnp.sum(
            result * g_ref[span, :].astype(jnp.float32), axis=1, keepdims=True
        )

    ends = [
        pltpu.make_async_copy(act.at[:, pl.ds(0, width)], out_ref, end_sem.at[0]),
        pltpu.make_async_copy(hg.at[:, pl.ds(0, width)], dx_ref, end_sem.at[1]),
    ]
    for copy in ends:
        copy.start()
    for copy in save(steps - 1) + ends:
        copy.wait()


def run_expert(rows_in, grad_in, gate_in, up_shift, down_shift, pieces):
    steps, ways = len(pieces), len(pieces[0])
    _, width, part = pieces[0][0].shape
    rows = rows_in.shape[0]
    block = part * ways
    low = jnp.bfloat16
    everywhere = pl.BlockSpec(memory_space=pl.ANY)
    local = pl.BlockSpec(memory_space=pltpu.VMEM)
    flat = [piece for line in pieces for piece in line]
    outs = pl.pallas_call(
        functools.partial(expert_kernel, steps, ways),
        name="expert_block",
        out_shape=[
            jax.ShapeDtypeStruct((rows, width), low),
            jax.ShapeDtypeStruct((rows, width), low),
            jax.ShapeDtypeStruct((rows, 1), jnp.float32),
            jax.ShapeDtypeStruct((steps, 1, block), jnp.float32),
            jax.ShapeDtypeStruct((1, width), jnp.float32),
        ]
        + [jax.ShapeDtypeStruct((2, width, part), low) for _ in flat],
        in_specs=[local] * 5 + [everywhere] * len(flat),
        out_specs=[everywhere, everywhere, local, local, local] + [everywhere] * len(flat),
        scratch_shapes=[
            pltpu.VMEM((rows, width), low),
            pltpu.VMEM((width, rows), low),
            pltpu.VMEM((width, rows), low),
            pltpu.VMEM((rows, block), low),
            pltpu.VMEM((rows, block), low),
            pltpu.VMEM((rows, width), jnp.float32),
            pltpu.VMEM((rows, width), jnp.float32),
            pltpu.VMEM((2, 2, width, block), low),
            pltpu.VMEM((2, width, block), low),
            pltpu.SemaphoreType.DMA((2, ways)),
            pltpu.SemaphoreType.DMA((ways,)),
            pltpu.SemaphoreType.DMA((2,)),
        ],
        compiler_params=pltpu.CompilerParams(vmem_limit_bytes=63 * 2**20),
        cost_estimate=pl.CostEstimate(
            flops=12 * rows * width * block * steps,
            bytes_accessed=12 * rows * width + 8 * width * block * steps,
            transcendentals=rows * block * steps,
        ),
    )(rows_in, grad_in, gate_in, up_shift, down_shift, *flat)
    grads = outs[5:]
    return list(outs[:5]) + [[grads[k * ways : (k + 1) * ways] for k in range(steps)]]


def slot_table(routes, chosen, slots):
    token_count = routes.shape[0]
    hits = (routes[:, :, None] == chosen[None, None, :]).any(axis=1)
    rows = lax.broadcasted_iota(jnp.int32, (token_count, token_count), 0)
    columns = lax.broadcasted_iota(jnp.int32, (token_count, token_count), 1)
    earlier = jnp.dot(
        (columns < rows).astype(jnp.bfloat16),
        hits.astype(jnp.bfloat16),
        preferred_element_type=jnp.float32,
    ).astype(jnp.int32)
    slot_of = jnp.where(hits, earlier, -1).T
    return slot_of[:, None, :] == jnp.arange(slots, dtype=jnp.int32)[None, :, None]


def shard_shift(value, lines, ways, along, across):
    pairs = [
        (line * ways + way, (line + along) % lines * ways + (way + across) % ways)
        for line in range(lines)
        for way in range(ways)
    ]
    return lax.ppermute(value, "shard", pairs)


def group_shift(value, copies, along):
    pairs = [
        (copy, copy // GROUP * GROUP + (copy % GROUP + along) % GROUP) for copy in range(copies)
    ]
    return lax.ppermute(value, "rep", pairs)


def exchange(blocks, copies):
    return [blocks[0]] + [group_shift(blocks[k], copies, k) for k in range(1, GROUP)]


def exchange_back(blocks, copies):
    return [blocks[0]] + [group_shift(blocks[k], copies, -k) for k in range(1, GROUP)]


def gather_all(piece):
    return lax.all_gather(piece, ("shard", "rep"), axis=0, tiled=True)


def my_piece(rows, copies):
    count = rows.shape[0] // copies
    return lax.dynamic_slice_in_dim(rows, lax.axis_index("rep") * count, count, axis=0)


def sum_rows(rows):
    return lax.psum_scatter(rows, ("shard", "rep"), scatter_dimension=0, tiled=True)


def share_rows(rows):
    return lax.all_gather(rows, "rep", axis=0, tiled=True)


def shards(
    tokens_in,
    routes,
    first_gain,
    first_shift,
    joint_weight,
    joint_bias,
    mixer_weight,
    mixer_bias,
    second_gain,
    second_shift,
    router_weight,
    expert_up,
    upward_bias,
    expert_down,
    downward_bias,
    out_grad,
    *,
    groups,
    copies,
):
    token_count, width = tokens_in.shape
    experts, _, part = expert_up.shape
    strip = first_gain.shape[0]
    hidden_width = part * groups
    images = token_count // SEQ
    head_scale = HEAD_DIM ** (-0.5)
    low = jnp.bfloat16
    bias_columns = experts * part // strip

    packed = jnp.concatenate(
        [
            joint_weight,
            mixer_weight,
            router_weight,
            first_gain[:, None],
            first_shift[:, None],
            joint_bias.T,
            mixer_bias[:, None],
            second_gain[:, None],
            second_shift[:, None],
            downward_bias.T,
            upward_bias.reshape(strip, bias_columns),
        ],
        axis=1,
    )
    used = packed.shape[1]
    packed_width = -(-used // 128) * 128
    packed = jnp.pad(packed, ((0, 0), (0, packed_width - used)))
    packed = gather_all(my_piece(packed, copies))
    lines = 4 if groups % 4 == 0 else 1
    ways = groups // lines
    me = lax.axis_index("rep") % GROUP
    shard = lax.axis_index("shard")
    mine = jnp.stack(
        [
            lax.dynamic_index_in_dim(expert_up, me, 0, keepdims=False),
            lax.dynamic_index_in_dim(expert_down, me, 0, keepdims=False).T,
        ]
    )
    pieces = []
    for k in range(lines):
        first = mine if k == 0 else shard_shift(mine, lines, ways, -k, 0)
        pieces.append([first] + [shard_shift(first, lines, ways, 0, -j) for j in range(1, ways)])
    near_shards = jnp.stack(
        [
            (shard // ways + k) % lines * ways + (shard % ways + j) % ways
            for k in range(lines)
            for j in range(ways)
        ]
    )
    near_experts = (me + jnp.arange(GROUP, dtype=jnp.int32)) % GROUP

    joint_full = packed[:, : 3 * width]
    mixer_full = packed[:, 3 * width : 4 * width]
    tail = packed[:, 4 * width :]
    router_full = tail[:, :experts]
    vectors = tail[:, experts : experts + 7].astype(jnp.float32).T
    gain_one, shift_one, shift_query, shift_value, mixer_shift, gain_two, shift_two = [
        vectors[i] for i in range(7)
    ]
    down_shift = tail[:, experts + 7 : 2 * experts + 7].astype(jnp.float32).T
    up_shift = (
        tail[:, 2 * experts + 7 : 2 * experts + 7 + bias_columns]
        .reshape(groups, experts, part)
        .astype(jnp.float32)
    )
    up_shift = lax.dynamic_index_in_dim(up_shift, me, 1, keepdims=False)[near_shards]
    up_shift = up_shift.reshape(lines, 1, ways * part)
    down_shift = lax.dynamic_index_in_dim(down_shift, me, 0, keepdims=True)
    normed_one, unit_one, factor_one = layer_norm(tokens_in, gain_one, shift_one)
    normed_one = normed_one.astype(low)
    shift_all = jnp.concatenate([shift_query, jnp.zeros((width,), jnp.float32), shift_value])
    projected = (
        jnp.dot(normed_one, joint_full, preferred_element_type=jnp.float32) + shift_all
    ).astype(low)
    parted = projected.reshape(images, SEQ, 3, HEADS, HEAD_DIM)
    queries = parted[:, :, 0]
    key_rows = parted[:, :, 1]
    value_rows = parted[:, :, 2]
    scores = (
        jnp.einsum("bqhd,bkhd->bhqk", queries, key_rows, preferred_element_type=jnp.float32)
        * head_scale
    )
    highest_score = jnp.max(scores, axis=-1, keepdims=True)
    log_total = highest_score + jnp.log(
        jnp.sum(jnp.exp(scores - highest_score), axis=-1, keepdims=True)
    )
    attention = jnp.exp(scores - log_total).astype(low)
    mixed = jnp.einsum("bhqk,bkhd->bqhd", attention, value_rows, preferred_element_type=jnp.float32)
    mixed = mixed.reshape(token_count, width).astype(low)
    residual_one = tokens_in + (
        jnp.dot(mixed, mixer_full, preferred_element_type=jnp.float32) + mixer_shift
    )
    normed_two, unit_two, factor_two = layer_norm(residual_one, gain_two, shift_two)
    normed_two = normed_two.astype(low)
    logits = jnp.dot(normed_two, router_full, preferred_element_type=jnp.float32)
    router_probs = jax.nn.softmax(logits, axis=-1)

    probs_near = router_probs[:, near_experts]
    seated = slot_table(routes, near_experts, SLOTS)
    seats = seated.astype(low)
    flat_seats = seats.reshape(experts * SLOTS, token_count)
    gate_slots = jnp.sum(jnp.where(seated, probs_near.T[:, None, :], 0.0), axis=-1)
    dispatched = (
        jnp.dot(flat_seats, normed_two, preferred_element_type=jnp.float32)
        .astype(low)
        .reshape(experts, SLOTS, width)
    )
    grad_slots = (
        jnp.dot(flat_seats, out_grad.astype(low), preferred_element_type=jnp.float32)
        .astype(low)
        .reshape(experts, SLOTS, width)
    )
    grad_in = jnp.concatenate(exchange(grad_slots, copies), axis=0)
    rows_in = jnp.concatenate(exchange(dispatched, copies), axis=0)
    gate_in = jnp.concatenate(exchange(gate_slots, copies), axis=0)[:, None]
    if part % 128:
        joined = [[jnp.concatenate(line, axis=2)] for line in pieces]
    else:
        joined = pieces
    weighted, dispatched_grad, gate_grad, up_shift_grad, down_shift_grad, grads = run_expert(
        rows_in, grad_in, gate_in, up_shift, down_shift, joined
    )
    if part % 128:
        grads = [
            [line[0][:, :, j * part : (j + 1) * part] for j in range(ways)] for line in grads
        ]

    sums = []
    for k in range(lines):
        total = grads[k][0].astype(jnp.float32)
        for j in range(1, ways):
            total = total + shard_shift(grads[k][j], lines, ways, 0, j).astype(jnp.float32)
        sums.append(total)
    total = sums[0]
    for k in range(1, lines):
        total = total + shard_shift(sums[k].astype(low), lines, ways, k, 0).astype(jnp.float32)
    expert_grads = lax.all_gather(total.astype(low), "rep", axis=0)
    expert_grads = expert_grads.astype(jnp.float32).reshape(-1, GROUP, 2, width, part).sum(axis=0)
    up_grad = expert_grads[:, 0]
    down_grad = expert_grads[:, 1].transpose(0, 2, 1)

    blocks = (GROUP, SLOTS, width)
    dispatched_grad = jnp.concatenate(
        exchange_back(dispatched_grad.reshape(blocks), copies), axis=0
    )
    weighted = jnp.concatenate(exchange_back(weighted.reshape(blocks), copies), axis=0)
    gate_grad = jnp.stack(exchange_back(gate_grad.reshape(GROUP, SLOTS), copies))
    block_out = residual_one + contract_first(flat_seats, weighted)
    probs_grad = jnp.sum(jnp.where(seated, gate_grad[:, :, None], 0.0), axis=1).T
    probs_grad = probs_grad[:, (jnp.arange(GROUP, dtype=jnp.int32) - me) % GROUP]
    own = (jnp.arange(experts, dtype=jnp.int32) == me).astype(jnp.float32)[:, None]
    down_shift_grad = own * down_shift_grad
    up_shift_grad = jnp.zeros((groups, part), jnp.float32).at[near_shards].set(
        up_shift_grad.reshape(groups, part)
    )
    up_shift_grad = own * up_shift_grad.reshape(1, hidden_width)
    logit_grad = (
        router_probs * (probs_grad - jnp.sum(router_probs * probs_grad, axis=-1, keepdims=True))
    ).astype(low)
    router_grad = contract_first(normed_two, logit_grad)
    normed_grad = contract_last(logit_grad, router_full) + contract_first(
        flat_seats, dispatched_grad
    )
    gain_two_grad = jnp.sum(normed_grad * unit_two, axis=0)
    shift_two_grad = jnp.sum(normed_grad, axis=0)
    residual_grad = out_grad + norm_back(normed_grad, unit_two, factor_two, gain_two)
    mixer_in_grad = residual_grad.astype(low)
    mixer_shift_grad = jnp.sum(mixer_in_grad.astype(jnp.float32), axis=0)
    mixer_grad = contract_first(mixed, mixer_in_grad)
    mixed_grad = (
        contract_last(mixer_in_grad, mixer_full)
        .astype(low)
        .reshape(images, SEQ, HEADS, HEAD_DIM)
    )
    scores_again = (
        jnp.einsum("bqhd,bkhd->bhqk", queries, key_rows, preferred_element_type=jnp.float32)
        * head_scale
    )
    attention_full = jnp.exp(scores_again - log_total)
    attention_low = attention_full.astype(low)
    weight_grad = jnp.einsum(
        "bqhd,bkhd->bhqk", mixed_grad, value_rows, preferred_element_type=jnp.float32
    )
    centre_grad = jnp.sum(attention_full * weight_grad, axis=-1, keepdims=True)
    score_grad = (attention_full * (weight_grad - centre_grad)).astype(low)
    query_grad = (
        jnp.einsum("bhqk,bkhd->bqhd", score_grad, key_rows, preferred_element_type=jnp.float32)
        * head_scale
    ).astype(low)
    key_grad = (
        jnp.einsum("bhqk,bqhd->bkhd", score_grad, queries, preferred_element_type=jnp.float32)
        * head_scale
    ).astype(low)
    value_grad = jnp.einsum(
        "bhqk,bqhd->bkhd", attention_low, mixed_grad, preferred_element_type=jnp.float32
    ).astype(low)
    projected_grad = jnp.concatenate(
        [
            query_grad.reshape(token_count, width),
            key_grad.reshape(token_count, width),
            value_grad.reshape(token_count, width),
        ],
        axis=1,
    )
    joint_sums = jnp.sum(projected_grad.astype(jnp.float32), axis=0)
    joint_grad = contract_first(normed_one, projected_grad)
    first_grad = contract_last(projected_grad, joint_full)
    gain_one_grad = jnp.sum(first_grad * unit_one, axis=0)
    shift_one_grad = jnp.sum(first_grad, axis=0)
    input_grad = residual_grad + norm_back(first_grad, unit_one, factor_one, gain_one)

    small = jnp.stack(
        [
            gain_one_grad,
            shift_one_grad,
            joint_sums[:width],
            joint_sums[2 * width :],
            mixer_shift_grad,
            gain_two_grad,
            shift_two_grad,
        ],
        axis=1,
    )
    packed_grad = jnp.concatenate(
        [
            joint_grad.astype(low),
            mixer_grad.astype(low),
            router_grad.astype(low),
            small.astype(low),
            down_shift_grad.T.astype(low),
            up_shift_grad.astype(low)
            .reshape(experts, groups, part)
            .transpose(1, 0, 2)
            .reshape(groups * strip, bias_columns),
        ],
        axis=1,
    )
    packed_grad = jnp.pad(packed_grad, ((0, 0), (0, packed_width - used)))
    packed_grad = share_rows(sum_rows(packed_grad)).astype(jnp.float32)
    end = packed_grad[:, 4 * width :]
    line = end[:, experts : experts + 7].T
    return (
        block_out,
        input_grad,
        line[0],
        line[1],
        packed_grad[:, : 3 * width],
        line[2:4],
        packed_grad[:, 3 * width : 4 * width],
        line[4],
        line[5],
        line[6],
        end[:, :experts],
        up_grad,
        end[:, 2 * experts + 7 : 2 * experts + 7 + bias_columns].reshape(experts, part),
        down_grad,
        end[:, experts + 7 : 2 * experts + 7].T,
    )


def solution(mesh):
    placed = (
        P(("shard", "rep"), None),
        P(("shard", "rep"), None),
        P("shard"),
        P("shard"),
        P("shard", None),
        P(None, "shard"),
        P("shard", None),
        P("shard"),
        P("shard"),
        P("shard"),
        P("shard", None),
        P(None, None, "shard"),
        P(None, "shard"),
        P(None, "shard", None),
        P(None, "shard"),
        P(("shard", "rep"), None),
    )
    return jax.shard_map(
        functools.partial(
            shards, groups=mesh.shape["shard"], copies=mesh.shape["rep"]
        ),
        mesh=mesh,
        in_specs=placed,
        out_specs=(
            P(("shard", "rep"), None),
            P(("shard", "rep"), None),
            P("shard"),
            P("shard"),
            P("shard", None),
            P(None, "shard"),
            P("shard", None),
            P("shard"),
            P("shard"),
            P("shard"),
            P("shard", None),
            P(None, None, "shard"),
            P(None, "shard"),
            P(None, "shard", None),
            P(None, "shard"),
        ),
        check_vma=False,
    )
```

```python
import functools

import jax
import jax.numpy as jnp
from jax import lax
from jax.experimental import pallas as pl
from jax.experimental.pallas import tpu as pltpu
from jax.sharding import PartitionSpec as P

HEADS = 12
HEAD_DIM = 64
SEQ = 197
SLOTS = 624
PADDED = 208
GROUP = 4


epsilon = 1e-06


def layer_norm(values, gain, shift):
    centre = jnp.mean(values, axis=-1, keepdims=True)
    centred = values - centre
    spread = jnp.mean(centred * centred, axis=-1, keepdims=True)
    factor = lax.rsqrt(spread + epsilon)
    unit_rows = centred * factor
    return (unit_rows * gain + shift, unit_rows, factor)


def norm_back(upstream, unit_rows, factor, gain):
    scaled = upstream * gain
    middle = jnp.mean(scaled, axis=-1, keepdims=True)
    along = jnp.mean(scaled * unit_rows, axis=-1, keepdims=True)
    return factor * (scaled - middle - unit_rows * along)


def contract_first(left_rows, right_rows):
    return lax.dot_general(
        left_rows, right_rows, (((0,), (0,)), ((), ())), preferred_element_type=jnp.float32
    )


def contract_last(left_rows, right_rows):
    return lax.dot_general(
        left_rows, right_rows, (((1,), (1,)), ((), ())), preferred_element_type=jnp.float32
    )


def transposed(left_rows, right_rows):
    return lax.dot_general(
        left_rows, right_rows, (((1,), (1,)), ((), ())), preferred_element_type=jnp.float32
    )


def plain(left_rows, right_rows):
    return jnp.dot(left_rows, right_rows, preferred_element_type=jnp.float32)


def normal_parts(hidden):
    bell = jnp.exp(-0.5 * hidden * hidden)
    near = 1.0 / (1.0 + (0.3275911 * 0.7071067811865476) * jnp.abs(hidden))
    tail = near * (
        0.127414796
        + near * (-0.142248368 + near * (0.7107068705 + near * (-0.7265760135 + near * 0.5307027145)))
    )
    tail = tail * bell
    return jnp.where(hidden < 0.0, tail, 1.0 - tail), bell * 0.3989422804014327


def expert_kernel(steps, ways, *refs):
    low = jnp.bfloat16
    x_ref, g_ref, gate_ref, up_shift_ref, down_shift_ref = refs[:5]
    refs = refs[5:]
    pieces = [refs[k * ways : (k + 1) * ways] for k in range(steps)]
    refs = refs[steps * ways :]
    out_ref, dx_ref, gate_grad_ref, up_shift_grad_ref, down_shift_grad_ref = refs[:5]
    refs = refs[5:]
    grads = [refs[k * ways : (k + 1) * ways] for k in range(steps)]
    refs = refs[steps * ways :]
    rg, xt, rgt, act, hg, y_sum, dx_sum, weights, grad_buf, in_sem, out_sem, end_sem = refs
    rows, width = x_ref.shape
    part = pieces[0][0].shape[2]
    block = part * ways
    chunk = SLOTS
    chunks = rows // chunk

    def load(step):
        return [
            pltpu.make_async_copy(
                pieces[step][j],
                weights.at[step % 2, :, :, pl.ds(j * part, part)],
                in_sem.at[step % 2, j],
            )
            for j in range(ways)
        ]

    def save(step):
        return [
            pltpu.make_async_copy(
                grad_buf.at[:, :, pl.ds(j * part, part)], grads[step][j], out_sem.at[j]
            )
            for j in range(ways)
        ]

    for copy in load(0):
        copy.start()

    down_shift_grad_ref[...] = jnp.zeros_like(down_shift_grad_ref)

    @pl.loop(0, chunks)
    def _(c):
        span = pl.ds(pl.multiple_of(c * chunk, chunk), chunk)
        scaled = (g_ref[span, :].astype(jnp.float32) * gate_ref[span, :]).astype(low)
        rg[span, :] = scaled
        down_shift_grad_ref[...] += jnp.sum(scaled.astype(jnp.float32), axis=0, keepdims=True)
        y_sum[span, :] = jnp.zeros((chunk, width), jnp.float32)
        dx_sum[span, :] = jnp.zeros((chunk, width), jnp.float32)

    for start in range(0, width, 256):
        xt[start : start + 256, :] = x_ref[:, start : start + 256].T
        rgt[start : start + 256, :] = rg[:, start : start + 256].T

    for step in range(steps):
        for copy in load(step):
            copy.wait()
        if step + 1 < steps:
            for copy in load(step + 1):
                copy.start()
        slot = step % 2
        up_shift_grad_ref[step] = jnp.zeros((1, block), jnp.float32)

        @pl.loop(0, chunks)
        def _(c):
            span = pl.ds(pl.multiple_of(c * chunk, chunk), chunk)
            x_rows = x_ref[span, :]
            g_rows = rg[span, :]
            for start in range(0, block, 256):
                part_span = slice(start, start + 256)
                hidden = plain(x_rows, weights[slot, 0, :, part_span]) + up_shift_ref[step, :, part_span]
                back = plain(g_rows, weights[slot, 1, :, part_span])
                cdf, density = normal_parts(hidden)
                act[span, part_span] = (hidden * cdf).astype(low)
                hidden_grad = (back * (cdf + hidden * density)).astype(low)
                hg[span, part_span] = hidden_grad
                up_shift_grad_ref[step, :, part_span] += jnp.sum(
                    hidden_grad.astype(jnp.float32), axis=0, keepdims=True
                )
            y_sum[span, :] += transposed(act[span, :], weights[slot, 1])
            dx_sum[span, :] += transposed(hg[span, :], weights[slot, 0])

        if step > 0:
            for copy in save(step - 1):
                copy.wait()

        @pl.loop(0, width // 256)
        def _(c):
            span = pl.ds(pl.multiple_of(c * 256, 256), 256)
            grad_buf[0, span, :] = plain(xt[span, :], hg[...]).astype(low)
            grad_buf[1, span, :] = plain(rgt[span, :], act[...]).astype(low)

        for copy in save(step):
            copy.start()

    @pl.loop(0, chunks)
    def _(c):
        span = pl.ds(pl.multiple_of(c * chunk, chunk), chunk)
        hg[span, :width] = dx_sum[span, :].astype(low)
        result = y_sum[span, :] + down_shift_ref[...]
        act[span, :width] = (result * gate_ref[span, :]).astype(low)
        gate_grad_ref[span, :] = jnp.sum(
            result * g_ref[span, :].astype(jnp.float32), axis=1, keepdims=True
        )

    ends = [
        pltpu.make_async_copy(act.at[:, pl.ds(0, width)], out_ref, end_sem.at[0]),
        pltpu.make_async_copy(hg.at[:, pl.ds(0, width)], dx_ref, end_sem.at[1]),
    ]
    for copy in ends:
        copy.start()
    for copy in save(steps - 1) + ends:
        copy.wait()


def run_expert(rows_in, grad_in, gate_in, up_shift, down_shift, pieces):
    steps, ways = len(pieces), len(pieces[0])
    _, width, part = pieces[0][0].shape
    rows = rows_in.shape[0]
    block = part * ways
    low = jnp.bfloat16
    everywhere = pl.BlockSpec(memory_space=pl.ANY)
    local = pl.BlockSpec(memory_space=pltpu.VMEM)
    flat = [piece for line in pieces for piece in line]
    outs = pl.pallas_call(
        functools.partial(expert_kernel, steps, ways),
        name="expert_block",
        out_shape=[
            jax.ShapeDtypeStruct((rows, width), low),
            jax.ShapeDtypeStruct((rows, width), low),
            jax.ShapeDtypeStruct((rows, 1), jnp.float32),
            jax.ShapeDtypeStruct((steps, 1, block), jnp.float32),
            jax.ShapeDtypeStruct((1, width), jnp.float32),
        ]
        + [jax.ShapeDtypeStruct((2, width, part), low) for _ in flat],
        in_specs=[local] * 5 + [everywhere] * len(flat),
        out_specs=[everywhere, everywhere, local, local, local] + [everywhere] * len(flat),
        scratch_shapes=[
            pltpu.VMEM((rows, width), low),
            pltpu.VMEM((width, rows), low),
            pltpu.VMEM((width, rows), low),
            pltpu.VMEM((rows, block), low),
            pltpu.VMEM((rows, block), low),
            pltpu.VMEM((rows, width), jnp.float32),
            pltpu.VMEM((rows, width), jnp.float32),
            pltpu.VMEM((2, 2, width, block), low),
            pltpu.VMEM((2, width, block), low),
            pltpu.SemaphoreType.DMA((2, ways)),
            pltpu.SemaphoreType.DMA((ways,)),
            pltpu.SemaphoreType.DMA((2,)),
        ],
        compiler_params=pltpu.CompilerParams(vmem_limit_bytes=63 * 2**20),
        cost_estimate=pl.CostEstimate(
            flops=12 * rows * width * block * steps,
            bytes_accessed=12 * rows * width + 8 * width * block * steps,
            transcendentals=rows * block * steps,
        ),
    )(rows_in, grad_in, gate_in, up_shift, down_shift, *flat)
    grads = outs[5:]
    return list(outs[:5]) + [[grads[k * ways : (k + 1) * ways] for k in range(steps)]]


def side_by_side(first, second):
    lane = lax.broadcasted_iota(jnp.int32, first.shape, 1)
    return jnp.where(lane < HEAD_DIM, first, second)


def head_of(pair, which):
    lane = lax.broadcasted_iota(jnp.int32, pair.shape, 1)
    keep = lane < HEAD_DIM if which == 0 else lane >= HEAD_DIM
    return jnp.where(keep, pair, jnp.zeros_like(pair))


def key_probs(query_pair, key_pair, which):
    scores = transposed(head_of(query_pair, which), key_pair) * HEAD_DIM ** (-0.5)
    column = lax.broadcasted_iota(jnp.int32, scores.shape, 1)
    scores = jnp.where(column < SEQ, scores, -1e30)
    raised = jnp.exp(scores - jnp.max(scores, axis=-1, keepdims=True))
    return raised * (1.0 / jnp.sum(raised, axis=-1, keepdims=True))


def forward_kernel(lines, ways, copies, *refs):
    low = jnp.bfloat16
    tokens_ref, packed_ref, mine_ref = refs[:3]
    refs = refs[3:]
    projected_ref, mixed_ref, residual_ref, normed_ref, logits_ref, weights_out = refs[:6]
    refs = refs[6:]
    pieces = [refs[k * ways : (k + 1) * ways] for k in range(lines)]
    refs = refs[lines * ways :]
    full, vectors = refs[:2]
    own_sem, save_sem = refs[2:4]
    line_sem, way_sem, core_sem, piece_line_sem, piece_way_sem = refs[4:]

    images, padded, width = tokens_ref.shape
    strip = packed_ref.shape[1]
    shard = lax.axis_index("shard")
    rep = lax.axis_index("rep")
    line, way = shard // ways, shard % ways
    half = rep % 2

    def place(k, j):
        return lax.rem(line + k + lines, lines) * ways + lax.rem(way + j + ways, ways)

    def at_shard(index):
        return {"shard": index}

    partner = {"rep": rep + 1 - 2 * half}
    friends = [at_shard(place(k, 0)) for k in range(1, lines)]
    friends += [at_shard(place(0, j)) for j in range(1, ways)] + [partner]
    barrier = pltpu.get_barrier_semaphore()
    for friend in friends:
        pl.semaphore_signal(barrier, inc=1, device_id=friend, device_id_type=pl.DeviceIdType.MESH)
    pl.semaphore_wait(barrier, len(friends))

    def remote(source, target, sems, index, device):
        return pltpu.make_async_remote_copy(
            src_ref=source,
            dst_ref=target,
            send_sem=sems.at[(0,) + index],
            recv_sem=sems.at[(1,) + index],
            device_id=device,
            device_id_type=pl.DeviceIdType.MESH,
        )

    def strip_of(k, j, side):
        rows = pl.ds(pl.multiple_of(place(k, j) * strip, strip), strip)
        return full.at[side, rows, :]

    def strip_line(k):
        return remote(packed_ref.at[half], strip_of(0, 0, half), line_sem, (k,), at_shard(place(-k, 0)))

    def strip_way(k, j):
        source = packed_ref.at[half] if k == 0 else strip_of(k, 0, half)
        return remote(source, strip_of(k, 0, half), way_sem, (k, j), at_shard(place(0, -j)))

    def strip_core(k, j):
        return remote(strip_of(k, j, half), strip_of(k, j, half), core_sem, (k, j), partner)

    def piece_line(k, u):
        return remote(
            mine_ref.at[u], pieces[k][0].at[u], piece_line_sem, (k, u), at_shard(place(-k, 0))
        )

    def piece_way(k, j, u):
        source = mine_ref.at[u] if k == 0 else pieces[k][0].at[u]
        return remote(source, pieces[k][j].at[u], piece_way_sem, (k, j, u), at_shard(place(0, -j)))

    own = pltpu.make_async_copy(
        packed_ref, full.at[:, pl.ds(pl.multiple_of(shard * strip, strip), strip), :], own_sem.at[0]
    )
    own_piece = pltpu.make_async_copy(mine_ref, pieces[0][0], own_sem.at[1])
    order = [k for k in (1, lines - 1, 2) if 0 < k < lines]
    order = list(dict.fromkeys(order))
    own.start()
    for k in order:
        strip_line(k).start()
    for j in range(1, ways):
        strip_way(0, j).start()
    own_piece.start()
    for j in range(1, ways):
        strip_way(0, j).wait_recv()
        strip_core(0, j).start()
    for k in order:
        strip_line(k).wait_recv()
        for j in range(1, ways):
            strip_way(k, j).start()
        strip_core(k, 0).start()
    for u in range(2):
        for k in order:
            piece_line(k, u).start()
        for j in range(1, ways):
            piece_way(0, j, u).start()
    for k in order:
        for j in range(1, ways):
            strip_way(k, j).wait_recv()
            strip_core(k, j).start()
    for k in range(lines):
        for j in range(ways):
            if k or j:
                strip_core(k, j).wait_recv()
    own.wait()
    save = pltpu.make_async_copy(full, weights_out, save_sem.at[0])
    save.start()

    vectors[...] = full[1, :, 1408:1536].astype(jnp.float32).T

    def pass_on(k, u):
        piece_line(k, u).wait_recv()
        for j in range(1, ways):
            piece_way(k, j, u).start()

    events = [(k, u) for u in range(2) for k in order]

    @pl.loop(0, images)
    def _(i):
        rows = tokens_ref[i]
        normed, _, _ = layer_norm(rows, vectors[4:5, :], vectors[5:6, :])
        normed = normed.astype(low)
        left = plain(normed, full[0])
        projected_ref[i, :, 0:768] = (left[:, 0:768] + vectors[6:7, :]).astype(low)
        projected_ref[i, :, 768:1536] = left[:, 768:1536].astype(low)
        right = plain(normed, full[1, :, 0:640])
        projected_ref[i, :, 1536:1664] = (left[:, 1536:1664] + vectors[7:8, 0:128]).astype(low)
        projected_ref[i, :, 1664:2304] = (right + vectors[7:8, 128:768]).astype(low)
        for pair in range(HEADS // 2):
            start = 128 * pair
            query_pair = projected_ref[i, :, start : start + 128]
            key_pair = projected_ref[i, :, 768 + start : 896 + start]
            value_pair = projected_ref[i, :, 1536 + start : 1664 + start]
            parts = [
                plain(key_probs(query_pair, key_pair, which).astype(low), value_pair)
                for which in (0, 1)
            ]
            mixed_ref[i, :, start : start + 128] = side_by_side(*parts).astype(low)
        residual = rows + (plain(mixed_ref[i], full[1, :, 640:1408]) + vectors[8:9, :])
        residual_ref[i] = residual
        normed_two, _, _ = layer_norm(residual, vectors[9:10, :], vectors[10:11, :])
        normed_two = normed_two.astype(low)
        normed_ref[i] = normed_two
        logits_ref[i] = plain(normed_two, full[1, :, 1408:1536])

        for number, event in enumerate(events[:2]):

            @pl.when(i == 2 * number + 1)
            def _():
                pass_on(*event)

    done = min(2, len(events)) if images >= 4 else 0
    for event in events[done:]:
        pass_on(*event)
    for u in range(2):
        for k in range(lines):
            for j in range(1, ways):
                piece_way(k, j, u).wait_recv()
    save.wait()
    own_piece.wait()
    for k in order:
        strip_line(k).wait_send()
        for u in range(2):
            piece_line(k, u).wait_send()
    for k in range(lines):
        for j in range(ways):
            if k or j:
                strip_core(k, j).wait_send()
            if j:
                strip_way(k, j).wait_send()
                for u in range(2):
                    piece_way(k, j, u).wait_send()


def run_forward(tokens, packed, mine, lines, ways, copies):
    images, padded, width = tokens.shape
    low = jnp.bfloat16
    everywhere = pl.BlockSpec(memory_space=pl.ANY)
    local = pl.BlockSpec(memory_space=pltpu.VMEM)
    half_width = packed.shape[2]
    dma = pltpu.SemaphoreType.DMA
    outs = pl.pallas_call(
        functools.partial(forward_kernel, lines, ways, copies),
        name="attention_forward",
        out_shape=[
            jax.ShapeDtypeStruct((images, padded, 3 * width), low),
            jax.ShapeDtypeStruct((images, padded, width), low),
            jax.ShapeDtypeStruct((images, padded, width), jnp.float32),
            jax.ShapeDtypeStruct((images, padded, width), low),
            jax.ShapeDtypeStruct((images, padded, 128), jnp.float32),
            jax.ShapeDtypeStruct((2, width, half_width), low),
        ]
        + [jax.ShapeDtypeStruct(mine.shape, low) for _ in range(lines * ways)],
        in_specs=[local, everywhere, everywhere],
        out_specs=[local] * 5 + [everywhere] * (1 + lines * ways),
        scratch_shapes=[
            pltpu.VMEM((2, width, half_width), low),
            pltpu.VMEM((128, width), jnp.float32),
            dma((2,)),
            dma((1,)),
            dma((2, lines)),
            dma((2, lines, ways)),
            dma((2, lines, ways)),
            dma((2, lines, 2)),
            dma((2, lines, ways, 2)),
        ],
        compiler_params=pltpu.CompilerParams(
            vmem_limit_bytes=60 * 2**20, collective_id=1, has_side_effects=True
        ),
        cost_estimate=pl.CostEstimate(
            flops=10 * images * padded * width * width,
            bytes_accessed=300 * 2**20,
            transcendentals=images * HEADS * padded * padded,
        ),
    )(tokens, packed, mine)
    pieces = outs[6:]
    return list(outs[:6]) + [[pieces[k * ways : (k + 1) * ways] for k in range(lines)]]


def backward_kernel(
    tokens_ref,
    out_grad_ref,
    residual_ref,
    normed_grad_ref,
    mixed_ref,
    projected_ref,
    tail_ref,
    full_ref,
    input_grad_ref,
    packed_ref,
    vectors,
    sums,
    projected_grad,
    mixer_in,
    normed_one,
    mixed_grad,
):
    low = jnp.bfloat16
    images, padded, width = tokens_ref.shape
    vectors[...] = full_ref[1, :, 1408:1536].astype(jnp.float32).T
    sums[...] = jnp.zeros_like(sums)
    head_scale = HEAD_DIM ** (-0.5)

    def add(row, values):
        sums[row : row + 1, :] += jnp.sum(values.astype(jnp.float32), axis=0, keepdims=True)

    @pl.loop(0, images)
    def _(i):
        span = pl.ds(pl.multiple_of(i * padded, padded), padded)
        _, unit, factor = layer_norm(residual_ref[i], 1.0, 0.0)
        upstream = normed_grad_ref[i]
        add(9, upstream * unit)
        add(10, upstream)
        residual_grad = out_grad_ref[i] + norm_back(upstream, unit, factor, vectors[9:10, :])
        input_grad_ref[i] = residual_grad
        rounded = residual_grad.astype(low)
        mixer_in[span, :] = rounded
        add(8, rounded)
        mixed_grad[...] = transposed(rounded, full_ref[1, :, 640:1408]).astype(low)
        for pair in range(HEADS // 2):
            start = 128 * pair
            query_pair = projected_ref[i, :, start : start + 128]
            key_pair = projected_ref[i, :, 768 + start : 896 + start]
            value_pair = projected_ref[i, :, 1536 + start : 1664 + start]
            grad_pair = mixed_grad[:, start : start + 128]
            found = []
            for which in (0, 1):
                probs = key_probs(query_pair, key_pair, which)
                back = transposed(head_of(grad_pair, which), value_pair)
                centre = jnp.sum(probs * back, axis=-1, keepdims=True)
                score_grad = (probs * (back - centre)).astype(low)
                found.append(
                    (
                        plain(score_grad, key_pair) * head_scale,
                        contract_first(score_grad, query_pair) * head_scale,
                        contract_first(probs.astype(low), grad_pair),
                    )
                )
            for part in range(3):
                columns = slice(768 * part + start, 768 * part + start + 128)
                projected_grad[span, columns] = side_by_side(
                    found[0][part], found[1][part]
                ).astype(low)
        whole = projected_grad[span, :]
        add(6, whole[:, 0:768])
        add(7, whole[:, 1536:2304])
        first_grad = transposed(whole[:, 0:1664], full_ref[0]) + transposed(
            whole[:, 1664:2304], full_ref[1, :, 0:640]
        )
        normed, unit, factor = layer_norm(tokens_ref[i], vectors[4:5, :], vectors[5:6, :])
        normed_one[span, :] = normed.astype(low)
        add(4, first_grad * unit)
        add(5, first_grad)
        input_grad_ref[i] += norm_back(first_grad, unit, factor, vectors[4:5, :])

    for start in range(0, width, 256):
        rows = slice(start, start + 256)
        left = normed_one[:, rows].T
        packed_ref[rows, 0:2304] = plain(left, projected_grad[...]).astype(low)
        left = mixed_ref[:, :, rows].reshape(images * padded, 256).T
        packed_ref[rows, 2304:3072] = plain(left, mixer_in[...]).astype(low)
    packed_ref[:, 3072:3200] = (tail_ref[...] + sums[...].T).astype(low)
    packed_ref[:, 3200:3328] = jnp.zeros((width, 128), low)


def run_backward(tokens, out_grad, residual, normed_grad, mixed, projected, tail, full):
    images, padded, width = tokens.shape
    low = jnp.bfloat16
    local = pl.BlockSpec(memory_space=pltpu.VMEM)
    rows = images * padded
    return pl.pallas_call(
        backward_kernel,
        name="attention_backward",
        out_shape=[
            jax.ShapeDtypeStruct((images, padded, width), jnp.float32),
            jax.ShapeDtypeStruct((width, 3328), low),
        ],
        in_specs=[local] * 8,
        out_specs=[local] * 2,
        scratch_shapes=[
            pltpu.VMEM((128, width), jnp.float32),
            pltpu.VMEM((128, width), jnp.float32),
            pltpu.VMEM((rows, 3 * width), low),
            pltpu.VMEM((rows, width), low),
            pltpu.VMEM((rows, width), low),
            pltpu.VMEM((padded, width), low),
        ],
        compiler_params=pltpu.CompilerParams(vmem_limit_bytes=60 * 2**20),
        cost_estimate=pl.CostEstimate(
            flops=60 * images * padded * width * width,
            bytes_accessed=40 * 2**20,
            transcendentals=images * HEADS * padded * padded,
        ),
    )(tokens, out_grad, residual, normed_grad, mixed, projected, tail, full)


def slot_table(routes, chosen, slots):
    token_count = routes.shape[0]
    hits = (routes[:, :, None] == chosen[None, None, :]).any(axis=1)
    rows = lax.broadcasted_iota(jnp.int32, (token_count, token_count), 0)
    columns = lax.broadcasted_iota(jnp.int32, (token_count, token_count), 1)
    earlier = jnp.dot(
        (columns < rows).astype(jnp.bfloat16),
        hits.astype(jnp.bfloat16),
        preferred_element_type=jnp.float32,
    ).astype(jnp.int32)
    slot_of = jnp.where(hits, earlier, -1).T
    return slot_of[:, None, :] == jnp.arange(slots, dtype=jnp.int32)[None, :, None]


def shard_shift(value, lines, ways, along, across):
    pairs = [
        (line * ways + way, (line + along) % lines * ways + (way + across) % ways)
        for line in range(lines)
        for way in range(ways)
    ]
    return lax.ppermute(value, "shard", pairs)


def group_shift(value, copies, along):
    pairs = [
        (copy, copy // GROUP * GROUP + (copy % GROUP + along) % GROUP) for copy in range(copies)
    ]
    return lax.ppermute(value, "rep", pairs)


def exchange(blocks, copies):
    return [blocks[0]] + [group_shift(blocks[k], copies, k) for k in range(1, GROUP)]


def exchange_back(blocks, copies):
    return [blocks[0]] + [group_shift(blocks[k], copies, -k) for k in range(1, GROUP)]


def sum_rows(rows):
    return lax.psum_scatter(rows, ("shard", "rep"), scatter_dimension=0, tiled=True)


def share_rows(rows):
    return lax.all_gather(rows, "rep", axis=0, tiled=True)


def shards(
    tokens_in,
    routes,
    first_gain,
    first_shift,
    joint_weight,
    joint_bias,
    mixer_weight,
    mixer_bias,
    second_gain,
    second_shift,
    router_weight,
    expert_up,
    upward_bias,
    expert_down,
    downward_bias,
    out_grad,
    *,
    groups,
    copies,
):
    row_count, width = tokens_in.shape
    experts, _, part = expert_up.shape
    strip = first_gain.shape[0]
    hidden_width = part * groups
    images = row_count // SEQ
    token_count = images * PADDED

    def widen(rows, fill=0):
        rows = rows.reshape(images, SEQ, rows.shape[1])
        return jnp.pad(rows, ((0, 0), (0, PADDED - SEQ), (0, 0)), constant_values=fill)

    def narrow(rows):
        return rows.reshape(images, PADDED, width)[:, :SEQ].reshape(row_count, width)

    token_images = widen(tokens_in)
    out_grad = widen(out_grad).reshape(token_count, width)
    routes = widen(routes, -1).reshape(token_count, 2)
    low = jnp.bfloat16
    bias_columns = experts * part // strip

    packed = jnp.concatenate(
        [
            joint_weight,
            mixer_weight,
            router_weight,
            first_gain[:, None],
            first_shift[:, None],
            joint_bias.T,
            mixer_bias[:, None],
            second_gain[:, None],
            second_shift[:, None],
            downward_bias.T,
            upward_bias.reshape(strip, bias_columns),
        ],
        axis=1,
    )
    used = packed.shape[1]
    packed_width = 2 * 1664
    packed = jnp.pad(packed, ((0, 0), (0, packed_width - used)))
    packed = packed.reshape(strip, 2, packed_width // 2).transpose(1, 0, 2)
    lines = 4 if groups % 4 == 0 else 1
    ways = groups // lines
    me = lax.axis_index("rep") % GROUP
    shard = lax.axis_index("shard")
    mine = jnp.stack(
        [
            lax.dynamic_index_in_dim(expert_up, me, 0, keepdims=False),
            lax.dynamic_index_in_dim(expert_down, me, 0, keepdims=False).T,
        ]
    )
    projected, mixed, residual_one, normed_two, logits, full, pieces = run_forward(
        token_images, packed, mine, lines, ways, copies
    )
    projected = projected.reshape(token_count, 3 * width)
    mixed = mixed.reshape(token_count, width)
    residual_one = residual_one.reshape(token_count, width)
    normed_two = normed_two.reshape(token_count, width)
    logits = logits.reshape(token_count, -1)[:, :experts]
    near_shards = jnp.stack(
        [
            (shard // ways + k) % lines * ways + (shard % ways + j) % ways
            for k in range(lines)
            for j in range(ways)
        ]
    )
    near_experts = (me + jnp.arange(GROUP, dtype=jnp.int32)) % GROUP

    tail = full[1, :, 1408:1536]
    router_full = tail[:, :experts]
    down_shift = tail[:, experts + 7 : 2 * experts + 7].astype(jnp.float32).T
    up_shift = (
        tail[:, 2 * experts + 7 : 2 * experts + 7 + bias_columns]
        .reshape(groups, experts, part)
        .astype(jnp.float32)
    )
    up_shift = lax.dynamic_index_in_dim(up_shift, me, 1, keepdims=False)[near_shards]
    up_shift = up_shift.reshape(lines, 1, ways * part)
    down_shift = lax.dynamic_index_in_dim(down_shift, me, 0, keepdims=True)
    router_probs = jax.nn.softmax(logits, axis=-1)

    probs_near = router_probs[:, near_experts]
    seated = slot_table(routes, near_experts, SLOTS)
    seats = seated.astype(low)
    flat_seats = seats.reshape(experts * SLOTS, token_count)
    gate_slots = jnp.sum(jnp.where(seated, probs_near.T[:, None, :], 0.0), axis=-1)
    dispatched = (
        jnp.dot(flat_seats, normed_two, preferred_element_type=jnp.float32)
        .astype(low)
        .reshape(experts, SLOTS, width)
    )
    grad_slots = (
        jnp.dot(flat_seats, out_grad.astype(low), preferred_element_type=jnp.float32)
        .astype(low)
        .reshape(experts, SLOTS, width)
    )
    grad_in = jnp.concatenate(exchange(grad_slots, copies), axis=0)
    rows_in = jnp.concatenate(exchange(dispatched, copies), axis=0)
    gate_in = jnp.concatenate(exchange(gate_slots, copies), axis=0)[:, None]
    if part % 128:
        joined = [[jnp.concatenate(line, axis=2)] for line in pieces]
    else:
        joined = pieces
    weighted, dispatched_grad, gate_grad, up_shift_grad, down_shift_grad, grads = run_expert(
        rows_in, grad_in, gate_in, up_shift, down_shift, joined
    )
    if part % 128:
        grads = [
            [line[0][:, :, j * part : (j + 1) * part] for j in range(ways)] for line in grads
        ]

    sums = []
    for k in range(lines):
        total = grads[k][0].astype(jnp.float32)
        for j in range(1, ways):
            total = total + shard_shift(grads[k][j], lines, ways, 0, j).astype(jnp.float32)
        sums.append(total)
    total = sums[0]
    for k in range(1, lines):
        total = total + shard_shift(sums[k].astype(low), lines, ways, k, 0).astype(jnp.float32)
    expert_grads = lax.all_gather(total.astype(low), "rep", axis=0)
    expert_grads = expert_grads.astype(jnp.float32).reshape(-1, GROUP, 2, width, part).sum(axis=0)
    up_grad = expert_grads[:, 0]
    down_grad = expert_grads[:, 1].transpose(0, 2, 1)

    blocks = (GROUP, SLOTS, width)
    dispatched_grad = jnp.concatenate(
        exchange_back(dispatched_grad.reshape(blocks), copies), axis=0
    )
    weighted = jnp.concatenate(exchange_back(weighted.reshape(blocks), copies), axis=0)
    gate_grad = jnp.stack(exchange_back(gate_grad.reshape(GROUP, SLOTS), copies))
    block_out = residual_one + contract_first(flat_seats, weighted)
    probs_grad = jnp.sum(jnp.where(seated, gate_grad[:, :, None], 0.0), axis=1).T
    probs_grad = probs_grad[:, (jnp.arange(GROUP, dtype=jnp.int32) - me) % GROUP]
    own = (jnp.arange(experts, dtype=jnp.int32) == me).astype(jnp.float32)[:, None]
    down_shift_grad = own * down_shift_grad
    up_shift_grad = jnp.zeros((groups, part), jnp.float32).at[near_shards].set(
        up_shift_grad.reshape(groups, part)
    )
    up_shift_grad = own * up_shift_grad.reshape(1, hidden_width)
    logit_grad = (
        router_probs * (probs_grad - jnp.sum(router_probs * probs_grad, axis=-1, keepdims=True))
    ).astype(low)
    router_grad = contract_first(normed_two, logit_grad)
    normed_grad = contract_last(logit_grad, router_full) + contract_first(
        flat_seats, dispatched_grad
    )
    tail_grad = jnp.concatenate(
        [
            router_grad,
            jnp.zeros((width, 7), jnp.float32),
            down_shift_grad.T,
            up_shift_grad.reshape(experts, groups, part)
            .transpose(1, 0, 2)
            .reshape(groups * strip, bias_columns),
        ],
        axis=1,
    )
    tail_grad = jnp.pad(tail_grad, ((0, 0), (0, 4 * width + 128 - used)))

    def by_image(rows):
        return rows.reshape(images, PADDED, rows.shape[1])

    input_grad, packed_grad = run_backward(
        token_images,
        by_image(out_grad),
        by_image(residual_one),
        by_image(normed_grad),
        by_image(mixed),
        by_image(projected),
        tail_grad,
        full,
    )
    packed_grad = packed_grad[:, : 4 * width + 128]
    packed_grad = share_rows(sum_rows(packed_grad)).astype(jnp.float32)
    end = packed_grad[:, 4 * width :]
    line = end[:, experts : experts + 7].T
    return (
        narrow(block_out),
        narrow(input_grad),
        line[0],
        line[1],
        packed_grad[:, : 3 * width],
        line[2:4],
        packed_grad[:, 3 * width : 4 * width],
        line[4],
        line[5],
        line[6],
        end[:, :experts],
        up_grad,
        end[:, 2 * experts + 7 : 2 * experts + 7 + bias_columns].reshape(experts, part),
        down_grad,
        end[:, experts + 7 : 2 * experts + 7].T,
    )


def solution(mesh):
    placed = (
        P(("shard", "rep"), None),
        P(("shard", "rep"), None),
        P("shard"),
        P("shard"),
        P("shard", None),
        P(None, "shard"),
        P("shard", None),
        P("shard"),
        P("shard"),
        P("shard"),
        P("shard", None),
        P(None, None, "shard"),
        P(None, "shard"),
        P(None, "shard", None),
        P(None, "shard"),
        P(("shard", "rep"), None),
    )
    return jax.shard_map(
        functools.partial(
            shards, groups=mesh.shape["shard"], copies=mesh.shape["rep"]
        ),
        mesh=mesh,
        in_specs=placed,
        out_specs=(
            P(("shard", "rep"), None),
            P(("shard", "rep"), None),
            P("shard"),
            P("shard"),
            P("shard", None),
            P(None, "shard"),
            P("shard", None),
            P("shard"),
            P("shard"),
            P("shard"),
            P("shard", None),
            P(None, None, "shard"),
            P(None, "shard"),
            P(None, "shard", None),
            P(None, "shard"),
        ),
        check_vma=False,
    )
```

```python
import functools

import jax
import jax.numpy as jnp
from jax import lax
from jax.experimental import pallas as pl
from jax.experimental.pallas import tpu as pltpu
from jax.sharding import PartitionSpec as P

HEADS = 12
HEAD_DIM = 64
SEQ = 197
SLOTS = 624
PADDED = 208
GROUP = 4


epsilon = 1e-06


def layer_norm(values, gain, shift):
    centre = jnp.mean(values, axis=-1, keepdims=True)
    centred = values - centre
    spread = jnp.mean(centred * centred, axis=-1, keepdims=True)
    factor = lax.rsqrt(spread + epsilon)
    unit_rows = centred * factor
    return (unit_rows * gain + shift, unit_rows, factor)


def norm_back(upstream, unit_rows, factor, gain):
    scaled = upstream * gain
    middle = jnp.mean(scaled, axis=-1, keepdims=True)
    along = jnp.mean(scaled * unit_rows, axis=-1, keepdims=True)
    return factor * (scaled - middle - unit_rows * along)


def contract_first(left_rows, right_rows):
    return lax.dot_general(
        left_rows, right_rows, (((0,), (0,)), ((), ())), preferred_element_type=jnp.float32
    )


def contract_last(left_rows, right_rows):
    return lax.dot_general(
        left_rows, right_rows, (((1,), (1,)), ((), ())), preferred_element_type=jnp.float32
    )


def transposed(left_rows, right_rows):
    return lax.dot_general(
        left_rows, right_rows, (((1,), (1,)), ((), ())), preferred_element_type=jnp.float32
    )


def plain(left_rows, right_rows):
    return jnp.dot(left_rows, right_rows, preferred_element_type=jnp.float32)


def normal_parts(hidden):
    bell = jnp.exp(-0.5 * hidden * hidden)
    near = 1.0 / (1.0 + (0.3275911 * 0.7071067811865476) * jnp.abs(hidden))
    tail = near * (
        0.127414796
        + near * (-0.142248368 + near * (0.7107068705 + near * (-0.7265760135 + near * 0.5307027145)))
    )
    tail = tail * bell
    return jnp.where(hidden < 0.0, tail, 1.0 - tail), bell * 0.3989422804014327


def expert_kernel(order, joined, ways, *refs):
    low = jnp.bfloat16
    x_ref, g_ref, gate_ref, up_shift_ref, down_shift_ref = refs[:5]
    refs = refs[5:]
    steps = len(order)
    pieces = [refs[k * joined : (k + 1) * joined] for k in range(steps)]
    refs = refs[steps * joined :]
    out_ref, dx_ref, gate_grad_ref, up_shift_grad_ref, down_shift_grad_ref = refs[:5]
    total_ref, own_ref, way_ref, line_ref = refs[5:9]
    refs = refs[9:]
    rg, xt, rgt, act, hg, y_sum, dx_sum, weights, grad_buf, stage = refs[:10]
    in_sem, own_sem, stage_sem, end_sem, way_sem, line_sem, back_sem = refs[10:]
    rows, width = x_ref.shape
    part = total_ref.shape[2]
    block = part * ways
    piece = block // joined
    chunk = SLOTS
    chunks = rows // chunk

    shard = lax.axis_index("shard")
    rep = lax.axis_index("rep")
    line, way = shard // ways, shard % ways
    lines = steps

    def place(k, j):
        index = lax.rem(line + k + lines, lines) * ways + lax.rem(way + j + ways, ways)
        return {"shard": index}

    def group(k):
        spot = rep % GROUP
        return {"rep": rep - spot + lax.rem(spot + k + GROUP, GROUP)}

    friends = [place(k, 0) for k in range(1, lines)] + [place(0, j) for j in range(1, ways)]
    friends += [group(k) for k in range(1, GROUP)]
    barrier = pltpu.get_barrier_semaphore()
    for friend in friends:
        pl.semaphore_signal(barrier, inc=1, device_id=friend, device_id_type=pl.DeviceIdType.MESH)

    def remote(source, target, sems, index, device):
        return pltpu.make_async_remote_copy(
            src_ref=source,
            dst_ref=target,
            send_sem=sems.at[(0,) + index],
            recv_sem=sems.at[(1,) + index],
            device_id=device,
            device_id_type=pl.DeviceIdType.MESH,
        )

    def load(step):
        return [
            pltpu.make_async_copy(
                pieces[order[step]][j],
                weights.at[step % 2, :, :, pl.ds(j * piece, piece)],
                in_sem.at[step % 2, j],
            )
            for j in range(joined)
        ]

    def keep(step):
        return pltpu.make_async_copy(grad_buf.at[0], own_ref.at[step], own_sem.at[0])

    def send_way(step, j):
        return remote(grad_buf.at[j], way_ref.at[step, j - 1], way_sem, (step, j), place(0, j))

    def send_line(step):
        k = order[step]
        return remote(own_ref.at[step], line_ref.at[k - 1], line_sem, (k,), place(k, 0))

    def fetch(source, slot):
        return pltpu.make_async_copy(source, stage.at[slot], stage_sem.at[slot])

    def add_ways(step):
        copies = [fetch(own_ref.at[step], 0)]
        for j in range(1, ways):
            send_way(step, j).wait_recv()
            copies.append(fetch(way_ref.at[step, j - 1], j))
        for copy in copies:
            copy.start()
        for copy in copies:
            copy.wait()

        @pl.loop(0, width // 256)
        def _(c):
            span = pl.ds(pl.multiple_of(c * 256, 256), 256)
            for u in range(2):
                total = stage[0, u, span, :].astype(jnp.float32)
                for j in range(1, ways):
                    total = total + stage[j, u, span, :].astype(jnp.float32)
                stage[0, u, span, :] = total.astype(low)

    def finish(step):
        add_ways(step)
        write = pltpu.make_async_copy(stage.at[0], own_ref.at[step], own_sem.at[1])
        write.start()
        write.wait()
        send_line(step).start()

    def send_back(k):
        block_rows = pl.ds(k * chunk, chunk)
        return remote(
            hg.at[block_rows, pl.ds(0, width)],
            dx_ref.at[block_rows, :],
            back_sem,
            (k,),
            group(-k),
        )

    for copy in load(0):
        copy.start()

    down_shift_grad_ref[...] = jnp.zeros_like(down_shift_grad_ref)

    @pl.loop(0, chunks)
    def _(c):
        span = pl.ds(pl.multiple_of(c * chunk, chunk), chunk)
        scaled = (g_ref[span, :].astype(jnp.float32) * gate_ref[span, :]).astype(low)
        rg[span, :] = scaled
        down_shift_grad_ref[...] += jnp.sum(scaled.astype(jnp.float32), axis=0, keepdims=True)
        y_sum[span, :] = jnp.zeros((chunk, width), jnp.float32)
        dx_sum[span, :] = jnp.zeros((chunk, width), jnp.float32)

    for start in range(0, width, 256):
        xt[start : start + 256, :] = x_ref[:, start : start + 256].T
        rgt[start : start + 256, :] = rg[:, start : start + 256].T

    for step in range(steps):
        for copy in load(step):
            copy.wait()
        if step + 1 < steps:
            for copy in load(step + 1):
                copy.start()
        slot = step % 2
        up_shift_grad_ref[step] = jnp.zeros((1, block), jnp.float32)

        @pl.loop(0, chunks)
        def _(c):
            span = pl.ds(pl.multiple_of(c * chunk, chunk), chunk)
            x_rows = x_ref[span, :]
            g_rows = rg[span, :]
            for start in range(0, block, 256):
                part_span = slice(start, start + 256)
                hidden = plain(x_rows, weights[slot, 0, :, part_span]) + up_shift_ref[step, :, part_span]
                back = plain(g_rows, weights[slot, 1, :, part_span])
                cdf, density = normal_parts(hidden)
                act[span, part_span] = (hidden * cdf).astype(low)
                hidden_grad = (back * (cdf + hidden * density)).astype(low)
                hg[span, part_span] = hidden_grad
                up_shift_grad_ref[step, :, part_span] += jnp.sum(
                    hidden_grad.astype(jnp.float32), axis=0, keepdims=True
                )
            y_sum[span, :] += transposed(act[span, :], weights[slot, 1])
            dx_sum[span, :] += transposed(hg[span, :], weights[slot, 0])

        if step == 0:
            pl.semaphore_wait(barrier, len(friends))
        else:
            keep(step - 1).wait()
            for j in range(1, ways):
                send_way(step - 1, j).wait_send()

        @pl.loop(0, width // 256)
        def _(c):
            span = pl.ds(pl.multiple_of(c * 256, 256), 256)
            for u, found in enumerate((plain(xt[span, :], hg[...]), plain(rgt[span, :], act[...]))):
                for j in range(ways):
                    grad_buf[j, u, span, :] = found[:, j * part : (j + 1) * part].astype(low)

        keep(step).start()
        for j in range(1, ways):
            send_way(step, j).start()
        if step > 0:
            finish(step - 1)

    @pl.loop(0, chunks)
    def _(c):
        span = pl.ds(pl.multiple_of(c * chunk, chunk), chunk)
        hg[span, :width] = dx_sum[span, :].astype(low)
        result = y_sum[span, :] + down_shift_ref[...]
        act[span, :width] = (result * gate_ref[span, :]).astype(low)
        gate_grad_ref[span, :] = jnp.sum(
            result * g_ref[span, :].astype(jnp.float32), axis=1, keepdims=True
        )

    home = pl.ds(0, chunk)
    ends = [
        pltpu.make_async_copy(hg.at[home, pl.ds(0, width)], dx_ref.at[home, :], end_sem.at[0]),
        pltpu.make_async_copy(act.at[:, pl.ds(0, width)], out_ref, end_sem.at[1]),
    ]
    for k in range(1, GROUP):
        send_back(k).start()
    for copy in ends:
        copy.start()

    last = steps - 1
    keep(last).wait()
    add_ways(last)
    for k in sorted(order[:-1], key=order.index):
        send_line(order.index(k)).wait_recv()
        copy = fetch(line_ref.at[k - 1], 1)
        copy.start()
        copy.wait()
        first, final = k == order[0], k == order[-2]

        @pl.loop(0, width // 256)
        def _(c):
            span = pl.ds(pl.multiple_of(c * 256, 256), 256)
            for u in range(2):
                sums = pl.ds(pl.multiple_of(u * width + c * 256, 256), 256)
                total = stage[1, u, span, :].astype(jnp.float32)
                if first:
                    total = total + stage[0, u, span, :].astype(jnp.float32)
                else:
                    total = total + y_sum[sums, 0:part]
                if final:
                    stage[0, u, span, :] = total.astype(low)
                else:
                    y_sum[sums, 0:part] = total

    write = pltpu.make_async_copy(stage.at[0], total_ref, own_sem.at[1])
    write.start()
    write.wait()
    for j in range(1, ways):
        send_way(last, j).wait_send()
    for step in range(last):
        send_line(step).wait_send()
    for k in range(1, GROUP):
        send_back(k).wait()
    for copy in ends:
        copy.wait()


def run_expert(rows_in, grad_in, gate_in, up_shift, down_shift, pieces, ways, part):
    steps, joined = len(pieces), len(pieces[0])
    order = [2, 1, 3, 0] if steps == 4 else list(range(1, steps)) + [0]
    rows, width = rows_in.shape
    block = part * ways
    low = jnp.bfloat16
    everywhere = pl.BlockSpec(memory_space=pl.ANY)
    local = pl.BlockSpec(memory_space=pltpu.VMEM)
    flat = [piece for line in pieces for piece in line]
    dma = pltpu.SemaphoreType.DMA
    up_shift = jnp.stack([up_shift[k] for k in order])
    outs = pl.pallas_call(
        functools.partial(expert_kernel, order, joined, ways),
        name="expert_block",
        out_shape=[
            jax.ShapeDtypeStruct((rows, width), low),
            jax.ShapeDtypeStruct((rows, width), low),
            jax.ShapeDtypeStruct((rows, 1), jnp.float32),
            jax.ShapeDtypeStruct((steps, 1, block), jnp.float32),
            jax.ShapeDtypeStruct((1, width), jnp.float32),
            jax.ShapeDtypeStruct((2, width, part), low),
            jax.ShapeDtypeStruct((steps, 2, width, part), low),
            jax.ShapeDtypeStruct((steps, ways - 1, 2, width, part), low),
            jax.ShapeDtypeStruct((steps - 1, 2, width, part), low),
        ],
        in_specs=[local] * 5 + [everywhere] * len(flat),
        out_specs=[everywhere, everywhere, local, local, local] + [everywhere] * 4,
        scratch_shapes=[
            pltpu.VMEM((rows, width), low),
            pltpu.VMEM((width, rows), low),
            pltpu.VMEM((width, rows), low),
            pltpu.VMEM((rows, block), low),
            pltpu.VMEM((rows, block), low),
            pltpu.VMEM((rows, width), jnp.float32),
            pltpu.VMEM((rows, width), jnp.float32),
            pltpu.VMEM((2, 2, width, block), low),
            pltpu.VMEM((ways, 2, width, part), low),
            pltpu.VMEM((ways, 2, width, part), low),
            dma((2, joined)),
            dma((2,)),
            dma((ways,)),
            dma((2,)),
            dma((2, steps, ways)),
            dma((2, steps)),
            dma((2, GROUP)),
        ],
        compiler_params=pltpu.CompilerParams(
            vmem_limit_bytes=63 * 2**20, collective_id=2, has_side_effects=True
        ),
        cost_estimate=pl.CostEstimate(
            flops=12 * rows * width * block * steps,
            bytes_accessed=12 * rows * width + 8 * width * block * steps,
            transcendentals=rows * block * steps,
        ),
    )(rows_in, grad_in, gate_in, up_shift, down_shift, *flat)
    weighted, dispatched_grad, gate_grad, up_shift_grad, down_shift_grad, total = outs[:6]
    up_shift_grad = jnp.stack([up_shift_grad[order.index(k)] for k in range(steps)])
    return weighted, dispatched_grad, gate_grad, up_shift_grad, down_shift_grad, total


def side_by_side(first, second):
    lane = lax.broadcasted_iota(jnp.int32, first.shape, 1)
    return jnp.where(lane < HEAD_DIM, first, second)


def head_of(pair, which):
    lane = lax.broadcasted_iota(jnp.int32, pair.shape, 1)
    keep = lane < HEAD_DIM if which == 0 else lane >= HEAD_DIM
    return jnp.where(keep, pair, jnp.zeros_like(pair))


def key_probs(query_pair, key_pair, which):
    scores = transposed(head_of(query_pair, which), key_pair) * HEAD_DIM ** (-0.5)
    column = lax.broadcasted_iota(jnp.int32, scores.shape, 1)
    scores = jnp.where(column < SEQ, scores, -1e30)
    raised = jnp.exp(scores - jnp.max(scores, axis=-1, keepdims=True))
    return raised * (1.0 / jnp.sum(raised, axis=-1, keepdims=True))


def forward_kernel(lines, ways, copies, *refs):
    low = jnp.bfloat16
    tokens_ref, packed_ref, mine_ref = refs[:3]
    refs = refs[3:]
    projected_ref, mixed_ref, residual_ref, normed_ref, logits_ref, weights_out = refs[:6]
    refs = refs[6:]
    pieces = [refs[k * ways : (k + 1) * ways] for k in range(lines)]
    refs = refs[lines * ways :]
    full, vectors = refs[:2]
    own_sem, save_sem = refs[2:4]
    line_sem, way_sem, core_sem, piece_line_sem, piece_way_sem = refs[4:]

    images, padded, width = tokens_ref.shape
    strip = packed_ref.shape[1]
    shard = lax.axis_index("shard")
    rep = lax.axis_index("rep")
    line, way = shard // ways, shard % ways
    half = rep % 2

    def place(k, j):
        return lax.rem(line + k + lines, lines) * ways + lax.rem(way + j + ways, ways)

    def at_shard(index):
        return {"shard": index}

    partner = {"rep": rep + 1 - 2 * half}
    friends = [at_shard(place(k, 0)) for k in range(1, lines)]
    friends += [at_shard(place(0, j)) for j in range(1, ways)] + [partner]
    barrier = pltpu.get_barrier_semaphore()
    for friend in friends:
        pl.semaphore_signal(barrier, inc=1, device_id=friend, device_id_type=pl.DeviceIdType.MESH)
    pl.semaphore_wait(barrier, len(friends))

    def remote(source, target, sems, index, device):
        return pltpu.make_async_remote_copy(
            src_ref=source,
            dst_ref=target,
            send_sem=sems.at[(0,) + index],
            recv_sem=sems.at[(1,) + index],
            device_id=device,
            device_id_type=pl.DeviceIdType.MESH,
        )

    def strip_of(k, j, side):
        rows = pl.ds(pl.multiple_of(place(k, j) * strip, strip), strip)
        return full.at[side, rows, :]

    def strip_line(k):
        return remote(packed_ref.at[half], strip_of(0, 0, half), line_sem, (k,), at_shard(place(-k, 0)))

    def strip_way(k, j):
        source = packed_ref.at[half] if k == 0 else strip_of(k, 0, half)
        return remote(source, strip_of(k, 0, half), way_sem, (k, j), at_shard(place(0, -j)))

    def strip_core(k, j):
        return remote(strip_of(k, j, half), strip_of(k, j, half), core_sem, (k, j), partner)

    def piece_line(k, u):
        return remote(
            mine_ref.at[u], pieces[k][0].at[u], piece_line_sem, (k, u), at_shard(place(-k, 0))
        )

    def piece_way(k, j, u):
        source = mine_ref.at[u] if k == 0 else pieces[k][0].at[u]
        return remote(source, pieces[k][j].at[u], piece_way_sem, (k, j, u), at_shard(place(0, -j)))

    own = pltpu.make_async_copy(
        packed_ref, full.at[:, pl.ds(pl.multiple_of(shard * strip, strip), strip), :], own_sem.at[0]
    )
    own_piece = pltpu.make_async_copy(mine_ref, pieces[0][0], own_sem.at[1])
    order = [k for k in (1, lines - 1, 2) if 0 < k < lines]
    order = list(dict.fromkeys(order))
    own.start()
    for k in order:
        strip_line(k).start()
    for j in range(1, ways):
        strip_way(0, j).start()
    own_piece.start()
    for j in range(1, ways):
        strip_way(0, j).wait_recv()
        strip_core(0, j).start()
    for k in order:
        strip_line(k).wait_recv()
        for j in range(1, ways):
            strip_way(k, j).start()
        strip_core(k, 0).start()
    for u in range(2):
        for k in order:
            piece_line(k, u).start()
        for j in range(1, ways):
            piece_way(0, j, u).start()
    for k in order:
        for j in range(1, ways):
            strip_way(k, j).wait_recv()
            strip_core(k, j).start()
    for k in range(lines):
        for j in range(ways):
            if k or j:
                strip_core(k, j).wait_recv()
    own.wait()
    save = pltpu.make_async_copy(full, weights_out, save_sem.at[0])
    save.start()

    vectors[...] = full[1, :, 1408:1536].astype(jnp.float32).T

    def pass_on(k, u):
        piece_line(k, u).wait_recv()
        for j in range(1, ways):
            piece_way(k, j, u).start()

    events = [(k, u) for u in range(2) for k in order]

    @pl.loop(0, images)
    def _(i):
        rows = tokens_ref[i]
        normed, _, _ = layer_norm(rows, vectors[4:5, :], vectors[5:6, :])
        normed = normed.astype(low)
        left = plain(normed, full[0])
        projected_ref[i, :, 0:768] = (left[:, 0:768] + vectors[6:7, :]).astype(low)
        projected_ref[i, :, 768:1536] = left[:, 768:1536].astype(low)
        right = plain(normed, full[1, :, 0:640])
        projected_ref[i, :, 1536:1664] = (left[:, 1536:1664] + vectors[7:8, 0:128]).astype(low)
        projected_ref[i, :, 1664:2304] = (right + vectors[7:8, 128:768]).astype(low)
        for pair in range(HEADS // 2):
            start = 128 * pair
            query_pair = projected_ref[i, :, start : start + 128]
            key_pair = projected_ref[i, :, 768 + start : 896 + start]
            value_pair = projected_ref[i, :, 1536 + start : 1664 + start]
            parts = [
                plain(key_probs(query_pair, key_pair, which).astype(low), value_pair)
                for which in (0, 1)
            ]
            mixed_ref[i, :, start : start + 128] = side_by_side(*parts).astype(low)
        residual = rows + (plain(mixed_ref[i], full[1, :, 640:1408]) + vectors[8:9, :])
        residual_ref[i] = residual
        normed_two, _, _ = layer_norm(residual, vectors[9:10, :], vectors[10:11, :])
        normed_two = normed_two.astype(low)
        normed_ref[i] = normed_two
        logits_ref[i] = plain(normed_two, full[1, :, 1408:1536])

        for number, event in enumerate(events[:2]):

            @pl.when(i == 2 * number + 1)
            def _():
                pass_on(*event)

    done = min(2, len(events)) if images >= 4 else 0
    for event in events[done:]:
        pass_on(*event)
    for u in range(2):
        for k in range(lines):
            for j in range(1, ways):
                piece_way(k, j, u).wait_recv()
    save.wait()
    own_piece.wait()
    for k in order:
        strip_line(k).wait_send()
        for u in range(2):
            piece_line(k, u).wait_send()
    for k in range(lines):
        for j in range(ways):
            if k or j:
                strip_core(k, j).wait_send()
            if j:
                strip_way(k, j).wait_send()
                for u in range(2):
                    piece_way(k, j, u).wait_send()


def run_forward(tokens, packed, mine, lines, ways, copies):
    images, padded, width = tokens.shape
    low = jnp.bfloat16
    everywhere = pl.BlockSpec(memory_space=pl.ANY)
    local = pl.BlockSpec(memory_space=pltpu.VMEM)
    half_width = packed.shape[2]
    dma = pltpu.SemaphoreType.DMA
    outs = pl.pallas_call(
        functools.partial(forward_kernel, lines, ways, copies),
        name="attention_forward",
        out_shape=[
            jax.ShapeDtypeStruct((images, padded, 3 * width), low),
            jax.ShapeDtypeStruct((images, padded, width), low),
            jax.ShapeDtypeStruct((images, padded, width), jnp.float32),
            jax.ShapeDtypeStruct((images, padded, width), low),
            jax.ShapeDtypeStruct((images, padded, 128), jnp.float32),
            jax.ShapeDtypeStruct((2, width, half_width), low),
        ]
        + [jax.ShapeDtypeStruct(mine.shape, low) for _ in range(lines * ways)],
        in_specs=[local, everywhere, everywhere],
        out_specs=[local] * 5 + [everywhere] * (1 + lines * ways),
        scratch_shapes=[
            pltpu.VMEM((2, width, half_width), low),
            pltpu.VMEM((128, width), jnp.float32),
            dma((2,)),
            dma((1,)),
            dma((2, lines)),
            dma((2, lines, ways)),
            dma((2, lines, ways)),
            dma((2, lines, 2)),
            dma((2, lines, ways, 2)),
        ],
        compiler_params=pltpu.CompilerParams(
            vmem_limit_bytes=60 * 2**20, collective_id=1, has_side_effects=True
        ),
        cost_estimate=pl.CostEstimate(
            flops=10 * images * padded * width * width,
            bytes_accessed=300 * 2**20,
            transcendentals=images * HEADS * padded * padded,
        ),
    )(tokens, packed, mine)
    pieces = outs[6:]
    return list(outs[:6]) + [[pieces[k * ways : (k + 1) * ways] for k in range(lines)]]


def backward_kernel(
    lines,
    ways,
    copies,
    tokens_ref,
    out_grad_ref,
    residual_ref,
    normed_grad_ref,
    mixed_ref,
    projected_ref,
    tail_ref,
    full_ref,
    input_grad_ref,
    reduced_ref,
    vectors,
    sums,
    projected_grad,
    mixer_in,
    normed_one,
    mixed_grad,
    packed,
    core_in,
    way_in,
    line_in,
    copy_in,
    done,
    core_sem,
    way_sem,
    line_sem,
    copy_sem,
):
    strip = reduced_ref.shape[1]
    shard = lax.axis_index("shard")
    rep = lax.axis_index("rep")
    line, way = shard // ways, shard % ways
    half = rep % 2
    pairs = copies // 2

    def place(k, j):
        return lax.rem(line + k + lines, lines) * ways + lax.rem(way + j + ways, ways)

    def at_shard(index):
        return {"shard": index}

    partner = {"rep": rep + 1 - 2 * half}

    def next_copy(m):
        return {"rep": lax.rem(rep + 2 * m, copies)}

    friends = [at_shard(place(k, 0)) for k in range(1, lines)]
    friends += [at_shard(place(0, j)) for j in range(1, ways)]
    friends += [partner] + [next_copy(m) for m in range(1, pairs)]
    barrier = pltpu.get_barrier_semaphore()
    for friend in friends:
        pl.semaphore_signal(barrier, inc=1, device_id=friend, device_id_type=pl.DeviceIdType.MESH)

    def remote(source, target, sems, index, device):
        return pltpu.make_async_remote_copy(
            src_ref=source,
            dst_ref=target,
            send_sem=sems.at[(0,) + index],
            recv_sem=sems.at[(1,) + index],
            device_id=device,
            device_id_type=pl.DeviceIdType.MESH,
        )

    def strip_rows(k, j):
        return pl.ds(pl.multiple_of(place(k, j) * strip, strip), strip)

    send_core = remote(packed.at[1 - half], core_in, core_sem, (0,), partner)

    def send_way(k, j):
        return remote(
            packed.at[half, strip_rows(k, j), :],
            way_in.at[k, j - 1],
            way_sem,
            (k, j),
            at_shard(place(0, j)),
        )

    def send_line(k):
        return remote(
            packed.at[half, strip_rows(k, 0), :],
            line_in.at[k - 1],
            line_sem,
            (k,),
            at_shard(place(k, 0)),
        )

    def send_copy(m):
        return remote(copy_in.at[rep // 2], copy_in.at[rep // 2], copy_sem, (m,), next_copy(m))

    send_done = remote(done.at[half], done.at[half], core_sem, (1,), partner)

    low = jnp.bfloat16
    images, padded, width = tokens_ref.shape
    vectors[...] = full_ref[1, :, 1408:1536].astype(jnp.float32).T
    sums[...] = jnp.zeros_like(sums)
    head_scale = HEAD_DIM ** (-0.5)

    def add(row, values):
        sums[row : row + 1, :] += jnp.sum(values.astype(jnp.float32), axis=0, keepdims=True)

    @pl.loop(0, images)
    def _(i):
        span = pl.ds(pl.multiple_of(i * padded, padded), padded)
        _, unit, factor = layer_norm(residual_ref[i], 1.0, 0.0)
        upstream = normed_grad_ref[i]
        add(9, upstream * unit)
        add(10, upstream)
        residual_grad = out_grad_ref[i] + norm_back(upstream, unit, factor, vectors[9:10, :])
        input_grad_ref[i] = residual_grad
        rounded = residual_grad.astype(low)
        mixer_in[span, :] = rounded
        add(8, rounded)
        mixed_grad[...] = transposed(rounded, full_ref[1, :, 640:1408]).astype(low)
        for pair in range(HEADS // 2):
            start = 128 * pair
            query_pair = projected_ref[i, :, start : start + 128]
            key_pair = projected_ref[i, :, 768 + start : 896 + start]
            value_pair = projected_ref[i, :, 1536 + start : 1664 + start]
            grad_pair = mixed_grad[:, start : start + 128]
            found = []
            for which in (0, 1):
                probs = key_probs(query_pair, key_pair, which)
                back = transposed(head_of(grad_pair, which), value_pair)
                centre = jnp.sum(probs * back, axis=-1, keepdims=True)
                score_grad = (probs * (back - centre)).astype(low)
                found.append(
                    (
                        plain(score_grad, key_pair) * head_scale,
                        contract_first(score_grad, query_pair) * head_scale,
                        contract_first(probs.astype(low), grad_pair),
                    )
                )
            for part in range(3):
                columns = slice(768 * part + start, 768 * part + start + 128)
                projected_grad[span, columns] = side_by_side(
                    found[0][part], found[1][part]
                ).astype(low)
        whole = projected_grad[span, :]
        add(6, whole[:, 0:768])
        add(7, whole[:, 1536:2304])
        first_grad = transposed(whole[:, 0:1664], full_ref[0]) + transposed(
            whole[:, 1664:2304], full_ref[1, :, 0:640]
        )
        normed, unit, factor = layer_norm(tokens_ref[i], vectors[4:5, :], vectors[5:6, :])
        normed_one[span, :] = normed.astype(low)
        add(4, first_grad * unit)
        add(5, first_grad)
        input_grad_ref[i] += norm_back(first_grad, unit, factor, vectors[4:5, :])

    for start in range(0, width, 256):
        rows = slice(start, start + 256)
        left = normed_one[:, rows].T
        packed[0, rows, :] = plain(left, projected_grad[:, 0:1664]).astype(low)
        packed[1, rows, 0:640] = plain(left, projected_grad[:, 1664:2304]).astype(low)
        left = mixed_ref[:, :, rows].reshape(images * padded, 256).T
        packed[1, rows, 640:1408] = plain(left, mixer_in[...]).astype(low)
    packed[1, :, 1408:1536] = (tail_ref[...] + sums[...].T).astype(low)
    packed[1, :, 1536:1664] = jnp.zeros((width, 128), low)

    pl.semaphore_wait(barrier, len(friends))
    order = [k for k in (2, 1, 3) if k < lines] + [0] if lines == 4 else [0]
    send_core.start()
    send_core.wait()
    for k in order:
        for j in range(1, ways):
            rows = strip_rows(k, j)
            packed[half, rows, :] = (
                packed[half, rows, :].astype(jnp.float32) + core_in[rows, :].astype(jnp.float32)
            ).astype(low)
            send_way(k, j).start()
    for k in order:
        rows = strip_rows(k, 0)
        total = packed[half, rows, :].astype(jnp.float32) + core_in[rows, :].astype(jnp.float32)
        for j in range(1, ways):
            send_way(k, j).wait_recv()
            total = total + way_in[k, j - 1].astype(jnp.float32)
        packed[half, rows, :] = total.astype(low)
        if k:
            send_line(k).start()
    total = packed[half, strip_rows(0, 0), :].astype(jnp.float32)
    for k in order[:-1]:
        send_line(k).wait_recv()
        total = total + line_in[k - 1].astype(jnp.float32)
    copy_in[rep // 2] = total.astype(low)
    for m in range(1, pairs):
        send_copy(m).start()
    for m in range(1, pairs):
        send_copy(m).wait()
    total = copy_in[0].astype(jnp.float32)
    for m in range(1, pairs):
        total = total + copy_in[m].astype(jnp.float32)
    done[half] = total.astype(low)
    send_done.start()
    send_done.wait()
    reduced_ref[...] = done[...]
    for k in order:
        for j in range(1, ways):
            send_way(k, j).wait_send()
        if k:
            send_line(k).wait_send()


def run_backward(lines, ways, copies, tokens, *rest):
    images, padded, width = tokens.shape
    low = jnp.bfloat16
    local = pl.BlockSpec(memory_space=pltpu.VMEM)
    rows = images * padded
    strip = width // (lines * ways)
    dma = pltpu.SemaphoreType.DMA
    return pl.pallas_call(
        functools.partial(backward_kernel, lines, ways, copies),
        name="attention_backward",
        out_shape=[
            jax.ShapeDtypeStruct((images, padded, width), jnp.float32),
            jax.ShapeDtypeStruct((2, strip, 1664), low),
        ],
        in_specs=[local] * 8,
        out_specs=[local] * 2,
        scratch_shapes=[
            pltpu.VMEM((128, width), jnp.float32),
            pltpu.VMEM((128, width), jnp.float32),
            pltpu.VMEM((rows, 3 * width), low),
            pltpu.VMEM((rows, width), low),
            pltpu.VMEM((rows, width), low),
            pltpu.VMEM((padded, width), low),
            pltpu.VMEM((2, width, 1664), low),
            pltpu.VMEM((width, 1664), low),
            pltpu.VMEM((lines, ways - 1, strip, 1664), low),
            pltpu.VMEM((lines - 1, strip, 1664), low),
            pltpu.VMEM((copies // 2, strip, 1664), low),
            pltpu.VMEM((2, strip, 1664), low),
            dma((2, 2)),
            dma((2, lines, ways)),
            dma((2, lines)),
            dma((2, copies // 2)),
        ],
        compiler_params=pltpu.CompilerParams(
            vmem_limit_bytes=62 * 2**20, collective_id=3, has_side_effects=True
        ),
        cost_estimate=pl.CostEstimate(
            flops=60 * images * padded * width * width,
            bytes_accessed=40 * 2**20,
            transcendentals=images * HEADS * padded * padded,
        ),
    )(tokens, *rest)


def dispatch_kernel(slot_ref, rows_ref, rows_out):
    low = jnp.bfloat16
    for k in range(GROUP):
        slot = lax.broadcasted_iota(jnp.int32, (SLOTS, slot_ref.shape[2]), 0)
        seats = (slot == slot_ref[k]).astype(low)
        rows_out[k] = plain(seats, rows_ref[...].astype(low)).astype(low)


def gated_dispatch_kernel(slot_ref, rows_ref, probs_ref, rows_out, gate_out):
    low = jnp.bfloat16
    for k in range(GROUP):
        slot = lax.broadcasted_iota(jnp.int32, (SLOTS, slot_ref.shape[2]), 0)
        seated = slot == slot_ref[k]
        rows_out[k] = plain(seated.astype(low), rows_ref[...]).astype(low)
        gate_out[k] = jnp.sum(jnp.where(seated, probs_ref[k], 0.0), axis=1, keepdims=True)


def run_dispatch(slot_of, rows, *probs):
    token_count, width = rows.shape
    local = pl.BlockSpec(memory_space=pltpu.VMEM)
    shapes = [
        jax.ShapeDtypeStruct((GROUP, SLOTS, width), jnp.bfloat16),
        jax.ShapeDtypeStruct((GROUP, SLOTS, 1), jnp.float32),
    ]
    return pl.pallas_call(
        gated_dispatch_kernel if probs else dispatch_kernel,
        name="dispatch_rows" if probs else "dispatch_gradient",
        out_shape=shapes if probs else shapes[:1],
        in_specs=[local] * (2 + len(probs)),
        out_specs=[local] * (1 + len(probs)),
        compiler_params=pltpu.CompilerParams(vmem_limit_bytes=48 * 2**20),
        cost_estimate=pl.CostEstimate(
            flops=2 * GROUP * SLOTS * token_count * width,
            bytes_accessed=8 * 2**20,
            transcendentals=0,
        ),
    )(slot_of, rows, *probs)


def seats_of(slot_ref, k):
    slot = lax.broadcasted_iota(jnp.int32, (slot_ref.shape[0], SLOTS), 1)
    return slot == slot_ref[:, k : k + 1]


def combine_kernel(slot_ref, grad_row_ref, grads_ref, normed_ref, probs_ref):
    normed = jnp.zeros(normed_ref.shape, jnp.float32)
    for k in range(GROUP):
        seated = seats_of(slot_ref, k)
        rows = slice(k * SLOTS, (k + 1) * SLOTS)
        normed = normed + plain(seated.astype(jnp.bfloat16), grads_ref[rows, :])
        probs_ref[:, k : k + 1] = jnp.sum(
            jnp.where(seated, grad_row_ref[k], 0.0), axis=1, keepdims=True
        )
    normed_ref[...] = normed


def result_kernel(slot_ref, residual_ref, *refs):
    blocks, out_ref = refs[:GROUP], refs[GROUP]
    total = residual_ref[...]
    for k in range(GROUP):
        total = total + plain(seats_of(slot_ref, k).astype(jnp.bfloat16), blocks[k][...])
    out_ref[...] = total


def run_combine(slot_of, grad_rows, grads):
    token_count, width = slot_of.shape[0], grads.shape[1]
    local = pl.BlockSpec(memory_space=pltpu.VMEM)
    return pl.pallas_call(
        combine_kernel,
        name="combine_gradient",
        out_shape=[
            jax.ShapeDtypeStruct((token_count, width), jnp.float32),
            jax.ShapeDtypeStruct((token_count, GROUP), jnp.float32),
        ],
        in_specs=[local] * 3,
        out_specs=[local] * 2,
        compiler_params=pltpu.CompilerParams(vmem_limit_bytes=56 * 2**20),
        cost_estimate=pl.CostEstimate(
            flops=2 * GROUP * SLOTS * token_count * width,
            bytes_accessed=10 * 2**20,
            transcendentals=0,
        ),
    )(slot_of, grad_rows, grads)


def run_result(slot_of, residual, blocks):
    token_count, width = residual.shape
    local = pl.BlockSpec(memory_space=pltpu.VMEM)
    return pl.pallas_call(
        result_kernel,
        name="combine_result",
        out_shape=jax.ShapeDtypeStruct((token_count, width), jnp.float32),
        in_specs=[local] * (2 + GROUP),
        out_specs=local,
        compiler_params=pltpu.CompilerParams(vmem_limit_bytes=56 * 2**20),
        cost_estimate=pl.CostEstimate(
            flops=2 * GROUP * SLOTS * token_count * width,
            bytes_accessed=10 * 2**20,
            transcendentals=0,
        ),
    )(slot_of, residual, *blocks)


def slot_table(routes, chosen):
    token_count = routes.shape[0]
    hits = (routes[:, :, None] == chosen[None, None, :]).any(axis=1)
    rows = lax.broadcasted_iota(jnp.int32, (token_count, token_count), 0)
    columns = lax.broadcasted_iota(jnp.int32, (token_count, token_count), 1)
    earlier = jnp.dot(
        (columns < rows).astype(jnp.bfloat16),
        hits.astype(jnp.bfloat16),
        preferred_element_type=jnp.float32,
    ).astype(jnp.int32)
    return jnp.where(hits, earlier, -1)


def group_shift(value, copies, along):
    pairs = [
        (copy, copy // GROUP * GROUP + (copy % GROUP + along) % GROUP) for copy in range(copies)
    ]
    return lax.ppermute(value, "rep", pairs)


def exchange(blocks, copies):
    return [blocks[0]] + [group_shift(blocks[k], copies, k) for k in range(1, GROUP)]


def exchange_back(blocks, copies):
    return [blocks[0]] + [group_shift(blocks[k], copies, -k) for k in range(1, GROUP)]


def shards(
    tokens_in,
    routes,
    first_gain,
    first_shift,
    joint_weight,
    joint_bias,
    mixer_weight,
    mixer_bias,
    second_gain,
    second_shift,
    router_weight,
    expert_up,
    upward_bias,
    expert_down,
    downward_bias,
    out_grad,
    *,
    groups,
    copies,
):
    row_count, width = tokens_in.shape
    experts, _, part = expert_up.shape
    strip = first_gain.shape[0]
    hidden_width = part * groups
    images = row_count // SEQ
    token_count = images * PADDED

    def widen(rows, fill=0):
        rows = rows.reshape(images, SEQ, rows.shape[1])
        return jnp.pad(rows, ((0, 0), (0, PADDED - SEQ), (0, 0)), constant_values=fill)

    def narrow(rows):
        return rows.reshape(images, PADDED, width)[:, :SEQ].reshape(row_count, width)

    token_images = widen(tokens_in)
    out_grad = widen(out_grad).reshape(token_count, width)
    routes = widen(routes, -1).reshape(token_count, 2)
    low = jnp.bfloat16
    bias_columns = experts * part // strip

    packed = jnp.concatenate(
        [
            joint_weight,
            mixer_weight,
            router_weight,
            first_gain[:, None],
            first_shift[:, None],
            joint_bias.T,
            mixer_bias[:, None],
            second_gain[:, None],
            second_shift[:, None],
            downward_bias.T,
            upward_bias.reshape(strip, bias_columns),
        ],
        axis=1,
    )
    used = packed.shape[1]
    packed_width = 2 * 1664
    packed = jnp.pad(packed, ((0, 0), (0, packed_width - used)))
    packed = packed.reshape(strip, 2, packed_width // 2).transpose(1, 0, 2)
    lines = 4 if groups % 4 == 0 else 1
    ways = groups // lines
    me = lax.axis_index("rep") % GROUP
    shard = lax.axis_index("shard")
    mine = jnp.stack(
        [
            lax.dynamic_index_in_dim(expert_up, me, 0, keepdims=False),
            lax.dynamic_index_in_dim(expert_down, me, 0, keepdims=False).T,
        ]
    )
    near_experts = (me + jnp.arange(GROUP, dtype=jnp.int32)) % GROUP
    slot_of = slot_table(routes, near_experts)
    slot_lines = slot_of.T[:, None, :]
    (grad_slots,) = run_dispatch(slot_lines, out_grad)
    token_images, grad_slots = lax.optimization_barrier((token_images, grad_slots))
    grad_in = jnp.concatenate(exchange(grad_slots, copies), axis=0)
    projected, mixed, residual_one, normed_two, logits, full, pieces = run_forward(
        token_images, packed, mine, lines, ways, copies
    )
    projected = projected.reshape(token_count, 3 * width)
    mixed = mixed.reshape(token_count, width)
    residual_one = residual_one.reshape(token_count, width)
    normed_two = normed_two.reshape(token_count, width)
    logits = logits.reshape(token_count, -1)[:, :experts]
    near_shards = jnp.stack(
        [
            (shard // ways + k) % lines * ways + (shard % ways + j) % ways
            for k in range(lines)
            for j in range(ways)
        ]
    )
    tail = full[1, :, 1408:1536]
    router_full = tail[:, :experts]
    down_shift = tail[:, experts + 7 : 2 * experts + 7].astype(jnp.float32).T
    up_shift = (
        tail[:, 2 * experts + 7 : 2 * experts + 7 + bias_columns]
        .reshape(groups, experts, part)
        .astype(jnp.float32)
    )
    up_shift = lax.dynamic_index_in_dim(up_shift, me, 1, keepdims=False)[near_shards]
    up_shift = up_shift.reshape(lines, 1, ways * part)
    down_shift = lax.dynamic_index_in_dim(down_shift, me, 0, keepdims=True)
    router_probs = jax.nn.softmax(logits, axis=-1)

    probs_near = router_probs[:, near_experts]
    dispatched, gate_slots = run_dispatch(slot_lines, normed_two, probs_near.T[:, None, :])
    gate_slots = gate_slots[:, :, 0]
    rows_in = jnp.concatenate(exchange(dispatched, copies), axis=0)
    gate_in = jnp.concatenate(exchange(gate_slots, copies), axis=0)[:, None]
    if part % 128:
        joined = [[jnp.concatenate(line, axis=2)] for line in pieces]
    else:
        joined = pieces
    weighted, dispatched_grad, gate_grad, up_shift_grad, down_shift_grad, total = run_expert(
        rows_in, grad_in, gate_in, up_shift, down_shift, joined, ways, part
    )
    expert_grads = lax.all_gather(total, "rep", axis=0)
    expert_grads = expert_grads.astype(jnp.float32).reshape(-1, GROUP, 2, width, part).sum(axis=0)
    up_grad = expert_grads[:, 0]
    down_grad = expert_grads[:, 1].transpose(0, 2, 1)

    gate_grad = jnp.stack(exchange_back(gate_grad.reshape(GROUP, SLOTS), copies))
    normed_grad, probs_grad = run_combine(slot_of, gate_grad[:, None, :], dispatched_grad)
    weighted = exchange_back(weighted.reshape(GROUP, SLOTS, width), copies)
    probs_grad = probs_grad[:, (jnp.arange(GROUP, dtype=jnp.int32) - me) % GROUP]
    own = (jnp.arange(experts, dtype=jnp.int32) == me).astype(jnp.float32)[:, None]
    down_shift_grad = own * down_shift_grad
    up_shift_grad = jnp.zeros((groups, part), jnp.float32).at[near_shards].set(
        up_shift_grad.reshape(groups, part)
    )
    up_shift_grad = own * up_shift_grad.reshape(1, hidden_width)
    logit_grad = (
        router_probs * (probs_grad - jnp.sum(router_probs * probs_grad, axis=-1, keepdims=True))
    ).astype(low)
    router_grad = contract_first(normed_two, logit_grad)
    normed_grad = normed_grad + contract_last(logit_grad, router_full)
    tail_grad = jnp.concatenate(
        [
            router_grad,
            jnp.zeros((width, 7), jnp.float32),
            down_shift_grad.T,
            up_shift_grad.reshape(experts, groups, part)
            .transpose(1, 0, 2)
            .reshape(groups * strip, bias_columns),
        ],
        axis=1,
    )
    tail_grad = jnp.pad(tail_grad, ((0, 0), (0, 4 * width + 128 - used)))

    def by_image(rows):
        return rows.reshape(images, PADDED, rows.shape[1])

    input_grad, reduced = run_backward(
        lines,
        ways,
        copies,
        token_images,
        by_image(out_grad),
        by_image(residual_one),
        by_image(normed_grad),
        by_image(mixed),
        by_image(projected),
        tail_grad,
        full,
    )
    late_residual, reduced = lax.optimization_barrier((residual_one, reduced))
    block_out = run_result(slot_of, late_residual, weighted)
    packed_grad = reduced.astype(jnp.float32).transpose(1, 0, 2).reshape(strip, packed_width)
    end = packed_grad[:, 4 * width :]
    line = end[:, experts : experts + 7].T
    return (
        narrow(block_out),
        narrow(input_grad),
        line[0],
        line[1],
        packed_grad[:, : 3 * width],
        line[2:4],
        packed_grad[:, 3 * width : 4 * width],
        line[4],
        line[5],
        line[6],
        end[:, :experts],
        up_grad,
        end[:, 2 * experts + 7 : 2 * experts + 7 + bias_columns].reshape(experts, part),
        down_grad,
        end[:, experts + 7 : 2 * experts + 7].T,
    )


def solution(mesh):
    placed = (
        P(("shard", "rep"), None),
        P(("shard", "rep"), None),
        P("shard"),
        P("shard"),
        P("shard", None),
        P(None, "shard"),
        P("shard", None),
        P("shard"),
        P("shard"),
        P("shard"),
        P("shard", None),
        P(None, None, "shard"),
        P(None, "shard"),
        P(None, "shard", None),
        P(None, "shard"),
        P(("shard", "rep"), None),
    )
    return jax.shard_map(
        functools.partial(
            shards, groups=mesh.shape["shard"], copies=mesh.shape["rep"]
        ),
        mesh=mesh,
        in_specs=placed,
        out_specs=(
            P(("shard", "rep"), None),
            P(("shard", "rep"), None),
            P("shard"),
            P("shard"),
            P("shard", None),
            P(None, "shard"),
            P("shard", None),
            P("shard"),
            P("shard"),
            P("shard"),
            P("shard", None),
            P(None, None, "shard"),
            P(None, "shard"),
            P(None, "shard", None),
            P(None, "shard"),
        ),
        check_vma=False,
    )
```

```python
import functools

import jax
import jax.numpy as jnp
from jax import lax
from jax.experimental import pallas as pl
from jax.experimental.pallas import tpu as pltpu
from jax.sharding import PartitionSpec as P

HEADS = 12
HEAD_DIM = 64
SEQ = 197
SLOTS = 624
PADDED = 208
GROUP = 4


epsilon = 1e-06


def layer_norm(values, gain, shift):
    centre = jnp.mean(values, axis=-1, keepdims=True)
    centred = values - centre
    spread = jnp.mean(centred * centred, axis=-1, keepdims=True)
    factor = lax.rsqrt(spread + epsilon)
    unit_rows = centred * factor
    return (unit_rows * gain + shift, unit_rows, factor)


def norm_back(upstream, unit_rows, factor, gain):
    scaled = upstream * gain
    middle = jnp.mean(scaled, axis=-1, keepdims=True)
    along = jnp.mean(scaled * unit_rows, axis=-1, keepdims=True)
    return factor * (scaled - middle - unit_rows * along)


def contract_first(left_rows, right_rows):
    return lax.dot_general(
        left_rows, right_rows, (((0,), (0,)), ((), ())), preferred_element_type=jnp.float32
    )


def contract_last(left_rows, right_rows):
    return lax.dot_general(
        left_rows, right_rows, (((1,), (1,)), ((), ())), preferred_element_type=jnp.float32
    )


def transposed(left_rows, right_rows):
    return lax.dot_general(
        left_rows, right_rows, (((1,), (1,)), ((), ())), preferred_element_type=jnp.float32
    )


def plain(left_rows, right_rows):
    return jnp.dot(left_rows, right_rows, preferred_element_type=jnp.float32)


def normal_parts(hidden):
    bell = jnp.exp(-0.5 * hidden * hidden)
    near = 1.0 / (1.0 + (0.3275911 * 0.7071067811865476) * jnp.abs(hidden))
    tail = near * (
        0.127414796
        + near * (-0.142248368 + near * (0.7107068705 + near * (-0.7265760135 + near * 0.5307027145)))
    )
    tail = tail * bell
    return jnp.where(hidden < 0.0, tail, 1.0 - tail), bell * 0.3989422804014327


def expert_kernel(order, joined, ways, *refs):
    low = jnp.bfloat16
    x_ref, g_ref, gate_ref, up_shift_ref, down_shift_ref = refs[:5]
    refs = refs[5:]
    steps = len(order)
    pieces = [refs[k * joined : (k + 1) * joined] for k in range(steps)]
    refs = refs[steps * joined :]
    out_ref, dx_ref, gate_grad_ref, up_shift_grad_ref, down_shift_grad_ref = refs[:5]
    up_ref, down_ref, own_ref, way_ref, line_ref = refs[5:10]
    refs = refs[10:]
    rg, xt, rgt, act, hg, y_sum, dx_sum, weights, grad_buf, stage = refs[:10]
    in_sem, own_sem, stage_sem, end_sem, way_sem, line_sem, back_sem = refs[10:]
    rows, width = x_ref.shape
    part = up_ref.shape[1]
    block = part * ways
    piece = block // joined
    chunk = SLOTS
    chunks = rows // chunk

    shard = lax.axis_index("shard")
    rep = lax.axis_index("rep")
    line, way = shard // ways, shard % ways
    lines = steps

    def place(k, j):
        index = lax.rem(line + k + lines, lines) * ways + lax.rem(way + j + ways, ways)
        return {"shard": index}

    def group(k):
        spot = rep % GROUP
        return {"rep": rep - spot + lax.rem(spot + k + GROUP, GROUP)}

    friends = [place(k, 0) for k in range(1, lines)] + [place(0, j) for j in range(1, ways)]
    friends += [group(k) for k in range(1, GROUP)]
    barrier = pltpu.get_barrier_semaphore()
    for friend in friends:
        pl.semaphore_signal(barrier, inc=1, device_id=friend, device_id_type=pl.DeviceIdType.MESH)

    def remote(source, target, sems, index, device):
        return pltpu.make_async_remote_copy(
            src_ref=source,
            dst_ref=target,
            send_sem=sems.at[(0,) + index],
            recv_sem=sems.at[(1,) + index],
            device_id=device,
            device_id_type=pl.DeviceIdType.MESH,
        )

    def load(step):
        return [
            pltpu.make_async_copy(
                pieces[order[step]][j],
                weights.at[step % 2, :, :, pl.ds(j * piece, piece)],
                in_sem.at[step % 2, j],
            )
            for j in range(joined)
        ]

    def keep(step):
        return pltpu.make_async_copy(grad_buf.at[0], own_ref.at[step], own_sem.at[0])

    def send_way(step, j):
        return remote(grad_buf.at[j], way_ref.at[step, j - 1], way_sem, (step, j), place(0, j))

    def send_line(step):
        k = order[step]
        return remote(own_ref.at[step], line_ref.at[k - 1], line_sem, (k,), place(k, 0))

    def fetch(source, slot):
        return pltpu.make_async_copy(source, stage.at[slot], stage_sem.at[slot])

    def add_ways(step):
        copies = [fetch(own_ref.at[step], 0)]
        for j in range(1, ways):
            send_way(step, j).wait_recv()
            copies.append(fetch(way_ref.at[step, j - 1], j))
        for copy in copies:
            copy.start()
        for copy in copies:
            copy.wait()

        @pl.loop(0, width // 256)
        def _(c):
            span = pl.ds(pl.multiple_of(c * 256, 256), 256)
            for u in range(2):
                total = stage[0, u, span, :].astype(jnp.float32)
                for j in range(1, ways):
                    total = total + stage[j, u, span, :].astype(jnp.float32)
                stage[0, u, span, :] = total.astype(low)

    def finish(step):
        add_ways(step)
        write = pltpu.make_async_copy(stage.at[0], own_ref.at[step], own_sem.at[1])
        write.start()
        write.wait()
        send_line(step).start()

    def send_back(k):
        block_rows = pl.ds(k * chunk, chunk)
        return remote(
            hg.at[block_rows, pl.ds(0, width)],
            dx_ref.at[block_rows, :],
            back_sem,
            (k,),
            group(-k),
        )

    for copy in load(0):
        copy.start()

    down_shift_grad_ref[...] = jnp.zeros_like(down_shift_grad_ref)

    @pl.loop(0, chunks)
    def _(c):
        span = pl.ds(pl.multiple_of(c * chunk, chunk), chunk)
        scaled = (g_ref[span, :].astype(jnp.float32) * gate_ref[span, :]).astype(low)
        rg[span, :] = scaled
        down_shift_grad_ref[...] += jnp.sum(scaled.astype(jnp.float32), axis=0, keepdims=True)
        y_sum[span, :] = jnp.zeros((chunk, width), jnp.float32)
        dx_sum[span, :] = jnp.zeros((chunk, width), jnp.float32)

    for start in range(0, width, 256):
        xt[start : start + 256, :] = x_ref[:, start : start + 256].T
        rgt[start : start + 256, :] = rg[:, start : start + 256].T

    for step in range(steps):
        for copy in load(step):
            copy.wait()
        if step + 1 < steps:
            for copy in load(step + 1):
                copy.start()
        slot = step % 2
        up_shift_grad_ref[step] = jnp.zeros((1, block), jnp.float32)

        @pl.loop(0, chunks)
        def _(c):
            span = pl.ds(pl.multiple_of(c * chunk, chunk), chunk)
            x_rows = x_ref[span, :]
            g_rows = rg[span, :]
            for start in range(0, block, 256):
                part_span = slice(start, start + 256)
                hidden = plain(x_rows, weights[slot, 0, :, part_span]) + up_shift_ref[step, :, part_span]
                back = plain(g_rows, weights[slot, 1, :, part_span])
                cdf, density = normal_parts(hidden)
                act[span, part_span] = (hidden * cdf).astype(low)
                hidden_grad = (back * (cdf + hidden * density)).astype(low)
                hg[span, part_span] = hidden_grad
                up_shift_grad_ref[step, :, part_span] += jnp.sum(
                    hidden_grad.astype(jnp.float32), axis=0, keepdims=True
                )
            y_sum[span, :] += transposed(act[span, :], weights[slot, 1])
            dx_sum[span, :] += transposed(hg[span, :], weights[slot, 0])

        if step == 0:
            pl.semaphore_wait(barrier, len(friends))
        else:
            keep(step - 1).wait()
            for j in range(1, ways):
                send_way(step - 1, j).wait_send()

        @pl.loop(0, width // 256)
        def _(c):
            span = pl.ds(pl.multiple_of(c * 256, 256), 256)
            for u, found in enumerate((plain(xt[span, :], hg[...]), plain(rgt[span, :], act[...]))):
                for j in range(ways):
                    grad_buf[j, u, span, :] = found[:, j * part : (j + 1) * part].astype(low)

        keep(step).start()
        for j in range(1, ways):
            send_way(step, j).start()
        if step > 0:
            finish(step - 1)

    @pl.loop(0, chunks)
    def _(c):
        span = pl.ds(pl.multiple_of(c * chunk, chunk), chunk)
        hg[span, :width] = dx_sum[span, :].astype(low)
        result = y_sum[span, :] + down_shift_ref[...]
        act[span, :width] = (result * gate_ref[span, :]).astype(low)
        gate_grad_ref[span, :] = jnp.sum(
            result * g_ref[span, :].astype(jnp.float32), axis=1, keepdims=True
        )

    home = pl.ds(0, chunk)
    ends = [
        pltpu.make_async_copy(hg.at[home, pl.ds(0, width)], dx_ref.at[home, :], end_sem.at[0]),
        pltpu.make_async_copy(act.at[:, pl.ds(0, width)], out_ref, end_sem.at[1]),
    ]
    for k in range(1, GROUP):
        send_back(k).start()
    for copy in ends:
        copy.start()

    last = steps - 1
    keep(last).wait()
    add_ways(last)
    for k in sorted(order[:-1], key=order.index):
        send_line(order.index(k)).wait_recv()
        copy = fetch(line_ref.at[k - 1], 1)
        copy.start()
        copy.wait()
        first, final = k == order[0], k == order[-2]

        @pl.loop(0, width // 256)
        def _(c):
            span = pl.ds(pl.multiple_of(c * 256, 256), 256)
            for u in range(2):
                sums = pl.ds(pl.multiple_of(u * width + c * 256, 256), 256)
                total = stage[1, u, span, :].astype(jnp.float32)
                if first:
                    total = total + stage[0, u, span, :].astype(jnp.float32)
                else:
                    total = total + y_sum[sums, 0:part]
                if final:
                    stage[0, u, span, :] = total.astype(low)
                else:
                    y_sum[sums, 0:part] = total

    up_ref[...] = stage[0, 0]
    down_ref[...] = stage[0, 1].astype(jnp.float32).T.astype(low)
    for j in range(1, ways):
        send_way(last, j).wait_send()
    for step in range(last):
        send_line(step).wait_send()
    for k in range(1, GROUP):
        send_back(k).wait()
    for copy in ends:
        copy.wait()


def run_expert(rows_in, grad_in, gate_in, up_shift, down_shift, pieces, ways, part):
    steps, joined = len(pieces), len(pieces[0])
    order = [2, 1, 3, 0] if steps == 4 else list(range(1, steps)) + [0]
    rows, width = rows_in.shape
    block = part * ways
    low = jnp.bfloat16
    everywhere = pl.BlockSpec(memory_space=pl.ANY)
    local = pl.BlockSpec(memory_space=pltpu.VMEM)
    flat = [piece for line in pieces for piece in line]
    dma = pltpu.SemaphoreType.DMA
    up_shift = jnp.stack([up_shift[k] for k in order])
    outs = pl.pallas_call(
        functools.partial(expert_kernel, order, joined, ways),
        name="expert_block",
        out_shape=[
            jax.ShapeDtypeStruct((rows, width), low),
            jax.ShapeDtypeStruct((rows, width), low),
            jax.ShapeDtypeStruct((rows, 1), jnp.float32),
            jax.ShapeDtypeStruct((steps, 1, block), jnp.float32),
            jax.ShapeDtypeStruct((1, width), jnp.float32),
            jax.ShapeDtypeStruct((width, part), low),
            jax.ShapeDtypeStruct((part, width), low),
            jax.ShapeDtypeStruct((steps, 2, width, part), low),
            jax.ShapeDtypeStruct((steps, ways - 1, 2, width, part), low),
            jax.ShapeDtypeStruct((steps - 1, 2, width, part), low),
        ],
        in_specs=[local] * 5 + [everywhere] * len(flat),
        out_specs=[everywhere, everywhere] + [local] * 5 + [everywhere] * 3,
        scratch_shapes=[
            pltpu.VMEM((rows, width), low),
            pltpu.VMEM((width, rows), low),
            pltpu.VMEM((width, rows), low),
            pltpu.VMEM((rows, block), low),
            pltpu.VMEM((rows, block), low),
            pltpu.VMEM((rows, width), jnp.float32),
            pltpu.VMEM((rows, width), jnp.float32),
            pltpu.VMEM((2, 2, width, block), low),
            pltpu.VMEM((ways, 2, width, part), low),
            pltpu.VMEM((ways, 2, width, part), low),
            dma((2, joined)),
            dma((2,)),
            dma((ways,)),
            dma((2,)),
            dma((2, steps, ways)),
            dma((2, steps)),
            dma((2, GROUP)),
        ],
        compiler_params=pltpu.CompilerParams(
            vmem_limit_bytes=63 * 2**20, collective_id=2, has_side_effects=True
        ),
        cost_estimate=pl.CostEstimate(
            flops=12 * rows * width * block * steps,
            bytes_accessed=12 * rows * width + 8 * width * block * steps,
            transcendentals=rows * block * steps,
        ),
    )(rows_in, grad_in, gate_in, up_shift, down_shift, *flat)
    weighted, dispatched_grad, gate_grad, up_shift_grad, down_shift_grad, up, down = outs[:7]
    up_shift_grad = jnp.stack([up_shift_grad[order.index(k)] for k in range(steps)])
    return weighted, dispatched_grad, gate_grad, up_shift_grad, down_shift_grad, up, down


def side_by_side(first, second):
    lane = lax.broadcasted_iota(jnp.int32, first.shape, 1)
    return jnp.where(lane < HEAD_DIM, first, second)


def head_of(pair, which):
    lane = lax.broadcasted_iota(jnp.int32, pair.shape, 1)
    keep = lane < HEAD_DIM if which == 0 else lane >= HEAD_DIM
    return jnp.where(keep, pair, jnp.zeros_like(pair))


def key_probs(query_pair, key_pair, which):
    scores = transposed(head_of(query_pair, which), key_pair) * HEAD_DIM ** (-0.5)
    column = lax.broadcasted_iota(jnp.int32, scores.shape, 1)
    scores = jnp.where(column < SEQ, scores, -1e30)
    raised = jnp.exp(scores - jnp.max(scores, axis=-1, keepdims=True))
    return raised * (1.0 / jnp.sum(raised, axis=-1, keepdims=True))


def forward_kernel(lines, ways, copies, *refs):
    low = jnp.bfloat16
    tokens_ref, slot_ref, packed_ref, mine_ref, grad_slots_ref = refs[:5]
    refs = refs[5:]
    projected_ref, mixed_ref, residual_ref, normed_ref, logits_ref, weights_out = refs[:6]
    rows_in_ref, grad_in_ref = refs[6:8]
    refs = refs[8:]
    pieces = [refs[k * ways : (k + 1) * ways] for k in range(lines)]
    refs = refs[lines * ways :]
    full, vectors, rows_out = refs[:3]
    own_sem, save_sem = refs[3:5]
    line_sem, way_sem, core_sem, piece_line_sem, piece_way_sem, token_sem = refs[5:]

    images, padded, width = tokens_ref.shape
    strip = packed_ref.shape[1]
    shard = lax.axis_index("shard")
    rep = lax.axis_index("rep")
    line, way = shard // ways, shard % ways
    half = rep % 2

    def place(k, j):
        return lax.rem(line + k + lines, lines) * ways + lax.rem(way + j + ways, ways)

    def at_shard(index):
        return {"shard": index}

    def group(k):
        spot = rep % GROUP
        return {"rep": rep - spot + lax.rem(spot + k, GROUP)}

    partner = {"rep": rep + 1 - 2 * half}
    friends = [at_shard(place(k, 0)) for k in range(1, lines)]
    friends += [at_shard(place(0, j)) for j in range(1, ways)]
    friends += [group(k) for k in range(1, GROUP)]
    barrier = pltpu.get_barrier_semaphore()
    for friend in friends:
        pl.semaphore_signal(barrier, inc=1, device_id=friend, device_id_type=pl.DeviceIdType.MESH)
    pl.semaphore_wait(barrier, len(friends))

    def remote(source, target, sems, index, device):
        return pltpu.make_async_remote_copy(
            src_ref=source,
            dst_ref=target,
            send_sem=sems.at[(0,) + index],
            recv_sem=sems.at[(1,) + index],
            device_id=device,
            device_id_type=pl.DeviceIdType.MESH,
        )

    def strip_of(k, j, side):
        rows = pl.ds(pl.multiple_of(place(k, j) * strip, strip), strip)
        return full.at[side, rows, :]

    def strip_line(k):
        return remote(packed_ref.at[half], strip_of(0, 0, half), line_sem, (k,), at_shard(place(-k, 0)))

    def strip_way(k, j):
        source = packed_ref.at[half] if k == 0 else strip_of(k, 0, half)
        return remote(source, strip_of(k, 0, half), way_sem, (k, j), at_shard(place(0, -j)))

    def strip_core(k, j):
        return remote(strip_of(k, j, half), strip_of(k, j, half), core_sem, (k, j), partner)

    def piece_line(k, u):
        return remote(
            mine_ref.at[u], pieces[k][0].at[u], piece_line_sem, (k, u), at_shard(place(-k, 0))
        )

    def piece_way(k, j, u):
        source = mine_ref.at[u] if k == 0 else pieces[k][0].at[u]
        return remote(source, pieces[k][j].at[u], piece_way_sem, (k, j, u), at_shard(place(0, -j)))

    def block_of(ref, k):
        return ref.at[pl.ds(k * SLOTS, SLOTS), :]

    def send_grad(k):
        return remote(grad_slots_ref.at[k], block_of(grad_in_ref, k), token_sem, (0, k), group(k))

    def send_rows(k):
        return remote(rows_out.at[k], block_of(rows_in_ref, k), token_sem, (1, k), group(k))

    own_grad = pltpu.make_async_copy(grad_slots_ref.at[0], block_of(grad_in_ref, 0), own_sem.at[2])
    own_rows = pltpu.make_async_copy(rows_out.at[0], block_of(rows_in_ref, 0), own_sem.at[3])
    own = pltpu.make_async_copy(
        packed_ref, full.at[:, pl.ds(pl.multiple_of(shard * strip, strip), strip), :], own_sem.at[0]
    )
    own_piece = pltpu.make_async_copy(mine_ref, pieces[0][0], own_sem.at[1])
    order = [k for k in (1, lines - 1, 2) if 0 < k < lines]
    order = list(dict.fromkeys(order))
    own.start()
    for k in order:
        strip_line(k).start()
    for j in range(1, ways):
        strip_way(0, j).start()
    own_piece.start()
    for j in range(1, ways):
        strip_way(0, j).wait_recv()
        strip_core(0, j).start()
    for k in order:
        strip_line(k).wait_recv()
        for j in range(1, ways):
            strip_way(k, j).start()
        strip_core(k, 0).start()
    for u in range(2):
        for k in order:
            piece_line(k, u).start()
        for j in range(1, ways):
            piece_way(0, j, u).start()
    for k in order:
        for j in range(1, ways):
            strip_way(k, j).wait_recv()
            strip_core(k, j).start()
    own_grad.start()
    for k in (2, 1, 3):
        send_grad(k).start()
    for k in range(lines):
        for j in range(ways):
            if k or j:
                strip_core(k, j).wait_recv()
    own.wait()
    save = pltpu.make_async_copy(full, weights_out, save_sem.at[0])
    save.start()

    vectors[...] = full[1, :, 1408:1536].astype(jnp.float32).T

    def pass_on(k, u):
        piece_line(k, u).wait_recv()
        for j in range(1, ways):
            piece_way(k, j, u).start()

    events = [(k, u) for u in range(2) for k in order]

    @pl.loop(0, images)
    def _(i):
        rows = tokens_ref[i]
        normed, _, _ = layer_norm(rows, vectors[4:5, :], vectors[5:6, :])
        normed = normed.astype(low)
        left = plain(normed, full[0])
        projected_ref[i, :, 0:768] = (left[:, 0:768] + vectors[6:7, :]).astype(low)
        projected_ref[i, :, 768:1536] = left[:, 768:1536].astype(low)
        right = plain(normed, full[1, :, 0:640])
        projected_ref[i, :, 1536:1664] = (left[:, 1536:1664] + vectors[7:8, 0:128]).astype(low)
        projected_ref[i, :, 1664:2304] = (right + vectors[7:8, 128:768]).astype(low)
        for pair in range(HEADS // 2):
            start = 128 * pair
            query_pair = projected_ref[i, :, start : start + 128]
            key_pair = projected_ref[i, :, 768 + start : 896 + start]
            value_pair = projected_ref[i, :, 1536 + start : 1664 + start]
            parts = [
                plain(key_probs(query_pair, key_pair, which).astype(low), value_pair)
                for which in (0, 1)
            ]
            mixed_ref[i, :, start : start + 128] = side_by_side(*parts).astype(low)
        residual = rows + (plain(mixed_ref[i], full[1, :, 640:1408]) + vectors[8:9, :])
        residual_ref[i] = residual
        normed_two, _, _ = layer_norm(residual, vectors[9:10, :], vectors[10:11, :])
        normed_two = normed_two.astype(low)
        normed_ref[i] = normed_two
        logits_ref[i] = plain(normed_two, full[1, :, 1408:1536])

        for number, event in enumerate(events[:2]):

            @pl.when(i == 2 * number + 1)
            def _():
                pass_on(*event)

    done = min(2, len(events)) if images >= 4 else 0
    for event in events[done : done + 1]:
        pass_on(*event)
    token_count = images * padded
    for k in (2, 1, 3, 0):
        slot = lax.broadcasted_iota(jnp.int32, (SLOTS, token_count), 0)
        seats = (slot == slot_ref[k]).astype(low)
        rows_out[k] = plain(seats, normed_ref[...].reshape(token_count, width)).astype(low)
        if k:
            send_rows(k).start()
    own_rows.start()
    for event in events[done + 1 :]:
        pass_on(*event)
    for u in range(2):
        for k in range(lines):
            for j in range(1, ways):
                piece_way(k, j, u).wait_recv()
    for k in range(1, GROUP):
        send_grad(k).wait()
        send_rows(k).wait()
    own_grad.wait()
    own_rows.wait()
    save.wait()
    own_piece.wait()
    for k in order:
        strip_line(k).wait_send()
        for u in range(2):
            piece_line(k, u).wait_send()
    for k in range(lines):
        for j in range(ways):
            if k or j:
                strip_core(k, j).wait_send()
            if j:
                strip_way(k, j).wait_send()
                for u in range(2):
                    piece_way(k, j, u).wait_send()


def run_forward(tokens, slot_lines, packed, mine, grad_slots, lines, ways, copies):
    images, padded, width = tokens.shape
    low = jnp.bfloat16
    everywhere = pl.BlockSpec(memory_space=pl.ANY)
    local = pl.BlockSpec(memory_space=pltpu.VMEM)
    half_width = packed.shape[2]
    dma = pltpu.SemaphoreType.DMA
    outs = pl.pallas_call(
        functools.partial(forward_kernel, lines, ways, copies),
        name="attention_forward",
        out_shape=[
            jax.ShapeDtypeStruct((images, padded, 3 * width), low),
            jax.ShapeDtypeStruct((images, padded, width), low),
            jax.ShapeDtypeStruct((images, padded, width), jnp.float32),
            jax.ShapeDtypeStruct((images, padded, width), low),
            jax.ShapeDtypeStruct((images, padded, 128), jnp.float32),
            jax.ShapeDtypeStruct((2, width, half_width), low),
            jax.ShapeDtypeStruct((GROUP * SLOTS, width), low),
            jax.ShapeDtypeStruct((GROUP * SLOTS, width), low),
        ]
        + [jax.ShapeDtypeStruct(mine.shape, low) for _ in range(lines * ways)],
        in_specs=[local, local, everywhere, everywhere, everywhere],
        out_specs=[local] * 5 + [everywhere] * (3 + lines * ways),
        scratch_shapes=[
            pltpu.VMEM((2, width, half_width), low),
            pltpu.VMEM((128, width), jnp.float32),
            pltpu.VMEM((GROUP, SLOTS, width), low),
            dma((4,)),
            dma((1,)),
            dma((2, lines)),
            dma((2, lines, ways)),
            dma((2, lines, ways)),
            dma((2, lines, 2)),
            dma((2, lines, ways, 2)),
            dma((2, 2, GROUP)),
        ],
        compiler_params=pltpu.CompilerParams(
            vmem_limit_bytes=60 * 2**20, collective_id=1, has_side_effects=True
        ),
        cost_estimate=pl.CostEstimate(
            flops=10 * images * padded * width * width,
            bytes_accessed=300 * 2**20,
            transcendentals=images * HEADS * padded * padded,
        ),
    )(tokens, slot_lines, packed, mine, grad_slots)
    pieces = outs[8:]
    return list(outs[:8]) + [[pieces[k * ways : (k + 1) * ways] for k in range(lines)]]


def backward_kernel(
    lines,
    ways,
    copies,
    tokens_ref,
    out_grad_ref,
    residual_ref,
    normed_grad_ref,
    mixed_ref,
    projected_ref,
    tail_ref,
    full_ref,
    input_grad_ref,
    reduced_ref,
    vectors,
    sums,
    projected_grad,
    mixer_in,
    normed_one,
    mixed_grad,
    packed,
    core_in,
    way_in,
    line_in,
    copy_in,
    done,
    core_sem,
    way_sem,
    line_sem,
    copy_sem,
):
    strip = reduced_ref.shape[1]
    shard = lax.axis_index("shard")
    rep = lax.axis_index("rep")
    line, way = shard // ways, shard % ways
    half = rep % 2
    pairs = copies // 2

    def place(k, j):
        return lax.rem(line + k + lines, lines) * ways + lax.rem(way + j + ways, ways)

    def at_shard(index):
        return {"shard": index}

    partner = {"rep": rep + 1 - 2 * half}

    def next_copy(m):
        return {"rep": lax.rem(rep + 2 * m, copies)}

    friends = [at_shard(place(k, 0)) for k in range(1, lines)]
    friends += [at_shard(place(0, j)) for j in range(1, ways)]
    friends += [partner] + [next_copy(m) for m in range(1, pairs)]
    barrier = pltpu.get_barrier_semaphore()
    for friend in friends:
        pl.semaphore_signal(barrier, inc=1, device_id=friend, device_id_type=pl.DeviceIdType.MESH)

    def remote(source, target, sems, index, device):
        return pltpu.make_async_remote_copy(
            src_ref=source,
            dst_ref=target,
            send_sem=sems.at[(0,) + index],
            recv_sem=sems.at[(1,) + index],
            device_id=device,
            device_id_type=pl.DeviceIdType.MESH,
        )

    def strip_rows(k, j):
        return pl.ds(pl.multiple_of(place(k, j) * strip, strip), strip)

    send_core = remote(packed.at[1 - half], core_in, core_sem, (0,), partner)

    def send_way(k, j):
        return remote(
            packed.at[half, strip_rows(k, j), :],
            way_in.at[k, j - 1],
            way_sem,
            (k, j),
            at_shard(place(0, j)),
        )

    def send_line(k):
        return remote(
            packed.at[half, strip_rows(k, 0), :],
            line_in.at[k - 1],
            line_sem,
            (k,),
            at_shard(place(k, 0)),
        )

    def send_copy(m):
        return remote(copy_in.at[rep // 2], copy_in.at[rep // 2], copy_sem, (m,), next_copy(m))

    send_done = remote(done.at[half], done.at[half], core_sem, (1,), partner)

    low = jnp.bfloat16
    images, padded, width = tokens_ref.shape
    vectors[...] = full_ref[1, :, 1408:1536].astype(jnp.float32).T
    sums[...] = jnp.zeros_like(sums)
    head_scale = HEAD_DIM ** (-0.5)

    def add(row, values):
        sums[row : row + 1, :] += jnp.sum(values.astype(jnp.float32), axis=0, keepdims=True)

    @pl.loop(0, images)
    def _(i):
        span = pl.ds(pl.multiple_of(i * padded, padded), padded)
        _, unit, factor = layer_norm(residual_ref[i], 1.0, 0.0)
        upstream = normed_grad_ref[i]
        add(9, upstream * unit)
        add(10, upstream)
        residual_grad = out_grad_ref[i] + norm_back(upstream, unit, factor, vectors[9:10, :])
        input_grad_ref[i] = residual_grad
        rounded = residual_grad.astype(low)
        mixer_in[span, :] = rounded
        add(8, rounded)
        mixed_grad[...] = transposed(rounded, full_ref[1, :, 640:1408]).astype(low)
        for pair in range(HEADS // 2):
            start = 128 * pair
            query_pair = projected_ref[i, :, start : start + 128]
            key_pair = projected_ref[i, :, 768 + start : 896 + start]
            value_pair = projected_ref[i, :, 1536 + start : 1664 + start]
            grad_pair = mixed_grad[:, start : start + 128]
            found = []
            for which in (0, 1):
                probs = key_probs(query_pair, key_pair, which)
                back = transposed(head_of(grad_pair, which), value_pair)
                centre = jnp.sum(probs * back, axis=-1, keepdims=True)
                score_grad = (probs * (back - centre)).astype(low)
                found.append(
                    (
                        plain(score_grad, key_pair) * head_scale,
                        contract_first(score_grad, query_pair) * head_scale,
                        contract_first(probs.astype(low), grad_pair),
                    )
                )
            for part in range(3):
                columns = slice(768 * part + start, 768 * part + start + 128)
                projected_grad[span, columns] = side_by_side(
                    found[0][part], found[1][part]
                ).astype(low)
        whole = projected_grad[span, :]
        add(6, whole[:, 0:768])
        add(7, whole[:, 1536:2304])
        first_grad = transposed(whole[:, 0:1664], full_ref[0]) + transposed(
            whole[:, 1664:2304], full_ref[1, :, 0:640]
        )
        normed, unit, factor = layer_norm(tokens_ref[i], vectors[4:5, :], vectors[5:6, :])
        normed_one[span, :] = normed.astype(low)
        add(4, first_grad * unit)
        add(5, first_grad)
        input_grad_ref[i] += norm_back(first_grad, unit, factor, vectors[4:5, :])

    for start in range(0, width, 256):
        rows = slice(start, start + 256)
        left = normed_one[:, rows].T
        packed[0, rows, :] = plain(left, projected_grad[:, 0:1664]).astype(low)
        packed[1, rows, 0:640] = plain(left, projected_grad[:, 1664:2304]).astype(low)
        left = mixed_ref[:, :, rows].reshape(images * padded, 256).T
        packed[1, rows, 640:1408] = plain(left, mixer_in[...]).astype(low)
    packed[1, :, 1408:1536] = (tail_ref[...] + sums[...].T).astype(low)
    packed[1, :, 1536:1664] = jnp.zeros((width, 128), low)

    pl.semaphore_wait(barrier, len(friends))
    order = [k for k in (2, 1, 3) if k < lines] + [0] if lines == 4 else [0]
    send_core.start()
    send_core.wait()
    for k in order:
        for j in range(1, ways):
            rows = strip_rows(k, j)
            packed[half, rows, :] = (
                packed[half, rows, :].astype(jnp.float32) + core_in[rows, :].astype(jnp.float32)
            ).astype(low)
            send_way(k, j).start()
    for k in order:
        rows = strip_rows(k, 0)
        total = packed[half, rows, :].astype(jnp.float32) + core_in[rows, :].astype(jnp.float32)
        for j in range(1, ways):
            send_way(k, j).wait_recv()
            total = total + way_in[k, j - 1].astype(jnp.float32)
        packed[half, rows, :] = total.astype(low)
        if k:
            send_line(k).start()
    total = packed[half, strip_rows(0, 0), :].astype(jnp.float32)
    for k in order[:-1]:
        send_line(k).wait_recv()
        total = total + line_in[k - 1].astype(jnp.float32)
    copy_in[rep // 2] = total.astype(low)
    for m in range(1, pairs):
        send_copy(m).start()
    for m in range(1, pairs):
        send_copy(m).wait()
    total = copy_in[0].astype(jnp.float32)
    for m in range(1, pairs):
        total = total + copy_in[m].astype(jnp.float32)
    done[half] = total.astype(low)
    send_done.start()
    send_done.wait()
    reduced_ref[...] = done[...]
    for k in order:
        for j in range(1, ways):
            send_way(k, j).wait_send()
        if k:
            send_line(k).wait_send()


def run_backward(lines, ways, copies, tokens, *rest):
    images, padded, width = tokens.shape
    low = jnp.bfloat16
    local = pl.BlockSpec(memory_space=pltpu.VMEM)
    rows = images * padded
    strip = width // (lines * ways)
    dma = pltpu.SemaphoreType.DMA
    return pl.pallas_call(
        functools.partial(backward_kernel, lines, ways, copies),
        name="attention_backward",
        out_shape=[
            jax.ShapeDtypeStruct((images, padded, width), jnp.float32),
            jax.ShapeDtypeStruct((2, strip, 1664), low),
        ],
        in_specs=[local] * 8,
        out_specs=[local] * 2,
        scratch_shapes=[
            pltpu.VMEM((128, width), jnp.float32),
            pltpu.VMEM((128, width), jnp.float32),
            pltpu.VMEM((rows, 3 * width), low),
            pltpu.VMEM((rows, width), low),
            pltpu.VMEM((rows, width), low),
            pltpu.VMEM((padded, width), low),
            pltpu.VMEM((2, width, 1664), low),
            pltpu.VMEM((width, 1664), low),
            pltpu.VMEM((lines, ways - 1, strip, 1664), low),
            pltpu.VMEM((lines - 1, strip, 1664), low),
            pltpu.VMEM((copies // 2, strip, 1664), low),
            pltpu.VMEM((2, strip, 1664), low),
            dma((2, 2)),
            dma((2, lines, ways)),
            dma((2, lines)),
            dma((2, copies // 2)),
        ],
        compiler_params=pltpu.CompilerParams(
            vmem_limit_bytes=62 * 2**20, collective_id=3, has_side_effects=True
        ),
        cost_estimate=pl.CostEstimate(
            flops=60 * images * padded * width * width,
            bytes_accessed=40 * 2**20,
            transcendentals=images * HEADS * padded * padded,
        ),
    )(tokens, *rest)


def dispatch_kernel(slot_ref, rows_ref, rows_out):
    low = jnp.bfloat16
    for k in range(GROUP):
        slot = lax.broadcasted_iota(jnp.int32, (SLOTS, slot_ref.shape[2]), 0)
        seats = (slot == slot_ref[k]).astype(low)
        rows_out[k] = plain(seats, rows_ref[...].astype(low)).astype(low)


def run_dispatch(slot_of, rows):
    token_count, width = rows.shape
    local = pl.BlockSpec(memory_space=pltpu.VMEM)
    return pl.pallas_call(
        dispatch_kernel,
        name="dispatch_gradient",
        out_shape=jax.ShapeDtypeStruct((GROUP, SLOTS, width), jnp.bfloat16),
        in_specs=[local] * 2,
        out_specs=local,
        compiler_params=pltpu.CompilerParams(vmem_limit_bytes=48 * 2**20),
        cost_estimate=pl.CostEstimate(
            flops=2 * GROUP * SLOTS * token_count * width,
            bytes_accessed=8 * 2**20,
            transcendentals=0,
        ),
    )(slot_of, rows)


def seats_of(slot_ref, k):
    slot = lax.broadcasted_iota(jnp.int32, (slot_ref.shape[0], SLOTS), 1)
    return slot == slot_ref[:, k : k + 1]


def combine_kernel(slot_ref, grad_row_ref, grads_ref, normed_ref, probs_ref):
    normed = jnp.zeros(normed_ref.shape, jnp.float32)
    for k in range(GROUP):
        seated = seats_of(slot_ref, k)
        rows = slice(k * SLOTS, (k + 1) * SLOTS)
        normed = normed + plain(seated.astype(jnp.bfloat16), grads_ref[rows, :])
        probs_ref[:, k : k + 1] = jnp.sum(
            jnp.where(seated, grad_row_ref[k], 0.0), axis=1, keepdims=True
        )
    normed_ref[...] = normed


def result_kernel(slot_ref, residual_ref, *refs):
    blocks, out_ref = refs[:GROUP], refs[GROUP]
    total = residual_ref[...]
    for k in range(GROUP):
        total = total + plain(seats_of(slot_ref, k).astype(jnp.bfloat16), blocks[k][...])
    out_ref[...] = total


def run_combine(slot_of, grad_rows, grads):
    token_count, width = slot_of.shape[0], grads.shape[1]
    local = pl.BlockSpec(memory_space=pltpu.VMEM)
    return pl.pallas_call(
        combine_kernel,
        name="combine_gradient",
        out_shape=[
            jax.ShapeDtypeStruct((token_count, width), jnp.float32),
            jax.ShapeDtypeStruct((token_count, GROUP), jnp.float32),
        ],
        in_specs=[local] * 3,
        out_specs=[local] * 2,
        compiler_params=pltpu.CompilerParams(vmem_limit_bytes=56 * 2**20),
        cost_estimate=pl.CostEstimate(
            flops=2 * GROUP * SLOTS * token_count * width,
            bytes_accessed=10 * 2**20,
            transcendentals=0,
        ),
    )(slot_of, grad_rows, grads)


def run_result(slot_of, residual, blocks):
    token_count, width = residual.shape
    local = pl.BlockSpec(memory_space=pltpu.VMEM)
    return pl.pallas_call(
        result_kernel,
        name="combine_result",
        out_shape=jax.ShapeDtypeStruct((token_count, width), jnp.float32),
        in_specs=[local] * (2 + GROUP),
        out_specs=local,
        compiler_params=pltpu.CompilerParams(vmem_limit_bytes=56 * 2**20),
        cost_estimate=pl.CostEstimate(
            flops=2 * GROUP * SLOTS * token_count * width,
            bytes_accessed=10 * 2**20,
            transcendentals=0,
        ),
    )(slot_of, residual, *blocks)


def slot_table(routes, chosen):
    token_count = routes.shape[0]
    hits = (routes[:, :, None] == chosen[None, None, :]).any(axis=1)
    rows = lax.broadcasted_iota(jnp.int32, (token_count, token_count), 0)
    columns = lax.broadcasted_iota(jnp.int32, (token_count, token_count), 1)
    earlier = jnp.dot(
        (columns < rows).astype(jnp.bfloat16),
        hits.astype(jnp.bfloat16),
        preferred_element_type=jnp.float32,
    ).astype(jnp.int32)
    return jnp.where(hits, earlier, -1)


def group_shift(value, copies, along):
    pairs = [
        (copy, copy // GROUP * GROUP + (copy % GROUP + along) % GROUP) for copy in range(copies)
    ]
    return lax.ppermute(value, "rep", pairs)


def exchange(blocks, copies):
    return [blocks[0]] + [group_shift(blocks[k], copies, k) for k in range(1, GROUP)]


def exchange_back(blocks, copies):
    return [blocks[0]] + [group_shift(blocks[k], copies, -k) for k in range(1, GROUP)]


def shards(
    tokens_in,
    routes,
    first_gain,
    first_shift,
    joint_weight,
    joint_bias,
    mixer_weight,
    mixer_bias,
    second_gain,
    second_shift,
    router_weight,
    expert_up,
    upward_bias,
    expert_down,
    downward_bias,
    out_grad,
    *,
    groups,
    copies,
):
    row_count, width = tokens_in.shape
    experts, _, part = expert_up.shape
    strip = first_gain.shape[0]
    hidden_width = part * groups
    images = row_count // SEQ
    token_count = images * PADDED

    def widen(rows, fill=0):
        rows = rows.reshape(images, SEQ, rows.shape[1])
        return jnp.pad(rows, ((0, 0), (0, PADDED - SEQ), (0, 0)), constant_values=fill)

    def narrow(rows):
        return rows.reshape(images, PADDED, width)[:, :SEQ].reshape(row_count, width)

    token_images = widen(tokens_in)
    out_grad = widen(out_grad).reshape(token_count, width)
    routes = widen(routes, -1).reshape(token_count, 2)
    low = jnp.bfloat16
    bias_columns = experts * part // strip

    packed = jnp.concatenate(
        [
            joint_weight,
            mixer_weight,
            router_weight,
            first_gain[:, None],
            first_shift[:, None],
            joint_bias.T,
            mixer_bias[:, None],
            second_gain[:, None],
            second_shift[:, None],
            downward_bias.T,
            upward_bias.reshape(strip, bias_columns),
        ],
        axis=1,
    )
    used = packed.shape[1]
    packed_width = 2 * 1664
    packed = jnp.pad(packed, ((0, 0), (0, packed_width - used)))
    packed = packed.reshape(strip, 2, packed_width // 2).transpose(1, 0, 2)
    lines = 4 if groups % 4 == 0 else 1
    ways = groups // lines
    me = lax.axis_index("rep") % GROUP
    shard = lax.axis_index("shard")
    mine = jnp.stack(
        [
            lax.dynamic_index_in_dim(expert_up, me, 0, keepdims=False),
            lax.dynamic_index_in_dim(expert_down, me, 0, keepdims=False).T,
        ]
    )
    near_experts = (me + jnp.arange(GROUP, dtype=jnp.int32)) % GROUP
    slot_of = slot_table(routes, near_experts)
    slot_lines = slot_of.T[:, None, :]
    grad_slots = run_dispatch(slot_lines, out_grad)
    projected, mixed, residual_one, normed_two, logits, full, rows_in, grad_in, pieces = run_forward(
        token_images, slot_lines, packed, mine, grad_slots, lines, ways, copies
    )
    projected = projected.reshape(token_count, 3 * width)
    mixed = mixed.reshape(token_count, width)
    residual_one = residual_one.reshape(token_count, width)
    normed_two = normed_two.reshape(token_count, width)
    logits = logits.reshape(token_count, -1)[:, :experts]
    near_shards = jnp.stack(
        [
            (shard // ways + k) % lines * ways + (shard % ways + j) % ways
            for k in range(lines)
            for j in range(ways)
        ]
    )
    tail = full[1, :, 1408:1536]
    router_full = tail[:, :experts]
    down_shift = tail[:, experts + 7 : 2 * experts + 7].astype(jnp.float32).T
    up_shift = (
        tail[:, 2 * experts + 7 : 2 * experts + 7 + bias_columns]
        .reshape(groups, experts, part)
        .astype(jnp.float32)
    )
    up_shift = lax.dynamic_index_in_dim(up_shift, me, 1, keepdims=False)[near_shards]
    up_shift = up_shift.reshape(lines, 1, ways * part)
    down_shift = lax.dynamic_index_in_dim(down_shift, me, 0, keepdims=True)
    router_probs = jax.nn.softmax(logits, axis=-1)

    probs_near = router_probs[:, near_experts]
    seated = slot_lines == jnp.arange(SLOTS, dtype=jnp.int32)[None, :, None]
    gate_slots = jnp.sum(jnp.where(seated, probs_near.T[:, None, :], 0.0), axis=-1)
    gate_in = jnp.concatenate(exchange(gate_slots, copies), axis=0)[:, None]
    if part % 128:
        joined = [[jnp.concatenate(line, axis=2)] for line in pieces]
    else:
        joined = pieces
    weighted, dispatched_grad, gate_grad, up_shift_grad, down_shift_grad, up, down = run_expert(
        rows_in, grad_in, gate_in, up_shift, down_shift, joined, ways, part
    )
    def from_group(value):
        every = lax.all_gather(value, "rep", axis=0)
        if copies == GROUP:
            return every.astype(jnp.float32)
        return every.astype(jnp.float32).reshape((-1, GROUP) + value.shape).sum(axis=0)

    up_grad = from_group(up)
    down_grad = from_group(down)

    gate_grad = jnp.stack(exchange_back(gate_grad.reshape(GROUP, SLOTS), copies))
    normed_grad, probs_grad = run_combine(slot_of, gate_grad[:, None, :], dispatched_grad)
    weighted = exchange_back(weighted.reshape(GROUP, SLOTS, width), copies)
    probs_grad = probs_grad[:, (jnp.arange(GROUP, dtype=jnp.int32) - me) % GROUP]
    own = (jnp.arange(experts, dtype=jnp.int32) == me).astype(jnp.float32)[:, None]
    down_shift_grad = own * down_shift_grad
    up_shift_grad = jnp.zeros((groups, part), jnp.float32).at[near_shards].set(
        up_shift_grad.reshape(groups, part)
    )
    up_shift_grad = own * up_shift_grad.reshape(1, hidden_width)
    logit_grad = (
        router_probs * (probs_grad - jnp.sum(router_probs * probs_grad, axis=-1, keepdims=True))
    ).astype(low)
    router_grad = contract_first(normed_two, logit_grad)
    normed_grad = normed_grad + contract_last(logit_grad, router_full)
    tail_grad = jnp.concatenate(
        [
            router_grad,
            jnp.zeros((width, 7), jnp.float32),
            down_shift_grad.T,
            up_shift_grad.reshape(experts, groups, part)
            .transpose(1, 0, 2)
            .reshape(groups * strip, bias_columns),
        ],
        axis=1,
    )
    tail_grad = jnp.pad(tail_grad, ((0, 0), (0, 4 * width + 128 - used)))

    def by_image(rows):
        return rows.reshape(images, PADDED, rows.shape[1])

    input_grad, reduced = run_backward(
        lines,
        ways,
        copies,
        token_images,
        by_image(out_grad),
        by_image(residual_one),
        by_image(normed_grad),
        by_image(mixed),
        by_image(projected),
        tail_grad,
        full,
    )
    late_residual, reduced = lax.optimization_barrier((residual_one, reduced))
    block_out = run_result(slot_of, late_residual, weighted)
    packed_grad = reduced.astype(jnp.float32).transpose(1, 0, 2).reshape(strip, packed_width)
    end = packed_grad[:, 4 * width :]
    line = end[:, experts : experts + 7].T
    return (
        narrow(block_out),
        narrow(input_grad),
        line[0],
        line[1],
        packed_grad[:, : 3 * width],
        line[2:4],
        packed_grad[:, 3 * width : 4 * width],
        line[4],
        line[5],
        line[6],
        end[:, :experts],
        up_grad,
        end[:, 2 * experts + 7 : 2 * experts + 7 + bias_columns].reshape(experts, part),
        down_grad,
        end[:, experts + 7 : 2 * experts + 7].T,
    )


def solution(mesh):
    placed = (
        P(("shard", "rep"), None),
        P(("shard", "rep"), None),
        P("shard"),
        P("shard"),
        P("shard", None),
        P(None, "shard"),
        P("shard", None),
        P("shard"),
        P("shard"),
        P("shard"),
        P("shard", None),
        P(None, None, "shard"),
        P(None, "shard"),
        P(None, "shard", None),
        P(None, "shard"),
        P(("shard", "rep"), None),
    )
    return jax.shard_map(
        functools.partial(
            shards, groups=mesh.shape["shard"], copies=mesh.shape["rep"]
        ),
        mesh=mesh,
        in_specs=placed,
        out_specs=(
            P(("shard", "rep"), None),
            P(("shard", "rep"), None),
            P("shard"),
            P("shard"),
            P("shard", None),
            P(None, "shard"),
            P("shard", None),
            P("shard"),
            P("shard"),
            P("shard"),
            P("shard", None),
            P(None, None, "shard"),
            P(None, "shard"),
            P(None, "shard", None),
            P(None, "shard"),
        ),
        check_vma=False,
    )
```

```python
import functools

import jax
import jax.numpy as jnp
from jax import lax
from jax.experimental import pallas as pl
from jax.experimental.pallas import tpu as pltpu
from jax.sharding import PartitionSpec as P

HEADS = 12
HEAD_DIM = 64
SEQ = 197
SLOTS = 624
PADDED = 208
GROUP = 4


epsilon = 1e-06


def layer_norm(values, gain, shift):
    centre = jnp.mean(values, axis=-1, keepdims=True)
    centred = values - centre
    spread = jnp.mean(centred * centred, axis=-1, keepdims=True)
    factor = lax.rsqrt(spread + epsilon)
    unit_rows = centred * factor
    return (unit_rows * gain + shift, unit_rows, factor)


def norm_back(upstream, unit_rows, factor, gain):
    scaled = upstream * gain
    middle = jnp.mean(scaled, axis=-1, keepdims=True)
    along = jnp.mean(scaled * unit_rows, axis=-1, keepdims=True)
    return factor * (scaled - middle - unit_rows * along)


def contract_first(left_rows, right_rows):
    return lax.dot_general(
        left_rows, right_rows, (((0,), (0,)), ((), ())), preferred_element_type=jnp.float32
    )


def contract_last(left_rows, right_rows):
    return lax.dot_general(
        left_rows, right_rows, (((1,), (1,)), ((), ())), preferred_element_type=jnp.float32
    )


def transposed(left_rows, right_rows):
    return lax.dot_general(
        left_rows, right_rows, (((1,), (1,)), ((), ())), preferred_element_type=jnp.float32
    )


def plain(left_rows, right_rows):
    return jnp.dot(left_rows, right_rows, preferred_element_type=jnp.float32)


def normal_parts(hidden):
    bell = jnp.exp(-0.5 * hidden * hidden)
    near = 1.0 / (1.0 + (0.3275911 * 0.7071067811865476) * jnp.abs(hidden))
    tail = near * (
        0.127414796
        + near * (-0.142248368 + near * (0.7107068705 + near * (-0.7265760135 + near * 0.5307027145)))
    )
    tail = tail * bell
    return jnp.where(hidden < 0.0, tail, 1.0 - tail), bell * 0.3989422804014327


def expert_kernel(order, joined, ways, *refs):
    low = jnp.bfloat16
    x_ref, g_ref, gate_ref, up_shift_ref, down_shift_ref = refs[:5]
    refs = refs[5:]
    steps = len(order)
    pieces = [refs[k * joined : (k + 1) * joined] for k in range(steps)]
    refs = refs[steps * joined :]
    out_ref, dx_ref, gate_grad_ref, up_shift_grad_ref, down_shift_grad_ref = refs[:5]
    up_ref, down_ref, own_ref, way_ref, line_ref = refs[5:10]
    refs = refs[10:]
    rg, xt, rgt, act, hg, y_sum, dx_sum, weights, grad_buf, stage = refs[:10]
    in_sem, own_sem, stage_sem, end_sem, way_sem, line_sem, back_sem = refs[10:]
    rows, width = x_ref.shape
    part = up_ref.shape[1]
    block = part * ways
    piece = block // joined
    chunk = SLOTS
    chunks = rows // chunk

    shard = lax.axis_index("shard")
    rep = lax.axis_index("rep")
    line, way = shard // ways, shard % ways
    lines = steps

    def place(k, j):
        index = lax.rem(line + k + lines, lines) * ways + lax.rem(way + j + ways, ways)
        return {"shard": index}

    def group(k):
        spot = rep % GROUP
        return {"rep": rep - spot + lax.rem(spot + k + GROUP, GROUP)}

    friends = [place(k, 0) for k in range(1, lines)] + [place(0, j) for j in range(1, ways)]
    friends += [group(k) for k in range(1, GROUP)]
    barrier = pltpu.get_barrier_semaphore()
    for friend in friends:
        pl.semaphore_signal(barrier, inc=1, device_id=friend, device_id_type=pl.DeviceIdType.MESH)

    def remote(source, target, sems, index, device):
        return pltpu.make_async_remote_copy(
            src_ref=source,
            dst_ref=target,
            send_sem=sems.at[(0,) + index],
            recv_sem=sems.at[(1,) + index],
            device_id=device,
            device_id_type=pl.DeviceIdType.MESH,
        )

    def load(step):
        return [
            pltpu.make_async_copy(
                pieces[order[step]][j],
                weights.at[step % 2, :, :, pl.ds(j * piece, piece)],
                in_sem.at[step % 2, j],
            )
            for j in range(joined)
        ]

    def keep(step):
        return pltpu.make_async_copy(grad_buf.at[0], own_ref.at[step], own_sem.at[0])

    def send_way(step, j):
        return remote(grad_buf.at[j], way_ref.at[step, j - 1], way_sem, (step, j), place(0, j))

    def send_line(step):
        k = order[step]
        return remote(own_ref.at[step], line_ref.at[k - 1], line_sem, (k,), place(k, 0))

    def fetch(source, slot):
        return pltpu.make_async_copy(source, stage.at[slot], stage_sem.at[slot])

    def add_ways(step):
        copies = [fetch(own_ref.at[step], 0)]
        for j in range(1, ways):
            send_way(step, j).wait_recv()
            copies.append(fetch(way_ref.at[step, j - 1], j))
        for copy in copies:
            copy.start()
        for copy in copies:
            copy.wait()

        @pl.loop(0, width // 256)
        def _(c):
            span = pl.ds(pl.multiple_of(c * 256, 256), 256)
            for u in range(2):
                total = stage[0, u, span, :].astype(jnp.float32)
                for j in range(1, ways):
                    total = total + stage[j, u, span, :].astype(jnp.float32)
                stage[0, u, span, :] = total.astype(low)

    def finish(step):
        add_ways(step)
        write = pltpu.make_async_copy(stage.at[0], own_ref.at[step], own_sem.at[1])
        write.start()
        write.wait()
        send_line(step).start()

    def send_back(k):
        block_rows = pl.ds(k * chunk, chunk)
        return remote(
            hg.at[block_rows, pl.ds(0, width)],
            dx_ref.at[block_rows, :],
            back_sem,
            (k,),
            group(-k),
        )

    for copy in load(0):
        copy.start()

    down_shift_grad_ref[...] = jnp.zeros_like(down_shift_grad_ref)

    @pl.loop(0, chunks)
    def _(c):
        span = pl.ds(pl.multiple_of(c * chunk, chunk), chunk)
        scaled = (g_ref[span, :].astype(jnp.float32) * gate_ref[span, :]).astype(low)
        rg[span, :] = scaled
        down_shift_grad_ref[...] += jnp.sum(scaled.astype(jnp.float32), axis=0, keepdims=True)
        y_sum[span, :] = jnp.zeros((chunk, width), jnp.float32)
        dx_sum[span, :] = jnp.zeros((chunk, width), jnp.float32)

    for start in range(0, width, 256):
        xt[start : start + 256, :] = x_ref[:, start : start + 256].T
        rgt[start : start + 256, :] = rg[:, start : start + 256].T

    for step in range(steps):
        for copy in load(step):
            copy.wait()
        if step + 1 < steps:
            for copy in load(step + 1):
                copy.start()
        slot = step % 2
        up_shift_grad_ref[step] = jnp.zeros((1, block), jnp.float32)

        @pl.loop(0, chunks)
        def _(c):
            span = pl.ds(pl.multiple_of(c * chunk, chunk), chunk)
            x_rows = x_ref[span, :]
            g_rows = rg[span, :]
            for start in range(0, block, 256):
                part_span = slice(start, start + 256)
                hidden = plain(x_rows, weights[slot, 0, :, part_span]) + up_shift_ref[step, :, part_span]
                back = plain(g_rows, weights[slot, 1, :, part_span])
                cdf, density = normal_parts(hidden)
                act[span, part_span] = (hidden * cdf).astype(low)
                hidden_grad = (back * (cdf + hidden * density)).astype(low)
                hg[span, part_span] = hidden_grad
                up_shift_grad_ref[step, :, part_span] += jnp.sum(
                    hidden_grad.astype(jnp.float32), axis=0, keepdims=True
                )
            y_sum[span, :] += transposed(act[span, :], weights[slot, 1])
            dx_sum[span, :] += transposed(hg[span, :], weights[slot, 0])

        if step == 0:
            pl.semaphore_wait(barrier, len(friends))
        else:
            keep(step - 1).wait()
            for j in range(1, ways):
                send_way(step - 1, j).wait_send()

        @pl.loop(0, width // 256)
        def _(c):
            span = pl.ds(pl.multiple_of(c * 256, 256), 256)
            for u, found in enumerate((plain(xt[span, :], hg[...]), plain(rgt[span, :], act[...]))):
                for j in range(ways):
                    grad_buf[j, u, span, :] = found[:, j * part : (j + 1) * part].astype(low)

        keep(step).start()
        for j in range(1, ways):
            send_way(step, j).start()
        if step > 0:
            finish(step - 1)

    @pl.loop(0, chunks)
    def _(c):
        span = pl.ds(pl.multiple_of(c * chunk, chunk), chunk)
        hg[span, :width] = dx_sum[span, :].astype(low)
        result = y_sum[span, :] + down_shift_ref[...]
        act[span, :width] = (result * gate_ref[span, :]).astype(low)
        gate_grad_ref[span, :] = jnp.sum(
            result * g_ref[span, :].astype(jnp.float32), axis=1, keepdims=True
        )

    home = pl.ds(0, chunk)
    ends = [
        pltpu.make_async_copy(hg.at[home, pl.ds(0, width)], dx_ref.at[home, :], end_sem.at[0]),
        pltpu.make_async_copy(act.at[:, pl.ds(0, width)], out_ref, end_sem.at[1]),
    ]
    for k in range(1, GROUP):
        send_back(k).start()
    for copy in ends:
        copy.start()

    last = steps - 1
    keep(last).wait()
    add_ways(last)
    for k in sorted(order[:-1], key=order.index):
        send_line(order.index(k)).wait_recv()
        copy = fetch(line_ref.at[k - 1], 1)
        copy.start()
        copy.wait()
        first, final = k == order[0], k == order[-2]

        @pl.loop(0, width // 256)
        def _(c):
            span = pl.ds(pl.multiple_of(c * 256, 256), 256)
            for u in range(2):
                sums = pl.ds(pl.multiple_of(u * width + c * 256, 256), 256)
                total = stage[1, u, span, :].astype(jnp.float32)
                if first:
                    total = total + stage[0, u, span, :].astype(jnp.float32)
                else:
                    total = total + y_sum[sums, 0:part]
                if final:
                    stage[0, u, span, :] = total.astype(low)
                else:
                    y_sum[sums, 0:part] = total

    up_ref[...] = stage[0, 0]
    down_ref[...] = stage[0, 1].astype(jnp.float32).T.astype(low)
    for j in range(1, ways):
        send_way(last, j).wait_send()
    for step in range(last):
        send_line(step).wait_send()
    for k in range(1, GROUP):
        send_back(k).wait()
    for copy in ends:
        copy.wait()


def run_expert(rows_in, grad_in, gate_in, up_shift, down_shift, pieces, ways, part):
    steps, joined = len(pieces), len(pieces[0])
    order = [2, 1, 3, 0] if steps == 4 else list(range(1, steps)) + [0]
    rows, width = rows_in.shape
    block = part * ways
    low = jnp.bfloat16
    everywhere = pl.BlockSpec(memory_space=pl.ANY)
    local = pl.BlockSpec(memory_space=pltpu.VMEM)
    flat = [piece for line in pieces for piece in line]
    dma = pltpu.SemaphoreType.DMA
    up_shift = jnp.stack([up_shift[k] for k in order])
    outs = pl.pallas_call(
        functools.partial(expert_kernel, order, joined, ways),
        name="expert_block",
        out_shape=[
            jax.ShapeDtypeStruct((rows, width), low),
            jax.ShapeDtypeStruct((rows, width), low),
            jax.ShapeDtypeStruct((rows, 1), jnp.float32),
            jax.ShapeDtypeStruct((steps, 1, block), jnp.float32),
            jax.ShapeDtypeStruct((1, width), jnp.float32),
            jax.ShapeDtypeStruct((width, part), low),
            jax.ShapeDtypeStruct((part, width), low),
            jax.ShapeDtypeStruct((steps, 2, width, part), low),
            jax.ShapeDtypeStruct((steps, ways - 1, 2, width, part), low),
            jax.ShapeDtypeStruct((steps - 1, 2, width, part), low),
        ],
        in_specs=[local] * 5 + [everywhere] * len(flat),
        out_specs=[everywhere, everywhere] + [local] * 5 + [everywhere] * 3,
        scratch_shapes=[
            pltpu.VMEM((rows, width), low),
            pltpu.VMEM((width, rows), low),
            pltpu.VMEM((width, rows), low),
            pltpu.VMEM((rows, block), low),
            pltpu.VMEM((rows, block), low),
            pltpu.VMEM((rows, width), jnp.float32),
            pltpu.VMEM((rows, width), jnp.float32),
            pltpu.VMEM((2, 2, width, block), low),
            pltpu.VMEM((ways, 2, width, part), low),
            pltpu.VMEM((ways, 2, width, part), low),
            dma((2, joined)),
            dma((2,)),
            dma((ways,)),
            dma((2,)),
            dma((2, steps, ways)),
            dma((2, steps)),
            dma((2, GROUP)),
        ],
        compiler_params=pltpu.CompilerParams(
            vmem_limit_bytes=63 * 2**20, collective_id=2, has_side_effects=True
        ),
        cost_estimate=pl.CostEstimate(
            flops=12 * rows * width * block * steps,
            bytes_accessed=12 * rows * width + 8 * width * block * steps,
            transcendentals=rows * block * steps,
        ),
    )(rows_in, grad_in, gate_in, up_shift, down_shift, *flat)
    weighted, dispatched_grad, gate_grad, up_shift_grad, down_shift_grad, up, down = outs[:7]
    up_shift_grad = jnp.stack([up_shift_grad[order.index(k)] for k in range(steps)])
    return weighted, dispatched_grad, gate_grad, up_shift_grad, down_shift_grad, up, down


def side_by_side(first, second):
    lane = lax.broadcasted_iota(jnp.int32, first.shape, 1)
    return jnp.where(lane < HEAD_DIM, first, second)


def head_of(pair, which):
    lane = lax.broadcasted_iota(jnp.int32, pair.shape, 1)
    keep = lane < HEAD_DIM if which == 0 else lane >= HEAD_DIM
    return jnp.where(keep, pair, jnp.zeros_like(pair))


def key_probs(query_pair, key_pair, which):
    scores = transposed(head_of(query_pair, which), key_pair) * HEAD_DIM ** (-0.5)
    column = lax.broadcasted_iota(jnp.int32, scores.shape, 1)
    scores = jnp.where(column < SEQ, scores, -1e30)
    raised = jnp.exp(scores - jnp.max(scores, axis=-1, keepdims=True))
    return raised * (1.0 / jnp.sum(raised, axis=-1, keepdims=True))


def forward_kernel(lines, ways, copies, *refs):
    low = jnp.bfloat16
    tokens_ref, slot_ref, packed_ref, mine_ref, grad_slots_ref = refs[:5]
    refs = refs[5:]
    projected_ref, mixed_ref, residual_ref, normed_ref, logits_ref, weights_out = refs[:6]
    rows_in_ref, grad_in_ref = refs[6:8]
    refs = refs[8:]
    pieces = [refs[k * ways : (k + 1) * ways] for k in range(lines)]
    refs = refs[lines * ways :]
    full, vectors, rows_out = refs[:3]
    own_sem, save_sem = refs[3:5]
    line_sem, way_sem, core_sem, piece_line_sem, piece_way_sem, token_sem = refs[5:]

    images, padded, width = tokens_ref.shape
    strip = packed_ref.shape[1]
    shard = lax.axis_index("shard")
    rep = lax.axis_index("rep")
    line, way = shard // ways, shard % ways
    half = rep % 2

    def place(k, j):
        return lax.rem(line + k + lines, lines) * ways + lax.rem(way + j + ways, ways)

    def at_shard(index):
        return {"shard": index}

    def group(k):
        spot = rep % GROUP
        return {"rep": rep - spot + lax.rem(spot + k, GROUP)}

    partner = {"rep": rep + 1 - 2 * half}
    friends = [at_shard(place(k, 0)) for k in range(1, lines)]
    friends += [at_shard(place(0, j)) for j in range(1, ways)]
    friends += [group(k) for k in range(1, GROUP)]
    barrier = pltpu.get_barrier_semaphore()
    for friend in friends:
        pl.semaphore_signal(barrier, inc=1, device_id=friend, device_id_type=pl.DeviceIdType.MESH)
    pl.semaphore_wait(barrier, len(friends))

    def remote(source, target, sems, index, device):
        return pltpu.make_async_remote_copy(
            src_ref=source,
            dst_ref=target,
            send_sem=sems.at[(0,) + index],
            recv_sem=sems.at[(1,) + index],
            device_id=device,
            device_id_type=pl.DeviceIdType.MESH,
        )

    def strip_of(k, j, side):
        rows = pl.ds(pl.multiple_of(place(k, j) * strip, strip), strip)
        return full.at[side, rows, :]

    def strip_line(k):
        return remote(packed_ref.at[half], strip_of(0, 0, half), line_sem, (k,), at_shard(place(-k, 0)))

    def strip_way(k, j):
        source = packed_ref.at[half] if k == 0 else strip_of(k, 0, half)
        return remote(source, strip_of(k, 0, half), way_sem, (k, j), at_shard(place(0, -j)))

    def strip_core(k, j):
        return remote(strip_of(k, j, half), strip_of(k, j, half), core_sem, (k, j), partner)

    def piece_line(k, u):
        return remote(
            mine_ref.at[u], pieces[k][0].at[u], piece_line_sem, (k, u), at_shard(place(-k, 0))
        )

    def piece_way(k, j, u):
        source = mine_ref.at[u] if k == 0 else pieces[k][0].at[u]
        return remote(source, pieces[k][j].at[u], piece_way_sem, (k, j, u), at_shard(place(0, -j)))

    def block_of(ref, k):
        return ref.at[pl.ds(k * SLOTS, SLOTS), :]

    def send_grad(k):
        return remote(grad_slots_ref.at[k], block_of(grad_in_ref, k), token_sem, (0, k), group(k))

    def send_rows(k):
        return remote(rows_out.at[k], block_of(rows_in_ref, k), token_sem, (1, k), group(k))

    own_grad = pltpu.make_async_copy(grad_slots_ref.at[0], block_of(grad_in_ref, 0), own_sem.at[2])
    own_rows = pltpu.make_async_copy(rows_out.at[0], block_of(rows_in_ref, 0), own_sem.at[3])
    own = pltpu.make_async_copy(
        packed_ref, full.at[:, pl.ds(pl.multiple_of(shard * strip, strip), strip), :], own_sem.at[0]
    )
    own_piece = pltpu.make_async_copy(mine_ref, pieces[0][0], own_sem.at[1])
    order = [k for k in (1, lines - 1, 2) if 0 < k < lines]
    order = list(dict.fromkeys(order))
    own.start()
    for k in order:
        strip_line(k).start()
    for j in range(1, ways):
        strip_way(0, j).start()
    own_piece.start()
    for j in range(1, ways):
        strip_way(0, j).wait_recv()
        strip_core(0, j).start()
    for k in order:
        strip_line(k).wait_recv()
        for j in range(1, ways):
            strip_way(k, j).start()
        strip_core(k, 0).start()
    for u in range(2):
        for k in order:
            piece_line(k, u).start()
        for j in range(1, ways):
            piece_way(0, j, u).start()
    for k in order:
        for j in range(1, ways):
            strip_way(k, j).wait_recv()
            strip_core(k, j).start()
    own_grad.start()
    for k in (2, 1, 3):
        send_grad(k).start()
    for k in range(lines):
        for j in range(ways):
            if k or j:
                strip_core(k, j).wait_recv()
    own.wait()
    save = pltpu.make_async_copy(full, weights_out, save_sem.at[0])
    save.start()

    vectors[...] = full[1, :, 1408:1536].astype(jnp.float32).T

    def pass_on(k, u):
        piece_line(k, u).wait_recv()
        for j in range(1, ways):
            piece_way(k, j, u).start()

    events = [(k, u) for u in range(2) for k in order]

    @pl.loop(0, images)
    def _(i):
        rows = tokens_ref[i]
        normed, _, _ = layer_norm(rows, vectors[4:5, :], vectors[5:6, :])
        normed = normed.astype(low)
        left = plain(normed, full[0])
        projected_ref[i, :, 0:768] = (left[:, 0:768] + vectors[6:7, :]).astype(low)
        projected_ref[i, :, 768:1536] = left[:, 768:1536].astype(low)
        right = plain(normed, full[1, :, 0:640])
        projected_ref[i, :, 1536:1664] = (left[:, 1536:1664] + vectors[7:8, 0:128]).astype(low)
        projected_ref[i, :, 1664:2304] = (right + vectors[7:8, 128:768]).astype(low)
        for pair in range(HEADS // 2):
            start = 128 * pair
            query_pair = projected_ref[i, :, start : start + 128]
            key_pair = projected_ref[i, :, 768 + start : 896 + start]
            value_pair = projected_ref[i, :, 1536 + start : 1664 + start]
            parts = [
                plain(key_probs(query_pair, key_pair, which).astype(low), value_pair)
                for which in (0, 1)
            ]
            mixed_ref[i, :, start : start + 128] = side_by_side(*parts).astype(low)
        residual = rows + (plain(mixed_ref[i], full[1, :, 640:1408]) + vectors[8:9, :])
        residual_ref[i] = residual
        normed_two, _, _ = layer_norm(residual, vectors[9:10, :], vectors[10:11, :])
        normed_two = normed_two.astype(low)
        normed_ref[i] = normed_two
        logits_ref[i] = plain(normed_two, full[1, :, 1408:1536])

        for number, event in enumerate(events[:2]):

            @pl.when(i == 2 * number + 1)
            def _():
                pass_on(*event)

    done = min(2, len(events)) if images >= 4 else 0
    for event in events[done : done + 1]:
        pass_on(*event)
    token_count = images * padded
    for k in (2, 1, 3, 0):
        slot = lax.broadcasted_iota(jnp.int32, (SLOTS, token_count), 0)
        seats = (slot == slot_ref[k]).astype(low)
        rows_out[k] = plain(seats, normed_ref[...].reshape(token_count, width)).astype(low)
        if k:
            send_rows(k).start()
    own_rows.start()
    for event in events[done + 1 :]:
        pass_on(*event)
    for u in range(2):
        for k in range(lines):
            for j in range(1, ways):
                piece_way(k, j, u).wait_recv()
    for k in range(1, GROUP):
        send_grad(k).wait()
        send_rows(k).wait()
    own_grad.wait()
    own_rows.wait()
    save.wait()
    own_piece.wait()
    for k in order:
        strip_line(k).wait_send()
        for u in range(2):
            piece_line(k, u).wait_send()
    for k in range(lines):
        for j in range(ways):
            if k or j:
                strip_core(k, j).wait_send()
            if j:
                strip_way(k, j).wait_send()
                for u in range(2):
                    piece_way(k, j, u).wait_send()


def run_forward(tokens, slot_lines, packed, mine, grad_slots, lines, ways, copies):
    images, padded, width = tokens.shape
    low = jnp.bfloat16
    everywhere = pl.BlockSpec(memory_space=pl.ANY)
    local = pl.BlockSpec(memory_space=pltpu.VMEM)
    half_width = packed.shape[2]
    dma = pltpu.SemaphoreType.DMA
    outs = pl.pallas_call(
        functools.partial(forward_kernel, lines, ways, copies),
        name="attention_forward",
        out_shape=[
            jax.ShapeDtypeStruct((images, padded, 3 * width), low),
            jax.ShapeDtypeStruct((images, padded, width), low),
            jax.ShapeDtypeStruct((images, padded, width), jnp.float32),
            jax.ShapeDtypeStruct((images, padded, width), low),
            jax.ShapeDtypeStruct((images, padded, 128), jnp.float32),
            jax.ShapeDtypeStruct((2, width, half_width), low),
            jax.ShapeDtypeStruct((GROUP * SLOTS, width), low),
            jax.ShapeDtypeStruct((GROUP * SLOTS, width), low),
        ]
        + [jax.ShapeDtypeStruct(mine.shape, low) for _ in range(lines * ways)],
        in_specs=[local, local, everywhere, everywhere, everywhere],
        out_specs=[local] * 5 + [everywhere] * (3 + lines * ways),
        scratch_shapes=[
            pltpu.VMEM((2, width, half_width), low),
            pltpu.VMEM((128, width), jnp.float32),
            pltpu.VMEM((GROUP, SLOTS, width), low),
            dma((4,)),
            dma((1,)),
            dma((2, lines)),
            dma((2, lines, ways)),
            dma((2, lines, ways)),
            dma((2, lines, 2)),
            dma((2, lines, ways, 2)),
            dma((2, 2, GROUP)),
        ],
        compiler_params=pltpu.CompilerParams(
            vmem_limit_bytes=60 * 2**20, collective_id=1, has_side_effects=True
        ),
        cost_estimate=pl.CostEstimate(
            flops=10 * images * padded * width * width,
            bytes_accessed=300 * 2**20,
            transcendentals=images * HEADS * padded * padded,
        ),
    )(tokens, slot_lines, packed, mine, grad_slots)
    pieces = outs[8:]
    return list(outs[:8]) + [[pieces[k * ways : (k + 1) * ways] for k in range(lines)]]


def backward_kernel(
    lines,
    ways,
    copies,
    tokens_ref,
    out_grad_ref,
    residual_ref,
    normed_grad_ref,
    mixed_ref,
    projected_ref,
    tail_ref,
    full_ref,
    slot_ref,
    results_ref,
    input_grad_ref,
    reduced_ref,
    out_ref,
    vectors,
    sums,
    projected_grad,
    mixer_in,
    normed_one,
    mixed_grad,
    packed,
    core_in,
    way_in,
    line_in,
    copy_in,
    done,
    results,
    core_sem,
    way_sem,
    line_sem,
    copy_sem,
    back_sem,
    own_sem,
):
    strip = reduced_ref.shape[1]
    shard = lax.axis_index("shard")
    rep = lax.axis_index("rep")
    line, way = shard // ways, shard % ways
    half = rep % 2
    pairs = copies // 2

    def place(k, j):
        return lax.rem(line + k + lines, lines) * ways + lax.rem(way + j + ways, ways)

    def at_shard(index):
        return {"shard": index}

    partner = {"rep": rep + 1 - 2 * half}

    def group(k):
        spot = rep % GROUP
        return {"rep": rep - spot + lax.rem(spot + k + GROUP, GROUP)}

    def next_copy(m):
        return {"rep": lax.rem(rep + 2 * m, copies)}

    friends = [at_shard(place(k, 0)) for k in range(1, lines)]
    friends += [at_shard(place(0, j)) for j in range(1, ways)]
    friends += [group(k) for k in range(1, GROUP)]
    if copies > GROUP:
        friends += [next_copy(m) for m in range(1, pairs)]
    barrier = pltpu.get_barrier_semaphore()
    for friend in friends:
        pl.semaphore_signal(barrier, inc=1, device_id=friend, device_id_type=pl.DeviceIdType.MESH)

    def remote(source, target, sems, index, device):
        return pltpu.make_async_remote_copy(
            src_ref=source,
            dst_ref=target,
            send_sem=sems.at[(0,) + index],
            recv_sem=sems.at[(1,) + index],
            device_id=device,
            device_id_type=pl.DeviceIdType.MESH,
        )

    def strip_rows(k, j):
        return pl.ds(pl.multiple_of(place(k, j) * strip, strip), strip)

    def send_core(start):
        rows = pl.ds(start, 256)
        return remote(
            packed.at[1 - half, rows, :], core_in.at[rows, :], core_sem, (start // 256,), partner
        )

    def send_way(k, j):
        return remote(
            packed.at[half, strip_rows(k, j), :],
            way_in.at[k, j - 1],
            way_sem,
            (k, j),
            at_shard(place(0, j)),
        )

    def send_line(k):
        return remote(
            packed.at[half, strip_rows(k, 0), :],
            line_in.at[k - 1],
            line_sem,
            (k,),
            at_shard(place(k, 0)),
        )

    def send_back(k):
        block_rows = pl.ds(k * SLOTS, SLOTS)
        return remote(
            results_ref.at[block_rows, :], results.at[block_rows, :], back_sem, (k,), group(-k)
        )

    home = pl.ds(0, SLOTS)
    own_results = pltpu.make_async_copy(
        results_ref.at[home, :], results.at[home, :], own_sem.at[0]
    )

    def send_copy(m):
        return remote(copy_in.at[rep // 2], copy_in.at[rep // 2], copy_sem, (m,), next_copy(m))

    send_done = remote(done.at[half], done.at[half], core_sem, (3,), partner)

    low = jnp.bfloat16
    images, padded, width = tokens_ref.shape
    vectors[...] = full_ref[1, :, 1408:1536].astype(jnp.float32).T
    sums[...] = jnp.zeros_like(sums)
    head_scale = HEAD_DIM ** (-0.5)

    pl.semaphore_wait(barrier, len(friends))
    own_results.start()
    for k in (2, 1, 3):
        send_back(k).start()

    def result(i):
        span = pl.ds(pl.multiple_of(i * padded, padded), padded)
        slots = slot_ref[span, :]
        total = residual_ref[i]
        column = lax.broadcasted_iota(jnp.int32, (padded, SLOTS), 1)
        for k in range(GROUP):
            seats = (column == slots[:, k : k + 1]).astype(low)
            total = total + plain(seats, results[k * SLOTS : (k + 1) * SLOTS, :])
        out_ref[i] = total

    def add(row, values):
        sums[row : row + 1, :] += jnp.sum(values.astype(jnp.float32), axis=0, keepdims=True)

    @pl.loop(0, images)
    def _(i):
        span = pl.ds(pl.multiple_of(i * padded, padded), padded)
        _, unit, factor = layer_norm(residual_ref[i], 1.0, 0.0)
        upstream = normed_grad_ref[i]
        add(9, upstream * unit)
        add(10, upstream)
        residual_grad = out_grad_ref[i] + norm_back(upstream, unit, factor, vectors[9:10, :])
        input_grad_ref[i] = residual_grad
        rounded = residual_grad.astype(low)
        mixer_in[span, :] = rounded
        add(8, rounded)
        mixed_grad[...] = transposed(rounded, full_ref[1, :, 640:1408]).astype(low)
        for pair in range(HEADS // 2):
            start = 128 * pair
            query_pair = projected_ref[i, :, start : start + 128]
            key_pair = projected_ref[i, :, 768 + start : 896 + start]
            value_pair = projected_ref[i, :, 1536 + start : 1664 + start]
            grad_pair = mixed_grad[:, start : start + 128]
            found = []
            for which in (0, 1):
                probs = key_probs(query_pair, key_pair, which)
                back = transposed(head_of(grad_pair, which), value_pair)
                centre = jnp.sum(probs * back, axis=-1, keepdims=True)
                score_grad = (probs * (back - centre)).astype(low)
                found.append(
                    (
                        plain(score_grad, key_pair) * head_scale,
                        contract_first(score_grad, query_pair) * head_scale,
                        contract_first(probs.astype(low), grad_pair),
                    )
                )
            for part in range(3):
                columns = slice(768 * part + start, 768 * part + start + 128)
                projected_grad[span, columns] = side_by_side(
                    found[0][part], found[1][part]
                ).astype(low)
        whole = projected_grad[span, :]
        add(6, whole[:, 0:768])
        add(7, whole[:, 1536:2304])
        first_grad = transposed(whole[:, 0:1664], full_ref[0]) + transposed(
            whole[:, 1664:2304], full_ref[1, :, 0:640]
        )
        normed, unit, factor = layer_norm(tokens_ref[i], vectors[4:5, :], vectors[5:6, :])
        normed_one[span, :] = normed.astype(low)
        add(4, first_grad * unit)
        add(5, first_grad)
        input_grad_ref[i] += norm_back(first_grad, unit, factor, vectors[4:5, :])

    packed[1, :, 1408:1536] = (tail_ref[...] + sums[...].T).astype(low)
    packed[1, :, 1536:1664] = jnp.zeros((width, 128), low)
    for start in range(0, width, 256):
        rows = slice(start, start + 256)
        left = normed_one[:, rows].T
        packed[0, rows, :] = plain(left, projected_grad[:, 0:1664]).astype(low)
        packed[1, rows, 0:640] = plain(left, projected_grad[:, 1664:2304]).astype(low)
        left = mixed_ref[:, :, rows].reshape(images * padded, 256).T
        packed[1, rows, 640:1408] = plain(left, mixer_in[...]).astype(low)
        send_core(start).start()
    order = [k for k in (2, 1, 3) if k < lines] + [0] if lines == 4 else [0]
    for start in range(0, width, 256):
        send_core(start).wait()
    for k in order:
        for j in range(1, ways):
            rows = strip_rows(k, j)
            packed[half, rows, :] = (
                packed[half, rows, :].astype(jnp.float32) + core_in[rows, :].astype(jnp.float32)
            ).astype(low)
            send_way(k, j).start()
    own_results.wait()
    for k in range(1, GROUP):
        send_back(k).wait()

    @pl.loop(0, images - 2)
    def _(i):
        result(i)

    for k in order:
        rows = strip_rows(k, 0)
        total = packed[half, rows, :].astype(jnp.float32) + core_in[rows, :].astype(jnp.float32)
        for j in range(1, ways):
            send_way(k, j).wait_recv()
            total = total + way_in[k, j - 1].astype(jnp.float32)
        packed[half, rows, :] = total.astype(low)
        if k:
            send_line(k).start()

    @pl.loop(images - 2, images)
    def _(i):
        result(i)

    total = packed[half, strip_rows(0, 0), :].astype(jnp.float32)
    for k in order[:-1]:
        send_line(k).wait_recv()
        total = total + line_in[k - 1].astype(jnp.float32)
    copy_in[rep // 2] = total.astype(low)
    for m in range(1, pairs):
        send_copy(m).start()
    for m in range(1, pairs):
        send_copy(m).wait()
    total = copy_in[0].astype(jnp.float32)
    for m in range(1, pairs):
        total = total + copy_in[m].astype(jnp.float32)
    done[half] = total.astype(low)
    send_done.start()
    send_done.wait()
    reduced_ref[...] = done[...]
    for k in order:
        for j in range(1, ways):
            send_way(k, j).wait_send()
        if k:
            send_line(k).wait_send()


def run_backward(lines, ways, copies, tokens, *rest):
    images, padded, width = tokens.shape
    low = jnp.bfloat16
    local = pl.BlockSpec(memory_space=pltpu.VMEM)
    rows = images * padded
    strip = width // (lines * ways)
    dma = pltpu.SemaphoreType.DMA
    return pl.pallas_call(
        functools.partial(backward_kernel, lines, ways, copies),
        name="attention_backward",
        out_shape=[
            jax.ShapeDtypeStruct((images, padded, width), jnp.float32),
            jax.ShapeDtypeStruct((2, strip, 1664), low),
            jax.ShapeDtypeStruct((images, padded, width), jnp.float32),
        ],
        in_specs=[local] * 9 + [pl.BlockSpec(memory_space=pl.ANY)],
        out_specs=[local] * 3,
        scratch_shapes=[
            pltpu.VMEM((128, width), jnp.float32),
            pltpu.VMEM((128, width), jnp.float32),
            pltpu.VMEM((rows, 3 * width), low),
            pltpu.VMEM((rows, width), low),
            pltpu.VMEM((rows, width), low),
            pltpu.VMEM((padded, width), low),
            pltpu.VMEM((2, width, 1664), low),
            pltpu.VMEM((width, 1664), low),
            pltpu.VMEM((lines, ways - 1, strip, 1664), low),
            pltpu.VMEM((lines - 1, strip, 1664), low),
            pltpu.VMEM((copies // 2, strip, 1664), low),
            pltpu.VMEM((2, strip, 1664), low),
            pltpu.VMEM((GROUP * SLOTS, width), low),
            dma((2, 4)),
            dma((2, lines, ways)),
            dma((2, lines)),
            dma((2, copies // 2)),
            dma((2, GROUP)),
            dma((1,)),
        ],
        compiler_params=pltpu.CompilerParams(
            vmem_limit_bytes=63 * 2**20, collective_id=3, has_side_effects=True
        ),
        cost_estimate=pl.CostEstimate(
            flops=60 * images * padded * width * width,
            bytes_accessed=40 * 2**20,
            transcendentals=images * HEADS * padded * padded,
        ),
    )(tokens, *rest)


def dispatch_kernel(slot_ref, rows_ref, rows_out):
    low = jnp.bfloat16
    for k in range(GROUP):
        slot = lax.broadcasted_iota(jnp.int32, (SLOTS, slot_ref.shape[2]), 0)
        seats = (slot == slot_ref[k]).astype(low)
        rows_out[k] = plain(seats, rows_ref[...].astype(low)).astype(low)


def run_dispatch(slot_of, rows):
    token_count, width = rows.shape
    local = pl.BlockSpec(memory_space=pltpu.VMEM)
    return pl.pallas_call(
        dispatch_kernel,
        name="dispatch_gradient",
        out_shape=jax.ShapeDtypeStruct((GROUP, SLOTS, width), jnp.bfloat16),
        in_specs=[local] * 2,
        out_specs=local,
        compiler_params=pltpu.CompilerParams(vmem_limit_bytes=48 * 2**20),
        cost_estimate=pl.CostEstimate(
            flops=2 * GROUP * SLOTS * token_count * width,
            bytes_accessed=8 * 2**20,
            transcendentals=0,
        ),
    )(slot_of, rows)


def seats_of(slot_ref, k):
    slot = lax.broadcasted_iota(jnp.int32, (slot_ref.shape[0], SLOTS), 1)
    return slot == slot_ref[:, k : k + 1]


def combine_kernel(slot_ref, grad_row_ref, grads_ref, normed_ref, probs_ref):
    normed = jnp.zeros(normed_ref.shape, jnp.float32)
    for k in range(GROUP):
        seated = seats_of(slot_ref, k)
        rows = slice(k * SLOTS, (k + 1) * SLOTS)
        normed = normed + plain(seated.astype(jnp.bfloat16), grads_ref[rows, :])
        probs_ref[:, k : k + 1] = jnp.sum(
            jnp.where(seated, grad_row_ref[k], 0.0), axis=1, keepdims=True
        )
    normed_ref[...] = normed


def run_combine(slot_of, grad_rows, grads):
    token_count, width = slot_of.shape[0], grads.shape[1]
    local = pl.BlockSpec(memory_space=pltpu.VMEM)
    return pl.pallas_call(
        combine_kernel,
        name="combine_gradient",
        out_shape=[
            jax.ShapeDtypeStruct((token_count, width), jnp.float32),
            jax.ShapeDtypeStruct((token_count, GROUP), jnp.float32),
        ],
        in_specs=[local] * 3,
        out_specs=[local] * 2,
        compiler_params=pltpu.CompilerParams(vmem_limit_bytes=56 * 2**20),
        cost_estimate=pl.CostEstimate(
            flops=2 * GROUP * SLOTS * token_count * width,
            bytes_accessed=10 * 2**20,
            transcendentals=0,
        ),
    )(slot_of, grad_rows, grads)


def slot_table(routes, chosen):
    token_count = routes.shape[0]
    hits = (routes[:, :, None] == chosen[None, None, :]).any(axis=1)
    rows = lax.broadcasted_iota(jnp.int32, (token_count, token_count), 0)
    columns = lax.broadcasted_iota(jnp.int32, (token_count, token_count), 1)
    earlier = jnp.dot(
        (columns < rows).astype(jnp.bfloat16),
        hits.astype(jnp.bfloat16),
        preferred_element_type=jnp.float32,
    ).astype(jnp.int32)
    return jnp.where(hits, earlier, -1)


def group_shift(value, copies, along):
    pairs = [
        (copy, copy // GROUP * GROUP + (copy % GROUP + along) % GROUP) for copy in range(copies)
    ]
    return lax.ppermute(value, "rep", pairs)


def exchange(blocks, copies):
    return [blocks[0]] + [group_shift(blocks[k], copies, k) for k in range(1, GROUP)]


def exchange_back(blocks, copies):
    return [blocks[0]] + [group_shift(blocks[k], copies, -k) for k in range(1, GROUP)]


def shards(
    tokens_in,
    routes,
    first_gain,
    first_shift,
    joint_weight,
    joint_bias,
    mixer_weight,
    mixer_bias,
    second_gain,
    second_shift,
    router_weight,
    expert_up,
    upward_bias,
    expert_down,
    downward_bias,
    out_grad,
    *,
    groups,
    copies,
):
    row_count, width = tokens_in.shape
    experts, _, part = expert_up.shape
    strip = first_gain.shape[0]
    hidden_width = part * groups
    images = row_count // SEQ
    token_count = images * PADDED

    def widen(rows, fill=0):
        rows = rows.reshape(images, SEQ, rows.shape[1])
        return jnp.pad(rows, ((0, 0), (0, PADDED - SEQ), (0, 0)), constant_values=fill)

    def narrow(rows):
        return rows.reshape(images, PADDED, width)[:, :SEQ].reshape(row_count, width)

    token_images = widen(tokens_in)
    out_grad = widen(out_grad).reshape(token_count, width)
    routes = widen(routes, -1).reshape(token_count, 2)
    low = jnp.bfloat16
    bias_columns = experts * part // strip

    packed = jnp.concatenate(
        [
            joint_weight,
            mixer_weight,
            router_weight,
            first_gain[:, None],
            first_shift[:, None],
            joint_bias.T,
            mixer_bias[:, None],
            second_gain[:, None],
            second_shift[:, None],
            downward_bias.T,
            upward_bias.reshape(strip, bias_columns),
        ],
        axis=1,
    )
    used = packed.shape[1]
    packed_width = 2 * 1664
    packed = jnp.pad(packed, ((0, 0), (0, packed_width - used)))
    packed = packed.reshape(strip, 2, packed_width // 2).transpose(1, 0, 2)
    lines = 4 if groups % 4 == 0 else 1
    ways = groups // lines
    me = lax.axis_index("rep") % GROUP
    shard = lax.axis_index("shard")
    mine = jnp.stack(
        [
            lax.dynamic_index_in_dim(expert_up, me, 0, keepdims=False),
            lax.dynamic_index_in_dim(expert_down, me, 0, keepdims=False).T,
        ]
    )
    near_experts = (me + jnp.arange(GROUP, dtype=jnp.int32)) % GROUP
    slot_of = slot_table(routes, near_experts)
    slot_lines = slot_of.T[:, None, :]
    grad_slots = run_dispatch(slot_lines, out_grad)
    projected, mixed, residual_one, normed_two, logits, full, rows_in, grad_in, pieces = run_forward(
        token_images, slot_lines, packed, mine, grad_slots, lines, ways, copies
    )
    projected = projected.reshape(token_count, 3 * width)
    mixed = mixed.reshape(token_count, width)
    residual_one = residual_one.reshape(token_count, width)
    normed_two = normed_two.reshape(token_count, width)
    logits = logits.reshape(token_count, -1)[:, :experts]
    near_shards = jnp.stack(
        [
            (shard // ways + k) % lines * ways + (shard % ways + j) % ways
            for k in range(lines)
            for j in range(ways)
        ]
    )
    tail = full[1, :, 1408:1536]
    router_full = tail[:, :experts]
    down_shift = tail[:, experts + 7 : 2 * experts + 7].astype(jnp.float32).T
    up_shift = (
        tail[:, 2 * experts + 7 : 2 * experts + 7 + bias_columns]
        .reshape(groups, experts, part)
        .astype(jnp.float32)
    )
    up_shift = lax.dynamic_index_in_dim(up_shift, me, 1, keepdims=False)[near_shards]
    up_shift = up_shift.reshape(lines, 1, ways * part)
    down_shift = lax.dynamic_index_in_dim(down_shift, me, 0, keepdims=True)
    router_probs = jax.nn.softmax(logits, axis=-1)

    probs_near = router_probs[:, near_experts]
    seated = slot_lines == jnp.arange(SLOTS, dtype=jnp.int32)[None, :, None]
    gate_slots = jnp.sum(jnp.where(seated, probs_near.T[:, None, :], 0.0), axis=-1)
    gate_in = jnp.concatenate(exchange(gate_slots, copies), axis=0)[:, None]
    if part % 128:
        joined = [[jnp.concatenate(line, axis=2)] for line in pieces]
    else:
        joined = pieces
    weighted, dispatched_grad, gate_grad, up_shift_grad, down_shift_grad, up, down = run_expert(
        rows_in, grad_in, gate_in, up_shift, down_shift, joined, ways, part
    )
    def from_group(value):
        every = lax.all_gather(value, "rep", axis=0)
        if copies == GROUP:
            return every.astype(jnp.float32)
        return every.astype(jnp.float32).reshape((-1, GROUP) + value.shape).sum(axis=0)

    up_grad = from_group(up)
    down_grad = from_group(down)

    gate_grad = jnp.stack(exchange_back(gate_grad.reshape(GROUP, SLOTS), copies))
    normed_grad, probs_grad = run_combine(slot_of, gate_grad[:, None, :], dispatched_grad)
    probs_grad = probs_grad[:, (jnp.arange(GROUP, dtype=jnp.int32) - me) % GROUP]
    own = (jnp.arange(experts, dtype=jnp.int32) == me).astype(jnp.float32)[:, None]
    down_shift_grad = own * down_shift_grad
    up_shift_grad = jnp.zeros((groups, part), jnp.float32).at[near_shards].set(
        up_shift_grad.reshape(groups, part)
    )
    up_shift_grad = own * up_shift_grad.reshape(1, hidden_width)
    logit_grad = (
        router_probs * (probs_grad - jnp.sum(router_probs * probs_grad, axis=-1, keepdims=True))
    ).astype(low)
    router_grad = contract_first(normed_two, logit_grad)
    normed_grad = normed_grad + contract_last(logit_grad, router_full)
    tail_grad = jnp.concatenate(
        [
            router_grad,
            jnp.zeros((width, 7), jnp.float32),
            down_shift_grad.T,
            up_shift_grad.reshape(experts, groups, part)
            .transpose(1, 0, 2)
            .reshape(groups * strip, bias_columns),
        ],
        axis=1,
    )
    tail_grad = jnp.pad(tail_grad, ((0, 0), (0, 4 * width + 128 - used)))

    def by_image(rows):
        return rows.reshape(images, PADDED, rows.shape[1])

    input_grad, reduced, block_out = run_backward(
        lines,
        ways,
        copies,
        token_images,
        by_image(out_grad),
        by_image(residual_one),
        by_image(normed_grad),
        by_image(mixed),
        by_image(projected),
        tail_grad,
        full,
        slot_of,
        weighted,
    )
    packed_grad = reduced.astype(jnp.float32).transpose(1, 0, 2).reshape(strip, packed_width)
    end = packed_grad[:, 4 * width :]
    line = end[:, experts : experts + 7].T
    return (
        narrow(block_out),
        narrow(input_grad),
        line[0],
        line[1],
        packed_grad[:, : 3 * width],
        line[2:4],
        packed_grad[:, 3 * width : 4 * width],
        line[4],
        line[5],
        line[6],
        end[:, :experts],
        up_grad,
        end[:, 2 * experts + 7 : 2 * experts + 7 + bias_columns].reshape(experts, part),
        down_grad,
        end[:, experts + 7 : 2 * experts + 7].T,
    )


def solution(mesh):
    placed = (
        P(("shard", "rep"), None),
        P(("shard", "rep"), None),
        P("shard"),
        P("shard"),
        P("shard", None),
        P(None, "shard"),
        P("shard", None),
        P("shard"),
        P("shard"),
        P("shard"),
        P("shard", None),
        P(None, None, "shard"),
        P(None, "shard"),
        P(None, "shard", None),
        P(None, "shard"),
        P(("shard", "rep"), None),
    )
    return jax.shard_map(
        functools.partial(
            shards, groups=mesh.shape["shard"], copies=mesh.shape["rep"]
        ),
        mesh=mesh,
        in_specs=placed,
        out_specs=(
            P(("shard", "rep"), None),
            P(("shard", "rep"), None),
            P("shard"),
            P("shard"),
            P("shard", None),
            P(None, "shard"),
            P("shard", None),
            P("shard"),
            P("shard"),
            P("shard"),
            P("shard", None),
            P(None, None, "shard"),
            P(None, "shard"),
            P(None, "shard", None),
            P(None, "shard"),
        ),
        check_vma=False,
    )
```

```python
import functools

import jax
import jax.numpy as jnp
from jax import lax
from jax.experimental import pallas as pl
from jax.experimental.pallas import tpu as pltpu
from jax.sharding import PartitionSpec as P

HEADS = 12
HEAD_DIM = 64
SEQ = 197
SLOTS = 624
PADDED = 208
GROUP = 4


epsilon = 1e-06


def layer_norm(values, gain, shift):
    centre = jnp.mean(values, axis=-1, keepdims=True)
    centred = values - centre
    spread = jnp.mean(centred * centred, axis=-1, keepdims=True)
    factor = lax.rsqrt(spread + epsilon)
    unit_rows = centred * factor
    return (unit_rows * gain + shift, unit_rows, factor)


def norm_back(upstream, unit_rows, factor, gain):
    scaled = upstream * gain
    middle = jnp.mean(scaled, axis=-1, keepdims=True)
    along = jnp.mean(scaled * unit_rows, axis=-1, keepdims=True)
    return factor * (scaled - middle - unit_rows * along)


def contract_first(left_rows, right_rows):
    return lax.dot_general(
        left_rows, right_rows, (((0,), (0,)), ((), ())), preferred_element_type=jnp.float32
    )


def contract_last(left_rows, right_rows):
    return lax.dot_general(
        left_rows, right_rows, (((1,), (1,)), ((), ())), preferred_element_type=jnp.float32
    )


def transposed(left_rows, right_rows):
    return lax.dot_general(
        left_rows, right_rows, (((1,), (1,)), ((), ())), preferred_element_type=jnp.float32
    )


def plain(left_rows, right_rows):
    return jnp.dot(left_rows, right_rows, preferred_element_type=jnp.float32)


def normal_parts(hidden):
    bell = jnp.exp(-0.5 * hidden * hidden)
    near = 1.0 / (1.0 + (0.3275911 * 0.7071067811865476) * jnp.abs(hidden))
    tail = near * (
        0.127414796
        + near * (-0.142248368 + near * (0.7107068705 + near * (-0.7265760135 + near * 0.5307027145)))
    )
    tail = tail * bell
    return jnp.where(hidden < 0.0, tail, 1.0 - tail), bell * 0.3989422804014327


def expert_kernel(order, joined, ways, *refs):
    low = jnp.bfloat16
    x_ref, g_ref, gate_ref, up_shift_ref, down_shift_ref = refs[:5]
    refs = refs[5:]
    steps = len(order)
    pieces = [refs[k * joined : (k + 1) * joined] for k in range(steps)]
    refs = refs[steps * joined :]
    out_ref, dx_ref, gate_grad_ref, up_shift_grad_ref, down_shift_grad_ref = refs[:5]
    up_ref, down_ref, own_ref, way_ref, line_ref = refs[5:10]
    refs = refs[10:]
    rg, xt, rgt, act, hg, y_sum, dx_sum, weights, grad_buf, stage = refs[:10]
    in_sem, own_sem, stage_sem, end_sem, way_sem, line_sem, back_sem = refs[10:]
    rows, width = x_ref.shape
    part = up_ref.shape[1]
    block = part * ways
    piece = block // joined
    chunk = SLOTS
    chunks = rows // chunk

    shard = lax.axis_index("shard")
    rep = lax.axis_index("rep")
    line, way = shard // ways, shard % ways
    lines = steps

    def place(k, j):
        index = lax.rem(line + k + lines, lines) * ways + lax.rem(way + j + ways, ways)
        return {"shard": index}

    def group(k):
        spot = rep % GROUP
        return {"rep": rep - spot + lax.rem(spot + k + GROUP, GROUP)}

    friends = [place(k, 0) for k in range(1, lines)] + [place(0, j) for j in range(1, ways)]
    friends += [group(k) for k in range(1, GROUP)]
    barrier = pltpu.get_barrier_semaphore()
    for friend in friends:
        pl.semaphore_signal(barrier, inc=1, device_id=friend, device_id_type=pl.DeviceIdType.MESH)

    def remote(source, target, sems, index, device):
        return pltpu.make_async_remote_copy(
            src_ref=source,
            dst_ref=target,
            send_sem=sems.at[(0,) + index],
            recv_sem=sems.at[(1,) + index],
            device_id=device,
            device_id_type=pl.DeviceIdType.MESH,
        )

    def load(step):
        return [
            pltpu.make_async_copy(
                pieces[order[step]][j],
                weights.at[step % 2, :, :, pl.ds(j * piece, piece)],
                in_sem.at[step % 2, j],
            )
            for j in range(joined)
        ]

    def keep(step):
        return pltpu.make_async_copy(grad_buf.at[0], own_ref.at[step], own_sem.at[0])

    def send_way(step, j):
        return remote(grad_buf.at[j], way_ref.at[step, j - 1], way_sem, (step, j), place(0, j))

    def send_line(step):
        k = order[step]
        return remote(own_ref.at[step], line_ref.at[k - 1], line_sem, (k,), place(k, 0))

    def fetch(source, slot):
        return pltpu.make_async_copy(source, stage.at[slot], stage_sem.at[slot])

    def add_ways(step):
        copies = [fetch(own_ref.at[step], 0)]
        for j in range(1, ways):
            send_way(step, j).wait_recv()
            copies.append(fetch(way_ref.at[step, j - 1], j))
        for copy in copies:
            copy.start()
        for copy in copies:
            copy.wait()

        @pl.loop(0, width // 256)
        def _(c):
            span = pl.ds(pl.multiple_of(c * 256, 256), 256)
            for u in range(2):
                total = stage[0, u, span, :].astype(jnp.float32)
                for j in range(1, ways):
                    total = total + stage[j, u, span, :].astype(jnp.float32)
                stage[0, u, span, :] = total.astype(low)

    def finish(step):
        add_ways(step)
        write = pltpu.make_async_copy(stage.at[0], own_ref.at[step], own_sem.at[1])
        write.start()
        write.wait()
        send_line(step).start()

    def send_back(k):
        block_rows = pl.ds(k * chunk, chunk)
        return remote(
            hg.at[block_rows, pl.ds(0, width)],
            dx_ref.at[block_rows, :],
            back_sem,
            (k,),
            group(-k),
        )

    for copy in load(0):
        copy.start()

    down_shift_grad_ref[...] = jnp.zeros_like(down_shift_grad_ref)

    @pl.loop(0, chunks)
    def _(c):
        span = pl.ds(pl.multiple_of(c * chunk, chunk), chunk)
        scaled = (g_ref[span, :].astype(jnp.float32) * gate_ref[span, :]).astype(low)
        rg[span, :] = scaled
        down_shift_grad_ref[...] += jnp.sum(scaled.astype(jnp.float32), axis=0, keepdims=True)
        y_sum[span, :] = jnp.zeros((chunk, width), jnp.float32)
        dx_sum[span, :] = jnp.zeros((chunk, width), jnp.float32)

    for start in range(0, width, 256):
        xt[start : start + 256, :] = x_ref[:, start : start + 256].T
        rgt[start : start + 256, :] = rg[:, start : start + 256].T

    for step in range(steps):
        for copy in load(step):
            copy.wait()
        if step + 1 < steps:
            for copy in load(step + 1):
                copy.start()
        slot = step % 2
        up_shift_grad_ref[step] = jnp.zeros((1, block), jnp.float32)

        @pl.loop(0, chunks)
        def _(c):
            span = pl.ds(pl.multiple_of(c * chunk, chunk), chunk)
            x_rows = x_ref[span, :]
            g_rows = rg[span, :]
            for start in range(0, block, 256):
                part_span = slice(start, start + 256)
                hidden = plain(x_rows, weights[slot, 0, :, part_span]) + up_shift_ref[step, :, part_span]
                back = plain(g_rows, weights[slot, 1, :, part_span])
                cdf, density = normal_parts(hidden)
                act[span, part_span] = (hidden * cdf).astype(low)
                hidden_grad = (back * (cdf + hidden * density)).astype(low)
                hg[span, part_span] = hidden_grad
                up_shift_grad_ref[step, :, part_span] += jnp.sum(
                    hidden_grad.astype(jnp.float32), axis=0, keepdims=True
                )
            y_sum[span, :] += transposed(act[span, :], weights[slot, 1])
            dx_sum[span, :] += transposed(hg[span, :], weights[slot, 0])

        if step == 0:
            pl.semaphore_wait(barrier, len(friends))
        else:
            keep(step - 1).wait()
            for j in range(1, ways):
                send_way(step - 1, j).wait_send()

        @pl.loop(0, width // 256)
        def _(c):
            span = pl.ds(pl.multiple_of(c * 256, 256), 256)
            for u, found in enumerate((plain(xt[span, :], hg[...]), plain(rgt[span, :], act[...]))):
                for j in range(ways):
                    grad_buf[j, u, span, :] = found[:, j * part : (j + 1) * part].astype(low)

        keep(step).start()
        for j in range(1, ways):
            send_way(step, j).start()
        if step > 0:
            finish(step - 1)

    @pl.loop(0, chunks)
    def _(c):
        span = pl.ds(pl.multiple_of(c * chunk, chunk), chunk)
        hg[span, :width] = dx_sum[span, :].astype(low)
        result = y_sum[span, :] + down_shift_ref[...]
        act[span, :width] = (result * gate_ref[span, :]).astype(low)
        gate_grad_ref[span, :] = jnp.sum(
            result * g_ref[span, :].astype(jnp.float32), axis=1, keepdims=True
        )

    home = pl.ds(0, chunk)
    ends = [
        pltpu.make_async_copy(hg.at[home, pl.ds(0, width)], dx_ref.at[home, :], end_sem.at[0]),
        pltpu.make_async_copy(act.at[:, pl.ds(0, width)], out_ref, end_sem.at[1]),
    ]
    for k in range(1, GROUP):
        send_back(k).start()
    for copy in ends:
        copy.start()

    last = steps - 1
    keep(last).wait()
    add_ways(last)
    for k in sorted(order[:-1], key=order.index):
        send_line(order.index(k)).wait_recv()
        copy = fetch(line_ref.at[k - 1], 1)
        copy.start()
        copy.wait()
        first, final = k == order[0], k == order[-2]

        @pl.loop(0, width // 256)
        def _(c):
            span = pl.ds(pl.multiple_of(c * 256, 256), 256)
            for u in range(2):
                sums = pl.ds(pl.multiple_of(u * width + c * 256, 256), 256)
                total = stage[1, u, span, :].astype(jnp.float32)
                if first:
                    total = total + stage[0, u, span, :].astype(jnp.float32)
                else:
                    total = total + y_sum[sums, 0:part]
                if final:
                    stage[0, u, span, :] = total.astype(low)
                else:
                    y_sum[sums, 0:part] = total

    up_ref[...] = stage[0, 0]
    down_ref[...] = stage[0, 1].astype(jnp.float32).T.astype(low)
    for j in range(1, ways):
        send_way(last, j).wait_send()
    for step in range(last):
        send_line(step).wait_send()
    for k in range(1, GROUP):
        send_back(k).wait()
    for copy in ends:
        copy.wait()


def run_expert(rows_in, grad_in, gate_in, up_shift, down_shift, pieces, ways, part):
    steps, joined = len(pieces), len(pieces[0])
    order = [2, 1, 3, 0] if steps == 4 else list(range(1, steps)) + [0]
    rows, width = rows_in.shape
    block = part * ways
    low = jnp.bfloat16
    everywhere = pl.BlockSpec(memory_space=pl.ANY)
    local = pl.BlockSpec(memory_space=pltpu.VMEM)
    flat = [piece for line in pieces for piece in line]
    dma = pltpu.SemaphoreType.DMA
    up_shift = jnp.stack([up_shift[k] for k in order])
    outs = pl.pallas_call(
        functools.partial(expert_kernel, order, joined, ways),
        name="expert_block",
        out_shape=[
            jax.ShapeDtypeStruct((rows, width), low),
            jax.ShapeDtypeStruct((rows, width), low),
            jax.ShapeDtypeStruct((rows, 1), jnp.float32),
            jax.ShapeDtypeStruct((steps, 1, block), jnp.float32),
            jax.ShapeDtypeStruct((1, width), jnp.float32),
            jax.ShapeDtypeStruct((width, part), low),
            jax.ShapeDtypeStruct((part, width), low),
            jax.ShapeDtypeStruct((steps, 2, width, part), low),
            jax.ShapeDtypeStruct((steps, ways - 1, 2, width, part), low),
            jax.ShapeDtypeStruct((steps - 1, 2, width, part), low),
        ],
        in_specs=[local] * 5 + [everywhere] * len(flat),
        out_specs=[everywhere, everywhere] + [local] * 5 + [everywhere] * 3,
        scratch_shapes=[
            pltpu.VMEM((rows, width), low),
            pltpu.VMEM((width, rows), low),
            pltpu.VMEM((width, rows), low),
            pltpu.VMEM((rows, block), low),
            pltpu.VMEM((rows, block), low),
            pltpu.VMEM((rows, width), jnp.float32),
            pltpu.VMEM((rows, width), jnp.float32),
            pltpu.VMEM((2, 2, width, block), low),
            pltpu.VMEM((ways, 2, width, part), low),
            pltpu.VMEM((ways, 2, width, part), low),
            dma((2, joined)),
            dma((2,)),
            dma((ways,)),
            dma((2,)),
            dma((2, steps, ways)),
            dma((2, steps)),
            dma((2, GROUP)),
        ],
        compiler_params=pltpu.CompilerParams(
            vmem_limit_bytes=63 * 2**20, collective_id=2, has_side_effects=True
        ),
        cost_estimate=pl.CostEstimate(
            flops=12 * rows * width * block * steps,
            bytes_accessed=12 * rows * width + 8 * width * block * steps,
            transcendentals=rows * block * steps,
        ),
    )(rows_in, grad_in, gate_in, up_shift, down_shift, *flat)
    weighted, dispatched_grad, gate_grad, up_shift_grad, down_shift_grad, up, down = outs[:7]
    up_shift_grad = jnp.stack([up_shift_grad[order.index(k)] for k in range(steps)])
    return weighted, dispatched_grad, gate_grad, up_shift_grad, down_shift_grad, up, down


def side_by_side(first, second):
    lane = lax.broadcasted_iota(jnp.int32, first.shape, 1)
    return jnp.where(lane < HEAD_DIM, first, second)


def head_of(pair, which):
    lane = lax.broadcasted_iota(jnp.int32, pair.shape, 1)
    keep = lane < HEAD_DIM if which == 0 else lane >= HEAD_DIM
    return jnp.where(keep, pair, jnp.zeros_like(pair))


def key_probs(query_pair, key_pair, which):
    scores = transposed(head_of(query_pair, which), key_pair) * HEAD_DIM ** (-0.5)
    column = lax.broadcasted_iota(jnp.int32, scores.shape, 1)
    scores = jnp.where(column < SEQ, scores, -1e30)
    raised = jnp.exp(scores - jnp.max(scores, axis=-1, keepdims=True))
    return raised * (1.0 / jnp.sum(raised, axis=-1, keepdims=True))


def forward_kernel(lines, ways, copies, *refs):
    low = jnp.bfloat16
    tokens_ref, slot_ref, packed_ref, mine_ref, grad_slots_ref = refs[:5]
    refs = refs[5:]
    projected_ref, mixed_ref, residual_ref, normed_ref, logits_ref, weights_out = refs[:6]
    rows_in_ref, grad_in_ref = refs[6:8]
    refs = refs[8:]
    pieces = [refs[k * ways : (k + 1) * ways] for k in range(lines)]
    refs = refs[lines * ways :]
    full, vectors, rows_out = refs[:3]
    own_sem, save_sem = refs[3:5]
    line_sem, way_sem, core_sem, piece_line_sem, piece_way_sem, token_sem = refs[5:]

    images, padded, width = tokens_ref.shape
    strip = packed_ref.shape[1]
    shard = lax.axis_index("shard")
    rep = lax.axis_index("rep")
    line, way = shard // ways, shard % ways
    half = rep % 2

    def place(k, j):
        return lax.rem(line + k + lines, lines) * ways + lax.rem(way + j + ways, ways)

    def at_shard(index):
        return {"shard": index}

    def group(k):
        spot = rep % GROUP
        return {"rep": rep - spot + lax.rem(spot + k, GROUP)}

    partner = {"rep": rep + 1 - 2 * half}
    friends = [at_shard(place(k, 0)) for k in range(1, lines)]
    friends += [at_shard(place(0, j)) for j in range(1, ways)]
    friends += [group(k) for k in range(1, GROUP)]
    barrier = pltpu.get_barrier_semaphore()
    for friend in friends:
        pl.semaphore_signal(barrier, inc=1, device_id=friend, device_id_type=pl.DeviceIdType.MESH)
    pl.semaphore_wait(barrier, len(friends))

    def remote(source, target, sems, index, device):
        return pltpu.make_async_remote_copy(
            src_ref=source,
            dst_ref=target,
            send_sem=sems.at[(0,) + index],
            recv_sem=sems.at[(1,) + index],
            device_id=device,
            device_id_type=pl.DeviceIdType.MESH,
        )

    def strip_of(k, j, side):
        rows = pl.ds(pl.multiple_of(place(k, j) * strip, strip), strip)
        return full.at[side, rows, :]

    def strip_line(k):
        return remote(packed_ref.at[half], strip_of(0, 0, half), line_sem, (k,), at_shard(place(-k, 0)))

    def strip_way(k, j):
        source = packed_ref.at[half] if k == 0 else strip_of(k, 0, half)
        return remote(source, strip_of(k, 0, half), way_sem, (k, j), at_shard(place(0, -j)))

    def strip_core(k, j):
        return remote(strip_of(k, j, half), strip_of(k, j, half), core_sem, (k, j), partner)

    def piece_line(k, u):
        return remote(
            mine_ref.at[u], pieces[k][0].at[u], piece_line_sem, (k, u), at_shard(place(-k, 0))
        )

    def piece_way(k, j, u):
        source = mine_ref.at[u] if k == 0 else pieces[k][0].at[u]
        return remote(source, pieces[k][j].at[u], piece_way_sem, (k, j, u), at_shard(place(0, -j)))

    def block_of(ref, k):
        return ref.at[pl.ds(k * SLOTS, SLOTS), :]

    def send_grad(k):
        return remote(grad_slots_ref.at[k], block_of(grad_in_ref, k), token_sem, (0, k), group(k))

    def send_rows(k):
        return remote(rows_out.at[k], block_of(rows_in_ref, k), token_sem, (1, k), group(k))

    own_grad = pltpu.make_async_copy(grad_slots_ref.at[0], block_of(grad_in_ref, 0), own_sem.at[2])
    own_rows = pltpu.make_async_copy(rows_out.at[0], block_of(rows_in_ref, 0), own_sem.at[3])
    own = pltpu.make_async_copy(
        packed_ref, full.at[:, pl.ds(pl.multiple_of(shard * strip, strip), strip), :], own_sem.at[0]
    )
    own_piece = pltpu.make_async_copy(mine_ref, pieces[0][0], own_sem.at[1])
    order = [k for k in (1, lines - 1, 2) if 0 < k < lines]
    order = list(dict.fromkeys(order))
    own.start()
    for k in order:
        strip_line(k).start()
    for j in range(1, ways):
        strip_way(0, j).start()
    own_piece.start()
    for j in range(1, ways):
        strip_way(0, j).wait_recv()
        strip_core(0, j).start()
    for k in order:
        strip_line(k).wait_recv()
        for j in range(1, ways):
            strip_way(k, j).start()
        strip_core(k, 0).start()
    for u in range(2):
        for k in order:
            piece_line(k, u).start()
        for j in range(1, ways):
            piece_way(0, j, u).start()
    for k in order:
        for j in range(1, ways):
            strip_way(k, j).wait_recv()
            strip_core(k, j).start()
    own_grad.start()
    for k in (2, 1, 3):
        send_grad(k).start()
    for k in range(lines):
        for j in range(ways):
            if k or j:
                strip_core(k, j).wait_recv()
    own.wait()
    save = pltpu.make_async_copy(full, weights_out, save_sem.at[0])
    save.start()

    vectors[...] = full[1, :, 1408:1536].astype(jnp.float32).T

    def pass_on(k, u):
        piece_line(k, u).wait_recv()
        for j in range(1, ways):
            piece_way(k, j, u).start()

    events = [(k, u) for u in range(2) for k in order]

    @pl.loop(0, images)
    def _(i):
        rows = tokens_ref[i]
        normed, _, _ = layer_norm(rows, vectors[4:5, :], vectors[5:6, :])
        normed = normed.astype(low)
        left = plain(normed, full[0])
        projected_ref[i, :, 0:768] = (left[:, 0:768] + vectors[6:7, :]).astype(low)
        projected_ref[i, :, 768:1536] = left[:, 768:1536].astype(low)
        right = plain(normed, full[1, :, 0:640])
        projected_ref[i, :, 1536:1664] = (left[:, 1536:1664] + vectors[7:8, 0:128]).astype(low)
        projected_ref[i, :, 1664:2304] = (right + vectors[7:8, 128:768]).astype(low)
        for pair in range(HEADS // 2):
            start = 128 * pair
            query_pair = projected_ref[i, :, start : start + 128]
            key_pair = projected_ref[i, :, 768 + start : 896 + start]
            value_pair = projected_ref[i, :, 1536 + start : 1664 + start]
            parts = [
                plain(key_probs(query_pair, key_pair, which).astype(low), value_pair)
                for which in (0, 1)
            ]
            mixed_ref[i, :, start : start + 128] = side_by_side(*parts).astype(low)
        residual = rows + (plain(mixed_ref[i], full[1, :, 640:1408]) + vectors[8:9, :])
        residual_ref[i] = residual
        normed_two, _, _ = layer_norm(residual, vectors[9:10, :], vectors[10:11, :])
        normed_two = normed_two.astype(low)
        normed_ref[i] = normed_two
        logits_ref[i] = plain(normed_two, full[1, :, 1408:1536])

        for number, event in enumerate(events[:2]):

            @pl.when(i == 2 * number + 1)
            def _():
                pass_on(*event)

    done = min(2, len(events)) if images >= 4 else 0
    for event in events[done : done + 1]:
        pass_on(*event)
    token_count = images * padded
    for k in (2, 1, 3, 0):
        slot = lax.broadcasted_iota(jnp.int32, (SLOTS, token_count), 0)
        seats = (slot == slot_ref[k]).astype(low)
        rows_out[k] = plain(seats, normed_ref[...].reshape(token_count, width)).astype(low)
        if k:
            send_rows(k).start()
    own_rows.start()
    for event in events[done + 1 :]:
        pass_on(*event)
    for u in range(2):
        for k in range(lines):
            for j in range(1, ways):
                piece_way(k, j, u).wait_recv()
    for k in range(1, GROUP):
        send_grad(k).wait()
        send_rows(k).wait()
    own_grad.wait()
    own_rows.wait()
    save.wait()
    own_piece.wait()
    for k in order:
        strip_line(k).wait_send()
        for u in range(2):
            piece_line(k, u).wait_send()
    for k in range(lines):
        for j in range(ways):
            if k or j:
                strip_core(k, j).wait_send()
            if j:
                strip_way(k, j).wait_send()
                for u in range(2):
                    piece_way(k, j, u).wait_send()


def run_forward(tokens, slot_lines, packed, mine, grad_slots, lines, ways, copies):
    images, padded, width = tokens.shape
    low = jnp.bfloat16
    everywhere = pl.BlockSpec(memory_space=pl.ANY)
    local = pl.BlockSpec(memory_space=pltpu.VMEM)
    half_width = packed.shape[2]
    dma = pltpu.SemaphoreType.DMA
    outs = pl.pallas_call(
        functools.partial(forward_kernel, lines, ways, copies),
        name="attention_forward",
        out_shape=[
            jax.ShapeDtypeStruct((images, padded, 3 * width), low),
            jax.ShapeDtypeStruct((images, padded, width), low),
            jax.ShapeDtypeStruct((images, padded, width), jnp.float32),
            jax.ShapeDtypeStruct((images, padded, width), low),
            jax.ShapeDtypeStruct((images, padded, 128), jnp.float32),
            jax.ShapeDtypeStruct((2, width, half_width), low),
            jax.ShapeDtypeStruct((GROUP * SLOTS, width), low),
            jax.ShapeDtypeStruct((GROUP * SLOTS, width), low),
        ]
        + [jax.ShapeDtypeStruct(mine.shape, low) for _ in range(lines * ways)],
        in_specs=[local, local, everywhere, everywhere, everywhere],
        out_specs=[local] * 5 + [everywhere] * (3 + lines * ways),
        scratch_shapes=[
            pltpu.VMEM((2, width, half_width), low),
            pltpu.VMEM((128, width), jnp.float32),
            pltpu.VMEM((GROUP, SLOTS, width), low),
            dma((4,)),
            dma((1,)),
            dma((2, lines)),
            dma((2, lines, ways)),
            dma((2, lines, ways)),
            dma((2, lines, 2)),
            dma((2, lines, ways, 2)),
            dma((2, 2, GROUP)),
        ],
        compiler_params=pltpu.CompilerParams(
            vmem_limit_bytes=60 * 2**20, collective_id=1, has_side_effects=True
        ),
        cost_estimate=pl.CostEstimate(
            flops=10 * images * padded * width * width,
            bytes_accessed=300 * 2**20,
            transcendentals=images * HEADS * padded * padded,
        ),
    )(tokens, slot_lines, packed, mine, grad_slots)
    pieces = outs[8:]
    return list(outs[:8]) + [[pieces[k * ways : (k + 1) * ways] for k in range(lines)]]


def backward_kernel(
    lines,
    ways,
    copies,
    tokens_ref,
    out_grad_ref,
    residual_ref,
    normed_grad_ref,
    mixed_ref,
    projected_ref,
    tail_ref,
    full_ref,
    slot_ref,
    results_ref,
    input_grad_ref,
    reduced_ref,
    out_ref,
    vectors,
    sums,
    projected_grad,
    mixer_in,
    normed_one,
    mixed_grad,
    packed,
    core_in,
    way_in,
    line_in,
    copy_in,
    done,
    results,
    core_sem,
    way_sem,
    line_sem,
    copy_sem,
    back_sem,
    own_sem,
):
    strip = reduced_ref.shape[1]
    shard = lax.axis_index("shard")
    rep = lax.axis_index("rep")
    line, way = shard // ways, shard % ways
    half = rep % 2
    pairs = copies // 2

    def place(k, j):
        return lax.rem(line + k + lines, lines) * ways + lax.rem(way + j + ways, ways)

    def at_shard(index):
        return {"shard": index}

    partner = {"rep": rep + 1 - 2 * half}

    def group(k):
        spot = rep % GROUP
        return {"rep": rep - spot + lax.rem(spot + k + GROUP, GROUP)}

    def next_copy(m):
        return {"rep": lax.rem(rep + 2 * m, copies)}

    friends = [at_shard(place(k, 0)) for k in range(1, lines)]
    friends += [at_shard(place(0, j)) for j in range(1, ways)]
    friends += [group(k) for k in range(1, GROUP)]
    if copies > GROUP:
        friends += [next_copy(m) for m in range(1, pairs)]
    barrier = pltpu.get_barrier_semaphore()
    for friend in friends:
        pl.semaphore_signal(barrier, inc=1, device_id=friend, device_id_type=pl.DeviceIdType.MESH)

    def remote(source, target, sems, index, device):
        return pltpu.make_async_remote_copy(
            src_ref=source,
            dst_ref=target,
            send_sem=sems.at[(0,) + index],
            recv_sem=sems.at[(1,) + index],
            device_id=device,
            device_id_type=pl.DeviceIdType.MESH,
        )

    def strip_rows(k, j):
        return pl.ds(pl.multiple_of(place(k, j) * strip, strip), strip)

    def send_core(start):
        rows = pl.ds(start, 256)
        return remote(
            packed.at[1 - half, rows, :], core_in.at[rows, :], core_sem, (start // 256,), partner
        )

    def send_way(k, j):
        return remote(
            packed.at[half, strip_rows(k, j), :],
            way_in.at[k, j - 1],
            way_sem,
            (k, j),
            at_shard(place(0, j)),
        )

    def send_line(k):
        return remote(
            packed.at[half, strip_rows(k, 0), :],
            line_in.at[k - 1],
            line_sem,
            (k,),
            at_shard(place(k, 0)),
        )

    def send_back(k):
        block_rows = pl.ds(k * SLOTS, SLOTS)
        return remote(
            results_ref.at[block_rows, :], results.at[block_rows, :], back_sem, (k,), group(-k)
        )

    home = pl.ds(0, SLOTS)
    own_results = pltpu.make_async_copy(
        results_ref.at[home, :], results.at[home, :], own_sem.at[0]
    )

    def send_copy(m):
        return remote(copy_in.at[rep // 2], copy_in.at[rep // 2], copy_sem, (m,), next_copy(m))

    send_done = remote(done.at[half], done.at[half], core_sem, (3,), partner)

    low = jnp.bfloat16
    images, padded, width = tokens_ref.shape
    vectors[...] = full_ref[1, :, 1408:1536].astype(jnp.float32).T
    sums[...] = jnp.zeros_like(sums)
    head_scale = HEAD_DIM ** (-0.5)

    pl.semaphore_wait(barrier, len(friends))
    own_results.start()
    for k in (2, 1, 3):
        send_back(k).start()

    def result(i):
        span = pl.ds(pl.multiple_of(i * padded, padded), padded)
        slots = slot_ref[span, :]
        total = residual_ref[i]
        column = lax.broadcasted_iota(jnp.int32, (padded, SLOTS), 1)
        for k in range(GROUP):
            seats = (column == slots[:, k : k + 1]).astype(low)
            total = total + plain(seats, results[k * SLOTS : (k + 1) * SLOTS, :])
        out_ref[i] = total

    def add(row, values):
        sums[row : row + 1, :] += jnp.sum(values.astype(jnp.float32), axis=0, keepdims=True)

    @pl.loop(0, images)
    def _(i):
        span = pl.ds(pl.multiple_of(i * padded, padded), padded)
        _, unit, factor = layer_norm(residual_ref[i], 1.0, 0.0)
        upstream = normed_grad_ref[i]
        add(9, upstream * unit)
        add(10, upstream)
        residual_grad = out_grad_ref[i] + norm_back(upstream, unit, factor, vectors[9:10, :])
        input_grad_ref[i] = residual_grad
        rounded = residual_grad.astype(low)
        mixer_in[span, :] = rounded
        add(8, rounded)
        mixed_grad[...] = transposed(rounded, full_ref[1, :, 640:1408]).astype(low)
        for pair in range(HEADS // 2):
            start = 128 * pair
            query_pair = projected_ref[i, :, start : start + 128]
            key_pair = projected_ref[i, :, 768 + start : 896 + start]
            value_pair = projected_ref[i, :, 1536 + start : 1664 + start]
            grad_pair = mixed_grad[:, start : start + 128]
            found = []
            for which in (0, 1):
                probs = key_probs(query_pair, key_pair, which)
                back = transposed(head_of(grad_pair, which), value_pair)
                centre = jnp.sum(probs * back, axis=-1, keepdims=True)
                score_grad = (probs * (back - centre)).astype(low)
                found.append(
                    (
                        plain(score_grad, key_pair) * head_scale,
                        contract_first(score_grad, query_pair) * head_scale,
                        contract_first(probs.astype(low), grad_pair),
                    )
                )
            for part in range(3):
                columns = slice(768 * part + start, 768 * part + start + 128)
                projected_grad[span, columns] = side_by_side(
                    found[0][part], found[1][part]
                ).astype(low)
        whole = projected_grad[span, :]
        add(6, whole[:, 0:768])
        add(7, whole[:, 1536:2304])
        first_grad = transposed(whole[:, 0:1664], full_ref[0]) + transposed(
            whole[:, 1664:2304], full_ref[1, :, 0:640]
        )
        normed, unit, factor = layer_norm(tokens_ref[i], vectors[4:5, :], vectors[5:6, :])
        normed_one[span, :] = normed.astype(low)
        add(4, first_grad * unit)
        add(5, first_grad)
        input_grad_ref[i] += norm_back(first_grad, unit, factor, vectors[4:5, :])

    packed[1, :, 1408:1536] = (tail_ref[...] + sums[...].T).astype(low)
    packed[1, :, 1536:1664] = jnp.zeros((width, 128), low)
    for start in range(0, width, 256):
        rows = slice(start, start + 256)
        left = normed_one[:, rows].T
        packed[0, rows, :] = plain(left, projected_grad[:, 0:1664]).astype(low)
        packed[1, rows, 0:640] = plain(left, projected_grad[:, 1664:2304]).astype(low)
        left = mixed_ref[:, :, rows].reshape(images * padded, 256).T
        packed[1, rows, 640:1408] = plain(left, mixer_in[...]).astype(low)
        send_core(start).start()
    order = [k for k in (2, 1, 3) if k < lines] + [0] if lines == 4 else [0]
    for start in range(0, width, 256):
        send_core(start).wait()
    for k in order:
        for j in range(1, ways):
            rows = strip_rows(k, j)
            packed[half, rows, :] = (
                packed[half, rows, :].astype(jnp.float32) + core_in[rows, :].astype(jnp.float32)
            ).astype(low)
            send_way(k, j).start()
    own_results.wait()
    for k in range(1, GROUP):
        send_back(k).wait()

    @pl.loop(0, 1)
    def _(i):
        result(i)

    for k in order:
        rows = strip_rows(k, 0)
        total = packed[half, rows, :].astype(jnp.float32) + core_in[rows, :].astype(jnp.float32)
        for j in range(1, ways):
            send_way(k, j).wait_recv()
            total = total + way_in[k, j - 1].astype(jnp.float32)
        packed[half, rows, :] = total.astype(low)
        if k:
            send_line(k).start()

    @pl.loop(1, images)
    def _(i):
        result(i)

    total = packed[half, strip_rows(0, 0), :].astype(jnp.float32)
    for k in order[:-1]:
        send_line(k).wait_recv()
        total = total + line_in[k - 1].astype(jnp.float32)
    copy_in[rep // 2] = total.astype(low)
    for m in range(1, pairs):
        send_copy(m).start()
    for m in range(1, pairs):
        send_copy(m).wait()
    total = copy_in[0].astype(jnp.float32)
    for m in range(1, pairs):
        total = total + copy_in[m].astype(jnp.float32)
    done[half] = total.astype(low)
    send_done.start()
    send_done.wait()
    reduced_ref[...] = done[...]
    for k in order:
        for j in range(1, ways):
            send_way(k, j).wait_send()
        if k:
            send_line(k).wait_send()


def run_backward(lines, ways, copies, tokens, *rest):
    images, padded, width = tokens.shape
    low = jnp.bfloat16
    local = pl.BlockSpec(memory_space=pltpu.VMEM)
    rows = images * padded
    strip = width // (lines * ways)
    dma = pltpu.SemaphoreType.DMA
    return pl.pallas_call(
        functools.partial(backward_kernel, lines, ways, copies),
        name="attention_backward",
        out_shape=[
            jax.ShapeDtypeStruct((images, padded, width), jnp.float32),
            jax.ShapeDtypeStruct((2, strip, 1664), low),
            jax.ShapeDtypeStruct((images, padded, width), jnp.float32),
        ],
        in_specs=[local] * 9 + [pl.BlockSpec(memory_space=pl.ANY)],
        out_specs=[local] * 3,
        scratch_shapes=[
            pltpu.VMEM((128, width), jnp.float32),
            pltpu.VMEM((128, width), jnp.float32),
            pltpu.VMEM((rows, 3 * width), low),
            pltpu.VMEM((rows, width), low),
            pltpu.VMEM((rows, width), low),
            pltpu.VMEM((padded, width), low),
            pltpu.VMEM((2, width, 1664), low),
            pltpu.VMEM((width, 1664), low),
            pltpu.VMEM((lines, ways - 1, strip, 1664), low),
            pltpu.VMEM((lines - 1, strip, 1664), low),
            pltpu.VMEM((copies // 2, strip, 1664), low),
            pltpu.VMEM((2, strip, 1664), low),
            pltpu.VMEM((GROUP * SLOTS, width), low),
            dma((2, 4)),
            dma((2, lines, ways)),
            dma((2, lines)),
            dma((2, copies // 2)),
            dma((2, GROUP)),
            dma((1,)),
        ],
        compiler_params=pltpu.CompilerParams(
            vmem_limit_bytes=63 * 2**20, collective_id=3, has_side_effects=True
        ),
        cost_estimate=pl.CostEstimate(
            flops=60 * images * padded * width * width,
            bytes_accessed=40 * 2**20,
            transcendentals=images * HEADS * padded * padded,
        ),
    )(tokens, *rest)


def dispatch_kernel(slot_ref, rows_ref, rows_out):
    low = jnp.bfloat16
    for k in range(GROUP):
        slot = lax.broadcasted_iota(jnp.int32, (SLOTS, slot_ref.shape[2]), 0)
        seats = (slot == slot_ref[k]).astype(low)
        rows_out[k] = plain(seats, rows_ref[...].astype(low)).astype(low)


def run_dispatch(slot_of, rows):
    token_count, width = rows.shape
    local = pl.BlockSpec(memory_space=pltpu.VMEM)
    return pl.pallas_call(
        dispatch_kernel,
        name="dispatch_gradient",
        out_shape=jax.ShapeDtypeStruct((GROUP, SLOTS, width), jnp.bfloat16),
        in_specs=[local] * 2,
        out_specs=local,
        compiler_params=pltpu.CompilerParams(vmem_limit_bytes=48 * 2**20),
        cost_estimate=pl.CostEstimate(
            flops=2 * GROUP * SLOTS * token_count * width,
            bytes_accessed=8 * 2**20,
            transcendentals=0,
        ),
    )(slot_of, rows)


def seats_of(slot_ref, k):
    slot = lax.broadcasted_iota(jnp.int32, (slot_ref.shape[0], SLOTS), 1)
    return slot == slot_ref[:, k : k + 1]


def combine_kernel(slot_ref, grad_row_ref, grads_ref, normed_ref, probs_ref):
    normed = jnp.zeros(normed_ref.shape, jnp.float32)
    for k in range(GROUP):
        seated = seats_of(slot_ref, k)
        rows = slice(k * SLOTS, (k + 1) * SLOTS)
        normed = normed + plain(seated.astype(jnp.bfloat16), grads_ref[rows, :])
        probs_ref[:, k : k + 1] = jnp.sum(
            jnp.where(seated, grad_row_ref[k], 0.0), axis=1, keepdims=True
        )
    normed_ref[...] = normed


def run_combine(slot_of, grad_rows, grads):
    token_count, width = slot_of.shape[0], grads.shape[1]
    local = pl.BlockSpec(memory_space=pltpu.VMEM)
    return pl.pallas_call(
        combine_kernel,
        name="combine_gradient",
        out_shape=[
            jax.ShapeDtypeStruct((token_count, width), jnp.float32),
            jax.ShapeDtypeStruct((token_count, GROUP), jnp.float32),
        ],
        in_specs=[local] * 3,
        out_specs=[local] * 2,
        compiler_params=pltpu.CompilerParams(vmem_limit_bytes=56 * 2**20),
        cost_estimate=pl.CostEstimate(
            flops=2 * GROUP * SLOTS * token_count * width,
            bytes_accessed=10 * 2**20,
            transcendentals=0,
        ),
    )(slot_of, grad_rows, grads)


def slot_table(routes, chosen):
    token_count = routes.shape[0]
    hits = (routes[:, :, None] == chosen[None, None, :]).any(axis=1)
    rows = lax.broadcasted_iota(jnp.int32, (token_count, token_count), 0)
    columns = lax.broadcasted_iota(jnp.int32, (token_count, token_count), 1)
    earlier = jnp.dot(
        (columns < rows).astype(jnp.bfloat16),
        hits.astype(jnp.bfloat16),
        preferred_element_type=jnp.float32,
    ).astype(jnp.int32)
    return jnp.where(hits, earlier, -1)


def group_shift(value, copies, along):
    pairs = [
        (copy, copy // GROUP * GROUP + (copy % GROUP + along) % GROUP) for copy in range(copies)
    ]
    return lax.ppermute(value, "rep", pairs)


def exchange(blocks, copies):
    return [blocks[0]] + [group_shift(blocks[k], copies, k) for k in range(1, GROUP)]


def exchange_back(blocks, copies):
    return [blocks[0]] + [group_shift(blocks[k], copies, -k) for k in range(1, GROUP)]


def shards(
    tokens_in,
    routes,
    first_gain,
    first_shift,
    joint_weight,
    joint_bias,
    mixer_weight,
    mixer_bias,
    second_gain,
    second_shift,
    router_weight,
    expert_up,
    upward_bias,
    expert_down,
    downward_bias,
    out_grad,
    *,
    groups,
    copies,
):
    row_count, width = tokens_in.shape
    experts, _, part = expert_up.shape
    strip = first_gain.shape[0]
    hidden_width = part * groups
    images = row_count // SEQ
    token_count = images * PADDED

    def widen(rows, fill=0):
        rows = rows.reshape(images, SEQ, rows.shape[1])
        return jnp.pad(rows, ((0, 0), (0, PADDED - SEQ), (0, 0)), constant_values=fill)

    def narrow(rows):
        return rows.reshape(images, PADDED, width)[:, :SEQ].reshape(row_count, width)

    token_images = widen(tokens_in)
    out_grad = widen(out_grad).reshape(token_count, width)
    routes = widen(routes, -1).reshape(token_count, 2)
    low = jnp.bfloat16
    bias_columns = experts * part // strip

    packed = jnp.concatenate(
        [
            joint_weight,
            mixer_weight,
            router_weight,
            first_gain[:, None],
            first_shift[:, None],
            joint_bias.T,
            mixer_bias[:, None],
            second_gain[:, None],
            second_shift[:, None],
            downward_bias.T,
            upward_bias.reshape(strip, bias_columns),
        ],
        axis=1,
    )
    used = packed.shape[1]
    packed_width = 2 * 1664
    packed = jnp.pad(packed, ((0, 0), (0, packed_width - used)))
    packed = packed.reshape(strip, 2, packed_width // 2).transpose(1, 0, 2)
    lines = 4 if groups % 4 == 0 else 1
    ways = groups // lines
    me = lax.axis_index("rep") % GROUP
    shard = lax.axis_index("shard")
    mine = jnp.stack(
        [
            lax.dynamic_index_in_dim(expert_up, me, 0, keepdims=False),
            lax.dynamic_index_in_dim(expert_down, me, 0, keepdims=False).T,
        ]
    )
    near_experts = (me + jnp.arange(GROUP, dtype=jnp.int32)) % GROUP
    slot_of = slot_table(routes, near_experts)
    slot_lines = slot_of.T[:, None, :]
    grad_slots = run_dispatch(slot_lines, out_grad)
    projected, mixed, residual_one, normed_two, logits, full, rows_in, grad_in, pieces = run_forward(
        token_images, slot_lines, packed, mine, grad_slots, lines, ways, copies
    )
    projected = projected.reshape(token_count, 3 * width)
    mixed = mixed.reshape(token_count, width)
    residual_one = residual_one.reshape(token_count, width)
    normed_two = normed_two.reshape(token_count, width)
    logits = logits.reshape(token_count, -1)[:, :experts]
    near_shards = jnp.stack(
        [
            (shard // ways + k) % lines * ways + (shard % ways + j) % ways
            for k in range(lines)
            for j in range(ways)
        ]
    )
    tail = full[1, :, 1408:1536]
    router_full = tail[:, :experts]
    down_shift = tail[:, experts + 7 : 2 * experts + 7].astype(jnp.float32).T
    up_shift = (
        tail[:, 2 * experts + 7 : 2 * experts + 7 + bias_columns]
        .reshape(groups, experts, part)
        .astype(jnp.float32)
    )
    up_shift = lax.dynamic_index_in_dim(up_shift, me, 1, keepdims=False)[near_shards]
    up_shift = up_shift.reshape(lines, 1, ways * part)
    down_shift = lax.dynamic_index_in_dim(down_shift, me, 0, keepdims=True)
    router_probs = jax.nn.softmax(logits, axis=-1)

    probs_near = router_probs[:, near_experts]
    seated = slot_lines == jnp.arange(SLOTS, dtype=jnp.int32)[None, :, None]
    gate_slots = jnp.sum(jnp.where(seated, probs_near.T[:, None, :], 0.0), axis=-1)
    gate_in = jnp.concatenate(exchange(gate_slots, copies), axis=0)[:, None]
    if part % 128:
        joined = [[jnp.concatenate(line, axis=2)] for line in pieces]
    else:
        joined = pieces
    weighted, dispatched_grad, gate_grad, up_shift_grad, down_shift_grad, up, down = run_expert(
        rows_in, grad_in, gate_in, up_shift, down_shift, joined, ways, part
    )
    def from_group(value):
        every = lax.all_gather(value, "rep", axis=0)
        if copies == GROUP:
            return every.astype(jnp.float32)
        return every.astype(jnp.float32).reshape((-1, GROUP) + value.shape).sum(axis=0)

    up_grad = from_group(up)
    down_grad = from_group(down)

    gate_grad = jnp.stack(exchange_back(gate_grad.reshape(GROUP, SLOTS), copies))
    normed_grad, probs_grad = run_combine(slot_of, gate_grad[:, None, :], dispatched_grad)
    probs_grad = probs_grad[:, (jnp.arange(GROUP, dtype=jnp.int32) - me) % GROUP]
    own = (jnp.arange(experts, dtype=jnp.int32) == me).astype(jnp.float32)[:, None]
    down_shift_grad = own * down_shift_grad
    up_shift_grad = jnp.zeros((groups, part), jnp.float32).at[near_shards].set(
        up_shift_grad.reshape(groups, part)
    )
    up_shift_grad = own * up_shift_grad.reshape(1, hidden_width)
    logit_grad = (
        router_probs * (probs_grad - jnp.sum(router_probs * probs_grad, axis=-1, keepdims=True))
    ).astype(low)
    router_grad = contract_first(normed_two, logit_grad)
    normed_grad = normed_grad + contract_last(logit_grad, router_full)
    tail_grad = jnp.concatenate(
        [
            router_grad,
            jnp.zeros((width, 7), jnp.float32),
            down_shift_grad.T,
            up_shift_grad.reshape(experts, groups, part)
            .transpose(1, 0, 2)
            .reshape(groups * strip, bias_columns),
        ],
        axis=1,
    )
    tail_grad = jnp.pad(tail_grad, ((0, 0), (0, 4 * width + 128 - used)))

    def by_image(rows):
        return rows.reshape(images, PADDED, rows.shape[1])

    input_grad, reduced, block_out = run_backward(
        lines,
        ways,
        copies,
        token_images,
        by_image(out_grad),
        by_image(residual_one),
        by_image(normed_grad),
        by_image(mixed),
        by_image(projected),
        tail_grad,
        full,
        slot_of,
        weighted,
    )
    packed_grad = reduced.astype(jnp.float32).transpose(1, 0, 2).reshape(strip, packed_width)
    end = packed_grad[:, 4 * width :]
    line = end[:, experts : experts + 7].T
    return (
        narrow(block_out),
        narrow(input_grad),
        line[0],
        line[1],
        packed_grad[:, : 3 * width],
        line[2:4],
        packed_grad[:, 3 * width : 4 * width],
        line[4],
        line[5],
        line[6],
        end[:, :experts],
        up_grad,
        end[:, 2 * experts + 7 : 2 * experts + 7 + bias_columns].reshape(experts, part),
        down_grad,
        end[:, experts + 7 : 2 * experts + 7].T,
    )


def solution(mesh):
    placed = (
        P(("shard", "rep"), None),
        P(("shard", "rep"), None),
        P("shard"),
        P("shard"),
        P("shard", None),
        P(None, "shard"),
        P("shard", None),
        P("shard"),
        P("shard"),
        P("shard"),
        P("shard", None),
        P(None, None, "shard"),
        P(None, "shard"),
        P(None, "shard", None),
        P(None, "shard"),
        P(("shard", "rep"), None),
    )
    return jax.shard_map(
        functools.partial(
            shards, groups=mesh.shape["shard"], copies=mesh.shape["rep"]
        ),
        mesh=mesh,
        in_specs=placed,
        out_specs=(
            P(("shard", "rep"), None),
            P(("shard", "rep"), None),
            P("shard"),
            P("shard"),
            P("shard", None),
            P(None, "shard"),
            P("shard", None),
            P("shard"),
            P("shard"),
            P("shard"),
            P("shard", None),
            P(None, None, "shard"),
            P(None, "shard"),
            P(None, "shard", None),
            P(None, "shard"),
        ),
        check_vma=False,
    )
```
